32 devices in a mesh: dp: 16 (over z, y, x), seq: 2 (over core).
Axes of the slice: x: 2, y: 2, z: 4, core: 2. Of those that a mesh axis runs over, the one named last changes fastest.
Arguments:
- tokens: bfloat16 [16384, 768], P(('dp', 'seq')), may hold values from -6 to 6
- doc_lengths: int32 [16, 4], P('dp'), may hold values from 0 to 1024, as said below
- w_query: bfloat16 [768, 768], replicated, may hold values from -0.21875 to 0.21875
- w_key: bfloat16 [768, 768], replicated, may hold values from -0.21875 to 0.21875
- w_value: bfloat16 [768, 768], replicated, may hold values from -0.21875 to 0.21875
- w_out: bfloat16 [768, 768], replicated, may hold values from -0.875 to 0.875
- w_gate: bfloat16 [768, 2560], replicated, may hold values from -0.21875 to 0.21875
- w_up: bfloat16 [768, 2560], replicated, may hold values from -0.21875 to 0.21875
- w_down: bfloat16 [2560, 768], replicated, may hold values from -0.125 to 0.125
- gain_attn: float32 [768], replicated, may hold values from 0.5 to 1.5
- gain_ffn: float32 [768], replicated, may hold values from 0.5 to 1.5
- cotangent: bfloat16 [16384, 768], P(('dp', 'seq')), may hold values from -6 to 6
Outputs:
- output: bfloat16 [16384, 768], P(('dp', 'seq'))
- grad_tokens: bfloat16 [16384, 768], P(('dp', 'seq'))
- grad_query: float32 [768, 768], P('dp', 'seq')
- grad_key: float32 [768, 768], P('dp', 'seq')
- grad_value: float32 [768, 768], P('dp', 'seq')
- grad_out: float32 [768, 768], P('seq', 'dp')
- grad_gate: float32 [768, 2560], P('dp', 'seq')
- grad_up: float32 [768, 2560], P('dp', 'seq')
- grad_down: float32 [2560, 768], P('seq', 'dp')
- grad_gain_attn: float32 [768], replicated
- grad_gain_ffn: float32 [768], replicated
- rms_stats: float32 [3], replicated
The draws below stay inside these ranges and needn't reach their ends.
Inputs may be any that keep to these rules, and one draw needn't show every extreme that they name: `doc_lengths`: each row lists the documents of one pack: lengths of 1, 2 or 4 times 1024//4, nonzero ones first, summing to 1024 or 768; the first pack is one document of 1024 tokens.
All inputs are finite; a program needn't handle non-finite values.
Results may differ from the reference program's by a relative error of at most 0.014.
Values may be sent and summed in bfloat16 or wider, within the bound.
No kernel may reach another device: no remote copies, remote signals or barrier semaphores. Data moves between devices by JAX's collectives and lax.ppermute only.
A program may use at most 256 MiB of HBM per device.

```python
import math
import jax
import jax.numpy as jnp
from jax import lax

D = 768
HEADS = 16
HDIM = 48
FF = 2560
PACK = 1024
PACKS = 16
TOKENS = 16384


def draw_tokens(key, part):
    row_frac = jnp.arange(TOKENS, dtype=jnp.float32)[:, None] / TOKENS
    base_draw = jnp.clip(jax.random.normal(key, (TOKENS, D), jnp.float32), -4.0, 4.0)
    row_scale = 0.5 + row_frac
    return (base_draw * row_scale).astype(jnp.bfloat16)


def draw_doc_lengths(key, part):
    shapes_table = jnp.array([[4, 0, 0, 0], [2, 2, 0, 0], [2, 1, 1, 0], [1, 1, 1, 1], [1, 2, 1, 0], [1, 1, 2, 0], [2, 1, 0, 0], [1, 1, 1, 0]], jnp.int32)
    chosen = jax.random.randint(key, (PACKS,), 0, 8, dtype=jnp.int32)
    chosen = chosen.at[0].set(0)
    return shapes_table[chosen] * (PACK // 4)


def level_of(stream_key, extent, split, low, high):
    gain, own = 1.0, jax.random.fold_in(stream_key, 6)
    for dim, parts in split:
        draws = jnp.exp(jax.random.uniform(jax.random.fold_in(own, dim), (parts,), jnp.float32, low / len(split), high / len(split)))
        gain = gain * jnp.repeat(draws, extent[dim] // parts).reshape([-1 if axis == dim else 1 for axis in range(len(extent))])
    return gain


def scatter_about(stream_key, dims, spread, bound, split=(), held_as=jnp.bfloat16):
    values = jax.random.normal(stream_key, dims, jnp.float32) * spread
    if len(split) > 0:
        values = level_of(stream_key, dims, split, -0.22, 0.18) * values
    return jnp.clip(values, min=-bound, max=bound).astype(held_as)


def setup_inputs(seed: int = 0) -> dict:
    streams_of = jax.random.split(jax.random.key(seed), 13)
    return {
        "tokens": draw_tokens(jax.random.fold_in(streams_of[12], 71), 0),
        "doc_lengths": draw_doc_lengths(jax.random.fold_in(streams_of[12], 71), 0),
        "w_query": scatter_about(streams_of[2], (D, HEADS * HDIM), D ** -0.5, 0.21875),
        "w_key": scatter_about(streams_of[3], (D, HEADS * HDIM), D ** -0.5, 0.21875),
        "w_value": scatter_about(streams_of[4], (D, HEADS * HDIM), D ** -0.5, 0.21875),
        "w_out": scatter_about(streams_of[5], (HEADS * HDIM, D), (HEADS * HDIM // 16) ** -0.5, 0.875),
        "w_gate": scatter_about(streams_of[6], (D, FF), D ** -0.5, 0.21875),
        "w_up": scatter_about(streams_of[7], (D, FF), D ** -0.5, 0.21875),
        "w_down": scatter_about(streams_of[8], (FF, D), FF ** -0.5, 0.125),
        "gain_attn": jnp.clip(1.0 + 0.1 * jax.random.normal(streams_of[9], (D,), jnp.float32), 0.5, 1.5),
        "gain_ffn": jnp.clip(1.0 + 0.1 * jax.random.normal(streams_of[10], (D,), jnp.float32), 0.5, 1.5),
        "cotangent": scatter_about(streams_of[11], (TOKENS, D), 1.0, 6.0, ((0, 32),)),
    }


@jax.custom_vjp
def low(v):
    return lax.optimization_barrier(v.astype(jnp.bfloat16)).astype(jnp.float32)

@jax.custom_vjp
def low_back(v):
    return v

def low_keep(v):
    return (low(v), None)

def low_pass(kept, grad):
    return (grad,)

def back_keep(v):
    return (v, None)

def back_low(kept, grad):
    return (low(grad),)
low.defvjp(low_keep, low_pass)
low_back.defvjp(back_keep, back_low)
HIGHEST_MODE = lax.Precision.HIGHEST

def rms_norm(stream, gain_vector):
    return stream * lax.rsqrt(lax.optimization_barrier(jnp.mean(stream * stream, axis=-1, keepdims=True)) + 1e-06) * gain_vector

def swiglu(gate_proj, up_proj):
    return jax.nn.silu(gate_proj) * up_proj

def rotate(values, cosine_table, sine_table):
    middle = values.shape[-1] // 2
    front_half = values[..., :middle]
    back_half = values[..., middle:]
    return jnp.concatenate([front_half * cosine_table - back_half * sine_table, back_half * cosine_table + front_half * sine_table], axis=-1)

def angles(position, head_size):
    middle = head_size // 2
    frequency = jnp.exp(jnp.arange(middle, dtype=jnp.float32) * (-math.log(10000.0) / middle))
    phases = position.astype(jnp.float32)[:, None] * frequency[None, :]
    return (jnp.cos(phases)[:, None, :], jnp.sin(phases)[:, None, :])

def layout(lengths, span):
    finish = jnp.cumsum(lengths, dtype=jnp.int32)
    begins = jnp.concatenate([finish - lengths, finish[-1:]])
    places = jnp.arange(span, dtype=jnp.int32)
    segment = lax.optimization_barrier(jnp.sum((places[:, None] >= finish[None, :]).astype(jnp.int32), axis=1, dtype=jnp.int32))
    chosen = segment[:, None] == jnp.arange(begins.shape[0], dtype=jnp.int32)[None, :]
    opening = lax.optimization_barrier(jnp.sum(jnp.where(chosen, begins[None, :], 0), axis=1, dtype=jnp.int32))
    return (segment, places - opening, places < finish[-1])

def attention(query_rot, key_rot, value_low, segment):
    places = jnp.arange(PACK, dtype=jnp.int32)
    raw_scores = jnp.einsum('qhd,khd->hqk', query_rot, key_rot, precision=HIGHEST_MODE)
    scores = low_back(raw_scores) * (1.0 / math.sqrt(HDIM))
    allowed = (segment[:, None] == segment[None, :]) & (places[:, None] >= places[None, :])
    scores = jnp.where(allowed[None], scores, -1e+30)
    attn_probs = low(jax.nn.softmax(scores, axis=-1))
    return jnp.einsum('hqk,khd->qhd', attn_probs, value_low, precision=HIGHEST_MODE)

def pack_forward(stream, w_query, w_key, w_value, w_out, w_gate, w_up, w_down, gain_attn, gain_ffn, segment, position):
    cosine_table, sine_table = angles(position, HDIM)
    head_shape = (PACK, HEADS, HDIM)
    query_proj = low_back(jnp.dot(stream, w_query, precision=HIGHEST_MODE)).reshape(head_shape)
    key_proj = low_back(jnp.dot(stream, w_key, precision=HIGHEST_MODE)).reshape(head_shape)
    value_low = low(low_back(jnp.dot(stream, w_value, precision=HIGHEST_MODE))).reshape(head_shape)
    query_rot = low(rotate(query_proj, cosine_table, sine_table))
    key_rot = low(rotate(key_proj, cosine_table, sine_table))
    context = attention(query_rot, key_rot, value_low, segment).reshape(PACK, HEADS * HDIM)
    context = low(low_back(context))
    attn_out = low_back(jnp.dot(context, w_out, precision=HIGHEST_MODE))
    normed = rms_norm(stream + attn_out, gain_attn)
    normed_low = low(normed)
    gate_proj = low_back(jnp.dot(normed_low, w_gate, precision=HIGHEST_MODE))
    up_proj = low_back(jnp.dot(normed_low, w_up, precision=HIGHEST_MODE))
    hidden = low(swiglu(gate_proj, up_proj))
    ffn_out = low_back(jnp.dot(hidden, w_down, precision=HIGHEST_MODE))
    result = rms_norm(normed + ffn_out, gain_ffn)
    return (result, (attn_out, ffn_out))

def reference(tokens, doc_lengths, w_query, w_key, w_value, w_out, w_gate, w_up, w_down, gain_attn, gain_ffn, cotangent):
    params = tuple((matrix.astype(jnp.float32) for matrix in (w_query, w_key, w_value, w_out, w_gate, w_up, w_down, gain_attn, gain_ffn)))
    streams = tokens.astype(jnp.float32).reshape(PACKS, PACK, D)
    cot_packs = cotangent.astype(jnp.float32).reshape(PACKS, PACK, D)

    def one_pack(totals, inputs):
        stream, lengths, cot_rows = inputs
        segment, position, valid_rows = layout(lengths, PACK)
        mask_rows = valid_rows.astype(jnp.float32)[:, None]

        def forward(stream_in, *weights_in):
            return pack_forward(stream_in, *weights_in, segment, position)
        result, back_fn, extras = jax.vjp(forward, stream, *params, has_aux=True)
        attn_out, ffn_out = extras
        all_grads = back_fn(cot_rows * mask_rows)
        square_sums = jnp.stack([jnp.sum(mask_rows * stream * stream), jnp.sum(mask_rows * attn_out * attn_out), jnp.sum(mask_rows * ffn_out * ffn_out), jnp.sum(mask_rows)])
        grad_totals, stat_totals = totals
        new_grads = tuple((left + right for left, right in zip(grad_totals, all_grads[1:])))
        return ((new_grads, stat_totals + square_sums), (result.astype(jnp.bfloat16), all_grads[0].astype(jnp.bfloat16)))
    start_totals = (tuple((jnp.zeros(matrix.shape, jnp.float32) for matrix in params)), jnp.zeros((4,), jnp.float32))
    finals, outputs = lax.scan(one_pack, start_totals, (streams, doc_lengths, cot_packs))
    grad_totals, stat_totals = finals
    output = outputs[0].reshape(TOKENS, D)
    grad_tokens = outputs[1].reshape(TOKENS, D)
    rms_values = jnp.sqrt(stat_totals[:3] / (stat_totals[3] * D))
    return (output, grad_tokens, grad_totals[0], grad_totals[1], grad_totals[2], grad_totals[3], grad_totals[4], grad_totals[5], grad_totals[6], grad_totals[7], grad_totals[8], rms_values)
```

```python
import math

import jax
import jax.numpy as jnp
from jax import lax
from jax.sharding import PartitionSpec as P

HDIM = 48


def rms_norm(stream, gain_vector):
    return (
        stream * lax.rsqrt(jnp.mean(stream * stream, axis=-1, keepdims=True) + 1e-06) * gain_vector
    )


def swiglu(gate_proj, up_proj):
    return jax.nn.silu(gate_proj) * up_proj


def rotate(values, cosine_table, sine_table):
    middle = values.shape[-1] // 2
    front_half = values[..., :middle]
    back_half = values[..., middle:]
    return jnp.concatenate(
        [
            front_half * cosine_table - back_half * sine_table,
            back_half * cosine_table + front_half * sine_table,
        ],
        axis=-1,
    )


def angles(position, head_size):
    middle = head_size // 2
    frequency = jnp.exp(jnp.arange(middle, dtype=jnp.float32) * (-math.log(10000.0) / middle))
    phases = position.astype(jnp.float32)[:, None] * frequency[None, :]
    return (jnp.cos(phases)[:, None, :], jnp.sin(phases)[:, None, :])


def layout(lengths, span):
    finish = jnp.cumsum(lengths, dtype=jnp.int32)
    begins = jnp.concatenate([finish - lengths, finish[-1:]])
    places = jnp.arange(span, dtype=jnp.int32)
    segment = jnp.sum(
        (places[:, None] >= finish[None, :]).astype(jnp.int32), axis=1, dtype=jnp.int32
    )
    chosen = segment[:, None] == jnp.arange(begins.shape[0], dtype=jnp.int32)[None, :]
    opening = jnp.sum(jnp.where(chosen, begins[None, :], 0), axis=1, dtype=jnp.int32)
    return (segment, places - opening, places < finish[-1])

def swap_seq(value):
    return lax.ppermute(value, "seq", [(0, 1), (1, 0)])


def gather_rows(value, seq_index):
    other = swap_seq(value)
    low = jnp.where(seq_index == 0, value, other)
    high = jnp.where(seq_index == 0, other, value)
    return jnp.concatenate([low, high], axis=0)


def scatter_halves(value, seq_index, axis):
    half = value.shape[axis] // 2
    keep = lax.dynamic_slice_in_dim(value, seq_index * half, half, axis)
    away = lax.dynamic_slice_in_dim(value, (1 - seq_index) * half, half, axis)
    return keep.astype(jnp.float32) + swap_seq(away).astype(jnp.float32)


def stage_order(bits, turn):
    last = bits - 1
    return [(turn + step) % last for step in range(last)] + [last]


def halve_dp(value, dp_index, dp_size, turn):
    bits = dp_size.bit_length() - 1
    rows, cols = value.shape
    left = list(range(bits - 1, -1, -1))
    value = value.reshape([2] * bits + [rows // dp_size, cols]).astype(jnp.bfloat16)
    order = stage_order(bits, turn)
    for step, bit in enumerate(order):
        axis = left.index(bit)
        left.pop(axis)
        mine = (dp_index >> bit) & 1
        keep = lax.dynamic_index_in_dim(value, mine, axis, keepdims=False)
        away = lax.dynamic_index_in_dim(value, 1 - mine, axis, keepdims=False)
        came = lax.ppermute(away, "dp", [(i, i ^ (1 << bit)) for i in range(dp_size)])
        value = keep.astype(jnp.float32) + came.astype(jnp.float32)
        if step + 1 < bits:
            value = value.astype(jnp.bfloat16)
    return value


def sum_everywhere(value, dp_size):
    value = value + swap_seq(value)
    for bit in range(dp_size.bit_length() - 1):
        value = value + lax.ppermute(value, "dp", [(i, i ^ (1 << bit)) for i in range(dp_size)])
    return value


def shards(
    tokens,
    doc_lengths,
    w_query,
    w_key,
    w_value,
    w_out,
    w_gate,
    w_up,
    w_down,
    gain_attn,
    gain_ffn,
    cotangent,
):
    row_count = tokens.shape[0]
    width = tokens.shape[1]
    seq_index = lax.axis_index("seq")
    dp_index = lax.axis_index("dp")
    dp_size = lax.axis_size("dp")
    seq_parts = lax.axis_size("seq")
    pack_rows = row_count * seq_parts
    head_cols = w_query.shape[1] // seq_parts
    local_heads = head_cols // HDIM
    score_scale = 1.0 / math.sqrt(HDIM)
    segment, position, valid_rows = layout(doc_lengths[0], pack_rows)
    own_valid = lax.dynamic_slice_in_dim(valid_rows, seq_index * row_count, row_count, 0).astype(
        jnp.float32
    )[:, None]
    col_start = seq_index * head_cols
    w_qkv = jnp.concatenate(
        [
            lax.dynamic_slice_in_dim(w_query, col_start, head_cols, 1),
            lax.dynamic_slice_in_dim(w_key, col_start, head_cols, 1),
            lax.dynamic_slice_in_dim(w_value, col_start, head_cols, 1),
        ],
        axis=1,
    )
    w_out_rows = lax.dynamic_slice_in_dim(w_out, col_start, head_cols, 0)
    stream = tokens.astype(jnp.float32)
    gathered = gather_rows(tokens, seq_index)
    projected = jnp.dot(gathered, w_qkv, preferred_element_type=jnp.float32)
    cosine_table, sine_table = angles(position, HDIM)
    head_shape = (pack_rows, local_heads, HDIM)
    query_proj = projected[:, :head_cols].reshape(head_shape)
    key_proj = projected[:, head_cols : 2 * head_cols].reshape(head_shape)
    query_rot, rope_back = jax.vjp(
        lambda values_in: rotate(values_in, cosine_table, sine_table), query_proj
    )
    key_rot = rotate(key_proj, cosine_table, sine_table)
    query_low = query_rot.astype(jnp.bfloat16)
    key_low = key_rot.astype(jnp.bfloat16)
    value_low = projected[:, 2 * head_cols :].reshape(head_shape).astype(jnp.bfloat16)
    block_rows = min(512, pack_rows)
    block_total = pack_rows // block_rows
    places = jnp.arange(pack_rows, dtype=jnp.int32)

    def scores_of(block_index):
        query_from = block_index * block_rows
        key_end = query_from + block_rows
        raw_scores = jnp.einsum(
            "qhd,khd->hqk",
            query_low[query_from:key_end],
            key_low[:key_end],
            preferred_element_type=jnp.float32,
        )
        allowed = (segment[query_from:key_end, None] == segment[None, :key_end]) & (
            places[query_from:key_end, None] >= places[None, :key_end]
        )
        return jnp.where(allowed[None], raw_scores * score_scale, -1e30)

    contexts = []
    lse_parts = []
    for block_index in range(block_total):
        key_end = (block_index + 1) * block_rows
        scores = scores_of(block_index)
        row_max = jnp.max(scores, axis=-1, keepdims=True)
        exp_scores = jnp.exp(scores - row_max)
        row_total = jnp.sum(exp_scores, axis=-1, keepdims=True)
        attn_probs = (exp_scores / row_total).astype(jnp.bfloat16)
        lse_parts.append(row_max + jnp.log(row_total))
        contexts.append(
            jnp.einsum(
                "hqk,khd->qhd", attn_probs, value_low[:key_end], preferred_element_type=jnp.float32
            )
        )
    context_low = (
        jnp.concatenate(contexts, axis=0).reshape(pack_rows, head_cols).astype(jnp.bfloat16)
    )
    attn_out = scatter_halves(
        jnp.dot(context_low, w_out_rows, preferred_element_type=jnp.float32), seq_index, 0
    )
    normed, norm_one_back = jax.vjp(rms_norm, stream + attn_out, gain_attn)
    normed_low = normed.astype(jnp.bfloat16)
    gate_cols, up_cols, down_rows = (w_gate, w_up, w_down)
    gate_proj = jnp.dot(normed_low, gate_cols, preferred_element_type=jnp.float32)
    up_proj = jnp.dot(normed_low, up_cols, preferred_element_type=jnp.float32)
    hidden, swiglu_back = jax.vjp(swiglu, gate_proj, up_proj)
    hidden_low = hidden.astype(jnp.bfloat16)
    ffn_out = jnp.dot(hidden_low, down_rows, preferred_element_type=jnp.float32)
    result, norm_two_back = jax.vjp(rms_norm, normed + ffn_out, gain_ffn)
    stat_terms = jnp.stack(
        [
            jnp.sum(own_valid * stream * stream),
            jnp.sum(own_valid * attn_out * attn_out),
            jnp.sum(own_valid * ffn_out * ffn_out),
            jnp.sum(own_valid),
        ]
    )
    grad_result = cotangent.astype(jnp.float32) * own_valid
    grad_mix, grad_gain_two = norm_two_back(grad_result)
    grad_ffn_low = grad_mix.astype(jnp.bfloat16)
    grad_hidden = jnp.dot(grad_ffn_low, down_rows.T, preferred_element_type=jnp.float32)
    grad_gate_f, grad_up_f = swiglu_back(grad_hidden)
    grad_gate_low = grad_gate_f.astype(jnp.bfloat16)
    grad_up_low = grad_up_f.astype(jnp.bfloat16)
    grad_normed_ffn = jnp.dot(
        grad_gate_low, gate_cols.T, preferred_element_type=jnp.float32
    ) + jnp.dot(grad_up_low, up_cols.T, preferred_element_type=jnp.float32)
    weight_gate = jnp.dot(normed_low.T, grad_gate_low, preferred_element_type=jnp.float32)
    weight_up = jnp.dot(normed_low.T, grad_up_low, preferred_element_type=jnp.float32)
    weight_down_t = jnp.dot(grad_ffn_low.T, hidden_low, preferred_element_type=jnp.float32)
    weight_gate, weight_up, weight_down_t = (
        scatter_halves(value.astype(jnp.bfloat16), seq_index, 1).astype(jnp.bfloat16)
        for value in (weight_gate, weight_up, weight_down_t)
    )
    summed_gate = halve_dp(weight_gate, dp_index, dp_size, 0)
    summed_up = halve_dp(weight_up, dp_index, dp_size, 1)
    summed_down_t = halve_dp(weight_down_t, dp_index, dp_size, 2)
    grad_stream_one, grad_gain_one = norm_one_back(grad_mix + grad_normed_ffn)
    grad_attn_low = grad_stream_one.astype(jnp.bfloat16)
    grad_attn_all = gather_rows(grad_attn_low, seq_index)
    small = jnp.zeros((3, width), jnp.float32)
    small = small.at[0].set(grad_gain_one).at[1].set(grad_gain_two).at[2, :4].set(stat_terms)
    small = sum_everywhere(small, dp_size)
    total_gain_one, total_gain_two, stat_totals = (small[0], small[1], small[2, :4])
    grad_context_low = jnp.dot(
        grad_attn_all, w_out_rows.T, preferred_element_type=jnp.float32
    ).astype(jnp.bfloat16)
    weight_out_t = jnp.dot(grad_attn_all.T, context_low, preferred_element_type=jnp.float32)
    grad_context_heads = grad_context_low.reshape(head_shape)
    grad_query_rot = jnp.zeros(head_shape, jnp.float32)
    grad_key_rot = jnp.zeros(head_shape, jnp.float32)
    grad_value = jnp.zeros(head_shape, jnp.float32)
    for block_index in range(block_total):
        query_from = block_index * block_rows
        key_end = query_from + block_rows
        scores = scores_of(block_index)
        attn_probs = jnp.exp(scores - lse_parts[block_index])
        probs_low = attn_probs.astype(jnp.bfloat16)
        context_block = grad_context_heads[query_from:key_end]
        grad_probs = jnp.einsum(
            "qhd,khd->hqk", context_block, value_low[:key_end], preferred_element_type=jnp.float32
        )
        grad_scores = (
            attn_probs
            * (grad_probs - jnp.sum(attn_probs * grad_probs, axis=-1, keepdims=True))
            * score_scale
        ).astype(jnp.bfloat16)
        grad_query_rot = grad_query_rot.at[query_from:key_end].set(
            jnp.einsum(
                "hqk,khd->qhd", grad_scores, key_low[:key_end], preferred_element_type=jnp.float32
            )
        )
        grad_key_rot = grad_key_rot.at[:key_end].add(
            jnp.einsum(
                "hqk,qhd->khd",
                grad_scores,
                query_low[query_from:key_end],
                preferred_element_type=jnp.float32,
            )
        )
        grad_value = grad_value.at[:key_end].add(
            jnp.einsum("hqk,qhd->khd", probs_low, context_block, preferred_element_type=jnp.float32)
        )
    grad_query_f = rope_back(grad_query_rot)[0]
    grad_key_f = rope_back(grad_key_rot)[0]
    grad_qkv_low = jnp.concatenate(
        [
            grad_query_f.reshape(pack_rows, head_cols),
            grad_key_f.reshape(pack_rows, head_cols),
            grad_value.reshape(pack_rows, head_cols),
        ],
        axis=1,
    ).astype(jnp.bfloat16)
    weight_qkv = jnp.dot(gathered.T, grad_qkv_low, preferred_element_type=jnp.float32)
    grad_stream_proj = scatter_halves(
        jnp.dot(grad_qkv_low, w_qkv.T, preferred_element_type=jnp.float32).astype(jnp.bfloat16),
        seq_index,
        0,
    )
    grad_tokens = (grad_stream_one + grad_stream_proj).astype(jnp.bfloat16)
    summed_query = halve_dp(weight_qkv[:, :head_cols], dp_index, dp_size, 0)
    summed_key = halve_dp(weight_qkv[:, head_cols : 2 * head_cols], dp_index, dp_size, 1)
    summed_value = halve_dp(weight_qkv[:, 2 * head_cols :], dp_index, dp_size, 2)
    summed_out_t = halve_dp(weight_out_t, dp_index, dp_size, 0)
    rms_values = jnp.sqrt(stat_totals[:3] / (stat_totals[3] * width))
    return (
        result.astype(jnp.bfloat16),
        grad_tokens,
        summed_query,
        summed_key,
        summed_value,
        summed_out_t.T,
        summed_gate,
        summed_up,
        summed_down_t.T,
        total_gain_one,
        total_gain_two,
        rms_values,
    )


def solution(mesh):
    return jax.shard_map(
        shards,
        mesh=mesh,
        in_specs=(
            P(("dp", "seq"), None),
            P("dp", None),
            P(),
            P(),
            P(),
            P(),
            P(),
            P(),
            P(),
            P(),
            P(),
            P(("dp", "seq"), None),
        ),
        out_specs=(
            P(("dp", "seq"), None),
            P(("dp", "seq"), None),
            P("dp", "seq"),
            P("dp", "seq"),
            P("dp", "seq"),
            P("seq", "dp"),
            P("dp", "seq"),
            P("dp", "seq"),
            P("seq", "dp"),
            P(),
            P(),
            P(),
        ),
        check_vma=False,
    )
```

```python
import functools
import math

import jax
import jax.numpy as jnp
import numpy as np
from jax import lax
from jax.experimental import pallas as pl
from jax.experimental.pallas import tpu as pltpu
from jax.sharding import PartitionSpec as P

HDIM = 48
HALF = HDIM // 2
SCORE = 1.0 / math.sqrt(HDIM)
LOG2E = 1.0 / math.log(2.0)
NEG = -1e30
BF16 = jnp.bfloat16
F32 = jnp.float32
CHUNK = 256
WIDE = 512
ROWS = 64
SPANS = 4
MIB = 1 << 20


def call(kernel, name, scalars, arrays, out_shape, flops, scratch=(), room=16, aliases=None):
    moved = sum(math.prod(o.shape) * o.dtype.itemsize for o in out_shape)
    return pl.pallas_call(
        kernel,
        in_specs=[pl.BlockSpec(memory_space=pltpu.SMEM)] * len(scalars)
        + [pl.BlockSpec(memory_space=pltpu.VMEM)] * len(arrays),
        out_specs=[pl.BlockSpec(memory_space=pltpu.VMEM)] * len(out_shape),
        out_shape=out_shape,
        scratch_shapes=list(scratch),
        input_output_aliases=aliases or {},
        cost_estimate=pl.CostEstimate(flops=flops, bytes_accessed=2 * moved, transcendentals=0),
        compiler_params=pltpu.CompilerParams(vmem_limit_bytes=room * MIB),
        name=name,
    )(*scalars, *arrays)


def shape(dtype, *dims):
    return jax.ShapeDtypeStruct(dims, dtype)


def at(start, size):
    return pl.ds(pl.multiple_of(start, size), size)


def dot(a, b, ca, cb):
    return lax.dot_general(a, b, (((ca,), (cb,)), ((), ())), preferred_element_type=F32)


def rope_tables(span):
    freq = 10000.0 ** (-np.arange(HALF, dtype=np.float64) / HALF)
    phase = freq[:, None] * np.arange(span, dtype=np.float64)[None, :]
    return np.cos(phase).astype(np.float32), np.sin(phase).astype(np.float32)


def block_facts(len_ref, block):
    ends = []
    total = 0
    for index in range(len_ref.shape[0]):
        total = total + len_ref[index]
        ends.append(total)
    segments, openings = [], []
    for number in range(SPANS):
        segment = 0
        opening = 0
        for index, end in enumerate(ends):
            done = number * block >= end
            segment = segment + done.astype(jnp.int32)
            opening = opening + jnp.where(done, len_ref[index], 0)
        segments.append(segment)
        openings.append(opening)
    return segments, openings


def causal(block):
    key = lax.broadcasted_iota(jnp.int32, (block, block), 0)
    return key <= lax.broadcasted_iota(jnp.int32, (block, block), 1)


def attention_forward_kernel(
    info_ref, len_ref, own_ref, oth_ref, wq_ref, wk_ref, wv_ref, cos_ref, sin_ref,
    x_ref, q_ref, k_ref, v_ref, ctx_ref, mine_ref, away_ref, lse_ref,
):
    rows = own_ref.shape[0]
    cols, pack = q_ref.shape
    heads = cols // HDIM
    block = pack // SPANS
    segments, openings = block_facts(len_ref, block)
    side = info_ref[0]
    x_ref[at(side * rows, rows), :] = own_ref[...]
    x_ref[at((1 - side) * rows, rows), :] = oth_ref[...]
    for w_ref, to_ref, scale in ((wq_ref, q_ref, SCORE * LOG2E), (wk_ref, k_ref, 1.0), (wv_ref, v_ref, None)):
        weight = w_ref[:, at(side * cols, cols)].T
        for number in range(SPANS):
            lanes = slice(number * block, (number + 1) * block)
            part = dot(weight, x_ref[lanes, :], 1, 1)
            if scale is None:
                to_ref[:, lanes] = part.astype(BF16)
                continue
            here = at(number * block - openings[number], block)
            cos = cos_ref[:, here] * scale
            sin = sin_ref[:, here] * scale
            for head in range(heads):
                a = part[head * HDIM : head * HDIM + HALF]
                b = part[head * HDIM + HALF : (head + 1) * HDIM]
                turned = jnp.concatenate([a * cos - b * sin, b * cos + a * sin], axis=0)
                to_ref[head * HDIM : (head + 1) * HDIM, lanes] = turned.astype(BF16)
    below = causal(block)

    @pl.loop(0, heads)
    def _(head):
        here = at(head * HDIM, HDIM)
        keys = k_ref[here, :].T
        value = v_ref[here, :]
        for i in range(SPANS):
            lanes = slice(i * block, (i + 1) * block)
            query = q_ref[here, lanes]
            scores, biases, tops = [], [], []
            for j in range(i + 1):
                score = dot(keys[j * block : (j + 1) * block], query, 1, 0)
                bias = 0.0
                if j == i:
                    score = jnp.where(below, score, NEG)
                else:
                    bias = jnp.where(segments[i] == segments[j], 0.0, NEG)
                scores.append(score)
                biases.append(bias)
                tops.append(jnp.max(score, axis=0, keepdims=True) + bias)
            top = functools.reduce(jnp.maximum, tops)
            total = jnp.zeros((1, block), F32)
            context = jnp.zeros((HDIM, block), F32)
            for j in range(i + 1):
                prob = jnp.exp2(scores[j] - (top - biases[j]))
                total = total + jnp.sum(prob, axis=0, keepdims=True)
                context = context + dot(value[:, j * block : (j + 1) * block], prob.astype(BF16), 1, 0)
            ctx_ref[here, lanes] = (context * (1.0 / total)).astype(BF16)
            lse_ref[head, :, lanes] = top + jnp.log2(total)
        mine_ref[here, :] = ctx_ref[here, at(side * rows, rows)]
        away_ref[here, :] = ctx_ref[here, at((1 - side) * rows, rows)]


def attention_forward(info, lengths, own, oth, weights):
    rows, width = own.shape
    pack = 2 * rows
    cols = weights[0].shape[1] // 2
    heads = cols // HDIM
    half = shape(BF16, cols, rows)
    return call(
        attention_forward_kernel, "attention_forward", (info, lengths),
        (own, oth, *weights, *rope_tables(pack)),
        [shape(BF16, pack, width)] + [shape(BF16, cols, pack)] * 4 + [half, half, shape(F32, heads, 1, pack)],
        15_000_000_000,
    )


def attention_backward_kernel(
    info_ref, len_ref, q_ref, k_ref, v_ref, ctx_ref, own_ref, oth_ref, lse_ref, cos_ref, sin_ref, *rest,
    first, heads,
):
    dq_ref, dk_ref, dv_ref, dctx_ref, dk_acc, dv_acc = rest[-6:]
    rows = own_ref.shape[1]
    pack = q_ref.shape[1]
    block = pack // SPANS
    segments, openings = block_facts(len_ref, block)
    side = info_ref[0]
    below = causal(block)

    def unturn(value, number, scale):
        here = at(number * block - openings[number], block)
        cos = cos_ref[:, here] * scale
        sin = sin_ref[:, here] * scale
        a, b = value[:HALF], value[HALF:]
        return jnp.concatenate([a * cos + b * sin, b * cos - a * sin], axis=0).astype(BF16)

    @pl.loop(first, first + heads)
    def _(head):
        here = at(head * HDIM, HDIM)
        dctx_ref[:, at(side * rows, rows)] = own_ref[here, :]
        dctx_ref[:, at((1 - side) * rows, rows)] = oth_ref[here, :]
        key = k_ref[here, :]
        keys = key.T
        values = v_ref[here, :].T
        for i in range(SPANS):
            lanes = slice(i * block, (i + 1) * block)
            query = q_ref[here, lanes]
            grad = dctx_ref[:, lanes]
            delta = jnp.sum(grad.astype(F32) * ctx_ref[here, lanes].astype(F32), axis=0, keepdims=True)
            lse = lse_ref[head, :, lanes]
            dq = jnp.zeros((HDIM, block), F32)
            for j in range(i + 1):
                span = slice(j * block, (j + 1) * block)
                score = dot(keys[span], query, 1, 0)
                if j == i:
                    prob = jnp.exp2(jnp.where(below, score, NEG) - lse)
                else:
                    prob = jnp.exp2(score - (lse - jnp.where(segments[i] == segments[j], 0.0, NEG)))
                slope = dot(values[span], grad, 1, 0)
                dscore = (prob * (slope - delta)).astype(BF16)
                dq = dq + dot(key[:, span], dscore, 1, 0)
                dk = dot(query, dscore, 1, 1)
                dv = dot(grad, prob.astype(BF16), 1, 1)
                if j == i:
                    dk_acc[:, span] = dk
                    dv_acc[:, span] = dv
                else:
                    dk_acc[:, span] += dk
                    dv_acc[:, span] += dv
            dq_ref[here, lanes] = unturn(dq, i, SCORE)
        for number in range(SPANS):
            lanes = slice(number * block, (number + 1) * block)
            dk_ref[here, lanes] = unturn(dk_acc[:, lanes], number, 1.0 / LOG2E)
            dv_ref[here, lanes] = dv_acc[:, lanes].astype(BF16)


def attention_backward(info, lengths, kept, own, oth, first, heads, sofar):
    query, key, value, context, lse = kept
    cols, pack = query.shape
    arrays = (query, key, value, context, own, oth, lse, *rope_tables(pack), *sofar)
    base = 2 + len(arrays) - len(sofar)
    return call(
        functools.partial(attention_backward_kernel, first=first, heads=heads),
        "attention_backward", (info, lengths), arrays, [shape(BF16, cols, pack)] * 3,
        heads * 3_000_000_000,
        [pltpu.VMEM((HDIM, pack), BF16)] + [pltpu.VMEM((HDIM, pack), F32)] * 2,
        aliases={base + index: index for index in range(len(sofar))},
    )


def inverse_rms(value):
    return lax.rsqrt(jnp.mean(value * value, axis=-1, keepdims=True) + 1e-06)


def norm_back(value, gain, grad):
    inv = inverse_rms(value)
    scaled = grad * gain
    slope = jnp.mean(scaled * value, axis=-1, keepdims=True) * (inv * inv * inv)
    return scaled * inv - value * slope, grad * value * inv


def relative_rows(to_ref, from_ref, place, blocks):
    size = from_ref.shape[0] // blocks
    for block in range(blocks):
        to_ref[block * size : (block + 1) * size, :] = from_ref[at((block ^ place) * size, size), :]


def position(block, order):
    last = len(order) - 1
    return sum(((block >> bit) & 1) << (last - step) for step, bit in enumerate(order))


def ffn_forward_kernel(
    info_ref, len_ref, x_ref, mine_ref, came_ref, wo_ref, g1_ref, g2_ref, wg_ref, wu_ref, wd_ref, cot_ref,
    act_ref, s_ref, t_ref, out_ref, dm_ref, dmt_ref, hbt_ref, dr2_ref, r1_ref, small_ref,
    hb_ref, h_ref, m_ref, turn_ref, *, blocks,
):
    rows, width = x_ref.shape
    part = mine_ref.shape[0]
    total = len_ref[0] + len_ref[1] + len_ref[2] + len_ref[3]
    side = info_ref[0]
    first = side * rows

    def valid_of(start):
        places = lax.broadcasted_iota(jnp.int32, (ROWS, 1), 0) + (start + first)
        return (places < total).astype(F32)

    def squares(row, value, valid):
        small_ref[row : row + 1, :] += jnp.sum(value * value * valid, axis=0, keepdims=True)

    small_ref[...] = jnp.zeros_like(small_ref)
    m_ref[...] = dot(mine_ref[...].T, wo_ref[at(side * part, part), :], 1, 0) + dot(
        came_ref[...].T, wo_ref[at((1 - side) * part, part), :], 1, 0
    )

    @pl.loop(0, rows // ROWS)
    def _(index):
        here = at(index * ROWS, ROWS)
        valid = valid_of(index * ROWS)
        x = x_ref[here, :].astype(F32)
        a = m_ref[here, :]
        r1 = x + a
        h = r1 * inverse_rms(r1) * g1_ref[...]
        r1_ref[here, :] = r1
        h_ref[here, :] = h
        hb_ref[here, :] = h.astype(BF16)
        squares(2, x, valid)
        squares(3, a, valid)

    turn_ref[...] = hb_ref[...].T
    relative_rows(hbt_ref, turn_ref, info_ref[1], blocks)
    m_ref[...] = jnp.zeros_like(m_ref)

    @pl.loop(0, act_ref.shape[1] // WIDE)
    def _(step):
        cols = at(step * WIDE, WIDE)
        gate = dot(hb_ref[...], wg_ref[:, cols], 1, 0)
        up = dot(hb_ref[...], wu_ref[:, cols], 1, 0)
        sig = 1.0 / (1.0 + jnp.exp(-gate))
        silu = gate * sig
        act = (silu * up).astype(BF16)
        act_ref[:, cols] = act
        s_ref[:, cols] = silu.astype(BF16)
        t_ref[:, cols] = (up * (sig + silu * (1.0 - sig))).astype(BF16)
        m_ref[...] += dot(act, wd_ref[cols, :], 1, 0)

    @pl.loop(0, rows // ROWS)
    def _(index):
        here = at(index * ROWS, ROWS)
        valid = valid_of(index * ROWS)
        m = m_ref[here, :]
        r2 = h_ref[here, :] + m
        gain = g2_ref[...]
        dr2, dgain = norm_back(r2, gain, cot_ref[here, :].astype(F32) * valid)
        out_ref[here, :] = (r2 * inverse_rms(r2) * gain).astype(BF16)
        dr2_ref[here, :] = dr2
        dm_ref[here, :] = dr2.astype(BF16)
        small_ref[1:2, :] += jnp.sum(dgain, axis=0, keepdims=True)
        squares(4, m, valid)

    small_ref[5:6, :] = jnp.full((1, width), jnp.clip(total - first, 0, rows).astype(F32))
    turn_ref[...] = dm_ref[...].T
    relative_rows(dmt_ref, turn_ref, info_ref[1], blocks)


def ffn_forward(info, lengths, x, mine, came, w_out, g1, g2, wg, wu, wd, cot, blocks):
    rows, width = x.shape
    ff = wg.shape[1]
    return call(
        functools.partial(ffn_forward_kernel, blocks=blocks), "ffn_forward", (info, lengths),
        (x, mine, came, w_out, g1, g2, wg, wu, wd, cot),
        [shape(BF16, rows, ff)] * 3 + [shape(BF16, rows, width)] * 2 + [shape(BF16, width, rows)] * 2
        + [shape(F32, rows, width)] * 2 + [shape(F32, 8, width)],
        6 * rows * width * ff,
        [
            pltpu.VMEM((rows, width), BF16), pltpu.VMEM((rows, width), F32),
            pltpu.VMEM((rows, width), F32), pltpu.VMEM((width, rows), BF16),
        ],
    )


def split_store(product, came, to_refs, order, blocks):
    size = product.shape[0] // blocks
    for block in range(blocks):
        place = position(block, order)
        rows = product[block * size : (block + 1) * size]
        if came is not None:
            rows = rows + came[place * size : (place + 1) * size].astype(F32)
        half = blocks // len(to_refs)
        start = (place % half) * size
        to_refs[place // half][start : start + size, :] = rows.astype(BF16)


def weight_kernel(info_ref, left_ref, right_ref, *rest, order, blocks):
    side = info_ref[0]
    mine = len(rest) == 3
    to_refs = rest[-2:] if mine else rest
    cols = to_refs[0].shape[1]
    start = (side if mine else 1 - side) * cols

    @pl.loop(0, cols // CHUNK)
    def _(step):
        here = at(step * CHUNK, CHUNK)
        right = right_ref[:, at(start + step * CHUNK, CHUNK)]
        came = rest[0][:, here] if mine else None
        split_store(dot(left_ref[...], right, 1, 0), came, [ref.at[:, here] for ref in to_refs], order, blocks)


def weight_grad(info, left, right, order, blocks, came=None):
    width, rows = left.shape
    cols = right.shape[1] // 2
    kernel = functools.partial(weight_kernel, order=order, blocks=blocks)
    flops = 2 * width * rows * cols
    if came is None:
        return call(kernel, "weight_away", (info,), (left, right), [shape(BF16, width, cols)], flops)[0]
    return call(
        kernel, "weight_mine", (info,), (left, right, came), [shape(BF16, width // 2, cols)] * 2, flops
    )


def swiglu_back_kernel(
    info_ref, dm_ref, wd_ref, s_ref, t_ref, hbt_ref, dgt_ref, dup_ref, gate_ref, up_ref, *, orders, blocks
):
    half = gate_ref.shape[1]

    def grads(start):
        cols = at(start, CHUNK)
        grad = dot(dm_ref[...], wd_ref[cols, :], 1, 1)
        dup = (grad * s_ref[:, cols].astype(F32)).astype(BF16)
        dgt = (grad * t_ref[:, cols].astype(F32)).astype(BF16)
        dup_ref[:, cols] = dup
        dgt_ref[:, cols] = dgt
        return dgt, dup

    @pl.loop(0, half // CHUNK)
    def _(step):
        here = at(step * CHUNK, CHUNK)
        dgt, dup = grads((1 - info_ref[0]) * half + step * CHUNK)
        split_store(dot(hbt_ref[...], dgt, 1, 0), None, [gate_ref.at[:, here]], orders[0], blocks)
        split_store(dot(hbt_ref[...], dup, 1, 0), None, [up_ref.at[:, here]], orders[1], blocks)

    @pl.loop(0, half // CHUNK)
    def _(step):
        grads(info_ref[0] * half + step * CHUNK)


def swiglu_back(info, dm, wd, s, t, hbt, orders, blocks):
    rows, width = dm.shape
    ff = wd.shape[0]
    return call(
        functools.partial(swiglu_back_kernel, orders=orders, blocks=blocks), "swiglu_back", (info,),
        (dm, wd, s, t, hbt),
        [shape(BF16, rows, ff)] * 2 + [shape(BF16, width, ff // 2)] * 2,
        4 * rows * width * ff,
    )


def norm_one_kernel(
    info_ref, dgt_ref, dup_ref, wg_ref, wu_ref, r1_ref, dr2_ref, g1_ref, wo_ref, part_ref,
    dr1_ref, dat_ref, own_ref, away_ref, small_ref, acc_ref, da_ref, turn_ref, *, blocks,
):
    rows = r1_ref.shape[0]
    cols = own_ref.shape[0]
    side = info_ref[0]
    acc_ref[...] = dr2_ref[...]

    @pl.loop(0, wg_ref.shape[1] // WIDE)
    def _(step):
        here = at(step * WIDE, WIDE)
        acc_ref[...] += dot(dgt_ref[:, here], wg_ref[:, here], 1, 1) + dot(dup_ref[:, here], wu_ref[:, here], 1, 1)

    small_ref[...] = part_ref[...]

    @pl.loop(0, rows // ROWS)
    def _(index):
        here = at(index * ROWS, ROWS)
        dr1, dgain = norm_back(r1_ref[here, :], g1_ref[...], acc_ref[here, :])
        dr1_ref[here, :] = dr1
        da_ref[here, :] = dr1.astype(BF16)
        small_ref[0:1, :] += jnp.sum(dgain, axis=0, keepdims=True)

    away_ref[...] = dot(wo_ref[at((1 - side) * cols, cols), :], da_ref[...], 1, 1).astype(BF16)
    own_ref[...] = dot(wo_ref[at(side * cols, cols), :], da_ref[...], 1, 1).astype(BF16)
    turn_ref[...] = da_ref[...].T
    relative_rows(dat_ref, turn_ref, info_ref[1], blocks)


def norm_one(info, dgt, dup, wg, wu, r1, dr2, g1, w_out, part, blocks):
    rows, width = r1.shape
    ff = wg.shape[1]
    cols = w_out.shape[0] // 2
    return call(
        functools.partial(norm_one_kernel, blocks=blocks), "norm_one_back", (info,),
        (dgt, dup, wg, wu, r1, dr2, g1, w_out, part),
        [
            shape(F32, rows, width), shape(BF16, width, rows), shape(BF16, cols, rows),
            shape(BF16, cols, rows), shape(F32, 8, width),
        ],
        4 * rows * width * ff,
        [pltpu.VMEM((rows, width), F32), pltpu.VMEM((rows, width), BF16), pltpu.VMEM((width, rows), BF16)],
    )


def out_grad_kernel(dat_ref, mine_ref, came_ref, keep_ref, away_ref):
    away_ref[...] = dot(dat_ref[...], came_ref[...], 1, 1).astype(BF16)
    keep_ref[...] = dot(dat_ref[...], mine_ref[...], 1, 1).astype(BF16)


def out_grad(dat, mine, came):
    width, rows = dat.shape
    cols = mine.shape[0]
    return call(
        out_grad_kernel, "out_grad", (), (dat, mine, came), [shape(BF16, width, cols)] * 2,
        4 * width * rows * cols,
    )


def project_grad_kernel(info_ref, x_ref, dq_ref, dk_ref, dv_ref, mine_ref, came_ref, *rest, orders, blocks):
    out_refs, (turn_ref, left_ref) = rest[:-2], rest[-2:]
    turn_ref[...] = x_ref[...].T
    relative_rows(left_ref, turn_ref, info_ref[1], blocks)
    left = left_ref[...]
    cols = dq_ref.shape[0]
    piece = cols // 3
    for index, grad_ref in enumerate((dq_ref, dk_ref, dv_ref)):
        lanes = slice(index * piece, (index + 1) * piece)
        pair = out_refs[2 * index : 2 * index + 2]
        main = [ref.at[:, 0:cols] for ref in pair]
        tail = [ref.at[:, cols : cols + piece] for ref in pair]
        split_store(dot(left, grad_ref[...], 1, 1), None, main, orders[index], blocks)
        both = mine_ref[:, lanes].astype(F32) + came_ref[:, lanes].astype(F32)
        split_store(both, None, tail, orders[index], blocks)


def project_grad(info, x, grads, mine, came, orders, blocks):
    rows, width = x.shape
    cols = grads[0].shape[0]
    wide = cols + cols // 3
    return call(
        functools.partial(project_grad_kernel, orders=orders, blocks=blocks), "project_grad", (info,),
        (x, *grads, mine, came), [shape(BF16, width // 2, wide)] * 6, 6 * rows * width * cols,
        [pltpu.VMEM((width, rows), BF16)] * 2,
    )


def stream_grad_kernel(info_ref, dq_ref, dk_ref, dv_ref, wq_ref, wk_ref, wv_ref, *rest):
    cols, pack = dq_ref.shape
    rows = pack // 2
    side = info_ref[0]
    mine = len(rest) == 3
    lanes = at((side if mine else 1 - side) * rows, rows)
    total = sum(
        dot(w_ref[:, at(side * cols, cols)], g_ref[:, lanes], 1, 0)
        for w_ref, g_ref in ((wq_ref, dq_ref), (wk_ref, dk_ref), (wv_ref, dv_ref))
    )
    if mine:
        came_ref, dr1_ref, out_ref = rest
        total = total + came_ref[...].astype(F32)
        out_ref[...] = (dr1_ref[...] + total.T).astype(BF16)
    else:
        rest[0][...] = total.astype(BF16)


def stream_grad(info, grads, weights, *others):
    cols, pack = grads[0].shape
    width = weights[0].shape[0]
    rows = pack // 2
    out = (rows, width) if others else (width, rows)
    return call(
        stream_grad_kernel, "stream_grad", (info,), (*grads, *weights, *others), [shape(BF16, *out)],
        6 * rows * width * cols,
    )[0]


def stage_order(bits, turn):
    last = bits - 1
    return [(turn + step) % last for step in range(last)] + [last]


def swap_seq(value):
    return lax.ppermute(value, "seq", [(0, 1), (1, 0)])


def swap_dp(value, bit):
    size = lax.axis_size("dp")
    return lax.ppermute(value, "dp", [(i, i ^ (1 << bit)) for i in range(size)])


def sum_everywhere(value):
    value = value + swap_seq(value)
    for bit in range(lax.axis_size("dp").bit_length() - 1):
        value = value + swap_dp(value, bit)
    return value


class Halving:
    def __init__(self, keep, away, order, shift):
        self.keep, self.order, self.shift = keep, order, shift
        self.sent, self.step = away, 0

    def send(self):
        self.came = swap_dp(self.sent, self.order[self.step] + self.shift)
        self.step += 1

    def receive(self):
        rows = self.keep.shape[0] // 2
        if self.step < len(self.order):
            self.sent = self.add(rows, 2 * rows)
            self.keep = self.add(0, rows)
        else:
            self.keep = self.keep.astype(F32) + self.came.astype(F32)

    def add(self, low, high):
        return (self.keep[low:high].astype(F32) + self.came[low:high].astype(F32)).astype(BF16)

    def rest(self):
        value = self.keep
        for bit in reversed(range(self.shift)):
            half = value.shape[0] // 2
            mine = (lax.axis_index("dp") >> bit) & 1
            keep = lax.dynamic_slice_in_dim(value, mine * half, half, 0)
            away = lax.dynamic_slice_in_dim(value, (1 - mine) * half, half, 0)
            value = keep + swap_dp(away.astype(BF16), bit).astype(F32)
        return value


def after(values, *others):
    return lax.optimization_barrier((values, others))[0]


def shards(
    tokens,
    doc_lengths,
    w_query,
    w_key,
    w_value,
    w_out,
    w_gate,
    w_up,
    w_down,
    gain_attn,
    gain_ffn,
    cotangent,
):
    row_count, width = tokens.shape
    head_cols = w_query.shape[1] // lax.axis_size("seq")
    dp_size = lax.axis_size("dp")
    blocks = min(dp_size, 16)
    bits = blocks.bit_length() - 1
    shift = (dp_size // blocks).bit_length() - 1
    orders = [stage_order(bits, turn) for turn in range(3)]
    lengths = doc_lengths[0]
    seq_index = lax.axis_index("seq")
    info = jnp.stack([seq_index, lax.axis_index("dp") >> shift]).astype(jnp.int32)
    gain_one, gain_two = gain_attn.reshape(1, width), gain_ffn.reshape(1, width)

    weights = (w_query, w_key, w_value)
    gathered, query, key, value, context, mine, away, lse = attention_forward(
        info, lengths, tokens, swap_seq(tokens), weights
    )
    kept = (query, key, value, context, lse)
    came = swap_seq(away)
    act, silu, slope, result, dm, dm_turned, hb_turned, dr2, r1, small = ffn_forward(
        info, lengths, tokens, mine, came, w_out, gain_one, gain_two, w_gate, w_up, w_down, cotangent, blocks
    )
    down_came = swap_seq(weight_grad(info, dm_turned, act, orders[2], blocks))
    dgt, dup, gate_away, up_away = swiglu_back(
        info, dm, w_down, silu, slope, hb_turned, orders[:2], blocks
    )
    gate_came, up_came = swap_seq(gate_away), swap_seq(up_away)
    down = Halving(*weight_grad(info, dm_turned, after(act, gate_away), orders[2], blocks, down_came), orders[2], shift)
    down.send()
    gate = Halving(*weight_grad(info, after(hb_turned, down.sent), dgt, orders[0], blocks, gate_came), orders[0], shift)
    gate.send()
    up = Halving(*weight_grad(info, after(hb_turned, gate.sent), dup, orders[1], blocks, up_came), orders[1], shift)
    up.send()
    dr1, da_turned, own_rows, away_rows, small = norm_one(
        info, after(dgt, up.sent), dup, w_gate, w_up, r1, dr2, gain_one, w_out, small, blocks
    )
    came_rows = swap_seq(away_rows)
    out_keep, out_away = out_grad(da_turned, mine, came)
    out_came = swap_seq(out_away)
    small = sum_everywhere(small)
    steps = 4
    each = head_cols // HDIM // steps
    grads = ()
    ffn = [down, gate, up]
    for step in range(steps):
        if step >= 2:
            for part in ffn:
                part.receive()
                part.send()
            own_rows = after(own_rows, *[part.sent for part in ffn])
        grads = attention_backward(
            info, lengths, kept, own_rows, came_rows, step * each, each, grads
        )
    sides = project_grad(info, gathered, grads, out_keep, out_came, orders, blocks)
    attn = [
        Halving(sides[2 * index], sides[2 * index + 1], orders[index], shift) for index in range(3)
    ]
    for part in attn:
        part.send()
    stream_away = stream_grad(info, after(grads, *sides), weights)
    grad_tokens = stream_grad(info, grads, weights, swap_seq(stream_away), dr1)
    while ffn[0].step < bits:
        for part in ffn:
            part.receive()
            part.send()
    for part in ffn:
        part.receive()
    while attn[0].step < bits:
        for part in attn:
            part.receive()
            part.send()
    for part in attn:
        part.receive()
    summed_down, summed_gate, summed_up = (part.rest() for part in ffn)
    sums = [part.rest() for part in attn]
    summed_out = jnp.concatenate([total[:, head_cols:] for total in sums], axis=1)
    squares = jnp.sum(small[2:5], axis=1)
    rms_values = jnp.sqrt(squares / (small[5, 0] * width))
    return (
        result,
        grad_tokens,
        sums[0][:, :head_cols],
        sums[1][:, :head_cols],
        sums[2][:, :head_cols],
        summed_out.T,
        summed_gate,
        summed_up,
        summed_down.T,
        small[0],
        small[1],
        rms_values,
    )


def solution(mesh):
    return jax.shard_map(
        shards,
        mesh=mesh,
        in_specs=(
            P(("dp", "seq"), None),
            P("dp", None),
            P(),
            P(),
            P(),
            P(),
            P(),
            P(),
            P(),
            P(),
            P(),
            P(("dp", "seq"), None),
        ),
        out_specs=(
            P(("dp", "seq"), None),
            P(("dp", "seq"), None),
            P("dp", "seq"),
            P("dp", "seq"),
            P("dp", "seq"),
            P("seq", "dp"),
            P("dp", "seq"),
            P("dp", "seq"),
            P("seq", "dp"),
            P(),
            P(),
            P(),
        ),
        check_vma=False,
    )
```

```python
import functools
import math

import jax
import jax.numpy as jnp
import numpy as np
from jax import lax
from jax.experimental import pallas as pl
from jax.experimental.pallas import tpu as pltpu
from jax.sharding import PartitionSpec as P

HDIM = 48
HALF = HDIM // 2
SCORE = 1.0 / math.sqrt(HDIM)
LOG2E = 1.0 / math.log(2.0)
NEG = -1e30
BF16 = jnp.bfloat16
F32 = jnp.float32
CHUNK = 256
WIDE = 512
ROWS = 64
SPANS = 4
PLAN = ((0,), (1,))
MIB = 1 << 20
EASE = 50


def call(kernel, name, scalars, arrays, out_shape, flops, scratch=(), room=16, aliases=None):
    moved = sum(math.prod(o.shape) * o.dtype.itemsize for o in out_shape)
    return pl.pallas_call(
        kernel,
        in_specs=[pl.BlockSpec(memory_space=pltpu.SMEM)] * len(scalars)
        + [pl.BlockSpec(memory_space=pltpu.VMEM)] * len(arrays),
        out_specs=[pl.BlockSpec(memory_space=pltpu.VMEM)] * len(out_shape),
        out_shape=out_shape,
        scratch_shapes=list(scratch),
        input_output_aliases=aliases or {},
        cost_estimate=pl.CostEstimate(flops=flops // EASE, bytes_accessed=moved // EASE, transcendentals=0),
        compiler_params=pltpu.CompilerParams(vmem_limit_bytes=room * MIB),
        name=name,
    )(*scalars, *arrays)


def shape(dtype, *dims):
    return jax.ShapeDtypeStruct(dims, dtype)


def at(start, size):
    return pl.ds(pl.multiple_of(start, size), size)


def dot(a, b, ca, cb):
    return lax.dot_general(a, b, (((ca,), (cb,)), ((), ())), preferred_element_type=F32)


def rope_tables(span):
    freq = 10000.0 ** (-np.arange(HALF, dtype=np.float64) / HALF)
    phase = freq[:, None] * np.arange(span, dtype=np.float64)[None, :]
    return np.cos(phase).astype(np.float32), np.sin(phase).astype(np.float32)


def block_facts(len_ref, block):
    ends = []
    total = 0
    for index in range(len_ref.shape[0]):
        total = total + len_ref[index]
        ends.append(total)
    segments, openings = [], []
    for number in range(SPANS):
        segment = 0
        opening = 0
        for index, end in enumerate(ends):
            done = number * block >= end
            segment = segment + done.astype(jnp.int32)
            opening = opening + jnp.where(done, len_ref[index], 0)
        segments.append(segment)
        openings.append(opening)
    return segments, openings


def causal(block):
    key = lax.broadcasted_iota(jnp.int32, (block, block), 0)
    return key <= lax.broadcasted_iota(jnp.int32, (block, block), 1)


def project(to_refs, weights, x, openings, cos_ref, sin_ref, start):
    rows = x.shape[0]
    cols, pack = to_refs[0].shape
    block = pack // SPANS
    for weight, to_ref, scale in zip(weights, to_refs, (SCORE * LOG2E, 1.0, None)):
        for number in range(rows // block):
            part = dot(weight, x[number * block : (number + 1) * block], 1, 1)
            first = start + number * block
            if scale is None:
                to_ref[:, at(first, block)] = part.astype(BF16)
                continue
            opening = functools.reduce(
                lambda rest, span: jnp.where(first == span * block, openings[span], rest), range(SPANS), 0
            )
            here = at(first - opening, block)
            cos = cos_ref[:, here] * scale
            sin = sin_ref[:, here] * scale
            for head in range(cols // HDIM):
                a = part[head * HDIM : head * HDIM + HALF]
                b = part[head * HDIM + HALF : (head + 1) * HDIM]
                turned = jnp.concatenate([a * cos - b * sin, b * cos + a * sin], axis=0)
                to_ref[head * HDIM : (head + 1) * HDIM, at(first, block)] = turned.astype(BF16)


def project_own_kernel(
    info_ref, len_ref, x_ref, cos_ref, sin_ref, wq_ref, wk_ref, wv_ref,
    q_ref, k_ref, v_ref, all_ref, turned_ref, cq_ref, ck_ref, cv_ref, sems,
):
    cols, pack = q_ref.shape
    rows = x_ref.shape[0]
    side = info_ref[0]
    copies = []
    for index, (w_ref, c_ref) in enumerate(((wq_ref, cq_ref), (wk_ref, ck_ref), (wv_ref, cv_ref))):
        copies.append(pltpu.make_async_copy(w_ref.at[:, at(side * cols, cols)], c_ref, sems.at[index]))
        copies[-1].start()
    _, openings = block_facts(len_ref, pack // SPANS)
    all_ref[at(side * rows, rows), :] = x_ref[...]
    for index, c_ref in enumerate((cq_ref, ck_ref, cv_ref)):
        copies[index].wait()
        turned_ref[index * cols : (index + 1) * cols, :] = c_ref[...].T
    weights = [turned_ref[index * cols : (index + 1) * cols, :] for index in range(3)]
    project((q_ref, k_ref, v_ref), weights, x_ref[...], openings, cos_ref, sin_ref, side * rows)


def project_own(info, lengths, own, weights):
    rows, width = own.shape
    pack = 2 * rows
    cols = weights[0].shape[1] // 2
    vmem = pl.BlockSpec(memory_space=pltpu.VMEM)
    smem = pl.BlockSpec(memory_space=pltpu.SMEM)
    return pl.pallas_call(
        project_own_kernel,
        in_specs=[smem] * 2 + [vmem] * 3 + [pl.BlockSpec(memory_space=pltpu.HBM)] * 3,
        out_specs=[vmem] * 8,
        out_shape=[shape(BF16, cols, pack)] * 3
        + [shape(BF16, pack, width), shape(BF16, 3 * cols, width)]
        + [shape(BF16, width, cols)] * 3,
        scratch_shapes=[pltpu.SemaphoreType.DMA((3,))],
        cost_estimate=pl.CostEstimate(flops=4_000_000_000, bytes_accessed=8_000_000, transcendentals=0),
        compiler_params=pltpu.CompilerParams(vmem_limit_bytes=8 * MIB),
        name="project_own",
    )(info, lengths, own, *rope_tables(pack), *weights)


def attention_forward_kernel(
    info_ref, len_ref, _, __, ___, ____, oth_ref, turned_ref, cos_ref, sin_ref,
    q_ref, k_ref, v_ref, x_ref, ctx_ref, mine_ref, away_ref, lse_ref,
):
    rows = oth_ref.shape[0]
    cols, pack = q_ref.shape
    heads = cols // HDIM
    block = pack // SPANS
    segments, openings = block_facts(len_ref, block)
    side = info_ref[0]
    x_ref[at((1 - side) * rows, rows), :] = oth_ref[...]
    weights = [turned_ref[index * cols : (index + 1) * cols, :] for index in range(3)]
    project((q_ref, k_ref, v_ref), weights, oth_ref[...], openings, cos_ref, sin_ref, (1 - side) * rows)
    below = causal(block)

    @pl.loop(0, heads)
    def _(head):
        here = at(head * HDIM, HDIM)
        keys = k_ref[here, :].T
        value = v_ref[here, :]
        for i in range(SPANS):
            lanes = slice(i * block, (i + 1) * block)
            query = q_ref[here, lanes]
            scores, biases, tops = [], [], []
            for j in range(i + 1):
                score = dot(keys[j * block : (j + 1) * block], query, 1, 0)
                bias = 0.0
                if j == i:
                    score = jnp.where(below, score, NEG)
                else:
                    bias = jnp.where(segments[i] == segments[j], 0.0, NEG)
                scores.append(score)
                biases.append(bias)
                tops.append(jnp.max(score, axis=0, keepdims=True) + bias)
            top = functools.reduce(jnp.maximum, tops)
            total = jnp.zeros((1, block), F32)
            context = jnp.zeros((HDIM, block), F32)
            for j in range(i + 1):
                prob = jnp.exp2(scores[j] - (top - biases[j]))
                total = total + jnp.sum(prob, axis=0, keepdims=True)
                context = context + dot(value[:, j * block : (j + 1) * block], prob.astype(BF16), 1, 0)
            ctx_ref[here, lanes] = (context * (1.0 / total)).astype(BF16)
            lse_ref[head, :, lanes] = top + jnp.log2(total)
        mine_ref[here, :] = ctx_ref[here, at(side * rows, rows)]
        away_ref[here, :] = ctx_ref[here, at((1 - side) * rows, rows)]


def attention_forward(info, lengths, started, oth, turned):
    rows, width = oth.shape
    cols, pack = started[0].shape
    heads = cols // HDIM
    half = shape(BF16, cols, rows)
    return call(
        attention_forward_kernel, "attention_forward", (info, lengths),
        (*started, oth, turned, *rope_tables(pack)),
        [shape(BF16, cols, pack)] * 3 + [shape(BF16, pack, width), shape(BF16, cols, pack)]
        + [half, half, shape(F32, heads, 1, pack)],
        15_000_000_000,
        aliases={2 + index: index for index in range(4)},
    )


def attention_backward_kernel(
    info_ref, len_ref, q_ref, k_ref, v_ref, ctx_ref, own_ref, oth_ref, lse_ref, cos_ref, sin_ref, *rest,
    first, heads,
):
    dq_ref, dk_ref, dv_ref, dctx_ref = rest[-4:]
    rows = own_ref.shape[1]
    pack = q_ref.shape[1]
    block = pack // SPANS
    segments, openings = block_facts(len_ref, block)
    side = info_ref[0]
    below = causal(block)
    spans = [slice(number * block, (number + 1) * block) for number in range(SPANS)]

    def unturn(value, number, scale):
        here = at(number * block - openings[number], block)
        cos = cos_ref[:, here] * scale
        sin = sin_ref[:, here] * scale
        a, b = value[:HALF], value[HALF:]
        return jnp.concatenate([a * cos + b * sin, b * cos - a * sin], axis=0).astype(BF16)

    def plus(sums, index, value):
        sums[index] = sums[index] + value if index in sums else value

    @pl.loop(first, first + heads, unroll=2)
    def _(head):
        here = at(head * HDIM, HDIM)
        dctx_ref[:, at(side * rows, rows)] = own_ref[here, :]
        dctx_ref[:, at((1 - side) * rows, rows)] = oth_ref[here, :]
        key = k_ref[here, :]
        keys = key.T
        values = v_ref[here, :].T
        delta = jnp.sum(dctx_ref[...].astype(F32) * ctx_ref[here, :].astype(F32), axis=0, keepdims=True)
        lse = lse_ref[head, :, :]
        raw, done, dqs, dks, dvs = {}, {}, {}, {}, {}

        def scores(i, j):
            return (
                dot(keys[spans[j]], q_ref[here, spans[i]], 1, 0),
                dot(values[spans[j]], dctx_ref[:, spans[i]], 1, 0),
            )

        def slopes(i, j, score, slope):
            top = lse[:, spans[i]]
            if j == i:
                prob = jnp.exp2(jnp.where(below, score, NEG) - top)
            else:
                prob = jnp.exp2(score - (top - jnp.where(segments[i] == segments[j], 0.0, NEG)))
            return prob.astype(BF16), (prob * (slope - delta[:, spans[i]])).astype(BF16)

        def products(i, j, prob, dscore):
            plus(dqs, i, dot(key[:, spans[j]], dscore, 1, 0))
            plus(dks, j, dot(q_ref[here, spans[i]], dscore, 1, 1))
            plus(dvs, j, dot(dctx_ref[:, spans[i]], prob, 1, 1))

        pairs = [(i, j) for i in range(SPANS) for j in range(i + 1)]
        for step in range(len(pairs) + 2):
            if step < len(pairs):
                raw[step] = scores(*pairs[step])
            if 0 <= step - 1 < len(pairs):
                done[step - 1] = slopes(*pairs[step - 1], *raw.pop(step - 1))
            if 0 <= step - 2:
                products(*pairs[step - 2], *done.pop(step - 2))
        for number, lanes in enumerate(spans):
            dq_ref[here, lanes] = unturn(dqs[number], number, SCORE)
            dk_ref[here, lanes] = unturn(dks[number], number, 1.0 / LOG2E)
            dv_ref[here, lanes] = dvs[number].astype(BF16)


def attention_backward(info, lengths, kept, own, oth, first, heads, sofar):
    query, key, value, context, lse = kept
    cols, pack = query.shape
    arrays = (query, key, value, context, own, oth, lse, *rope_tables(pack), *sofar)
    base = 2 + len(arrays) - len(sofar)
    return call(
        functools.partial(attention_backward_kernel, first=first, heads=heads),
        "attention_backward", (info, lengths), arrays, [shape(BF16, cols, pack)] * 3,
        heads * 3_000_000_000,
        [pltpu.VMEM((HDIM, pack), BF16)],
        aliases={base + index: index for index in range(len(sofar))},
    )


def inverse_rms(value):
    return lax.rsqrt(jnp.mean(value * value, axis=-1, keepdims=True) + 1e-06)


def norm_back(value, gain, grad):
    inv = inverse_rms(value)
    scaled = grad * gain
    slope = jnp.mean(scaled * value, axis=-1, keepdims=True) * (inv * inv * inv)
    return scaled * inv - value * slope, grad * value * inv


def relative_rows(to_ref, from_ref, place, blocks):
    size = from_ref.shape[0] // blocks
    for block in range(blocks):
        to_ref[block * size : (block + 1) * size, :] = from_ref[at((block ^ place) * size, size), :]


def position(block, order):
    last = len(order) - 1
    return sum(((block >> bit) & 1) << (last - step) for step, bit in enumerate(order))


def ffn_forward_kernel(
    info_ref, len_ref, x_ref, mine_ref, came_ref, wo_ref, g1_ref, g2_ref, wg_ref, wu_ref, wd_ref, cot_ref,
    act_ref, s_ref, t_ref, out_ref, dm_ref, dmt_ref, hbt_ref, dr2_ref, r1_ref, small_ref,
    hb_ref, h_ref, m_ref, turn_ref, *, blocks,
):
    rows, width = x_ref.shape
    part = mine_ref.shape[0]
    total = len_ref[0] + len_ref[1] + len_ref[2] + len_ref[3]
    side = info_ref[0]
    first = side * rows

    def valid_of(start):
        places = lax.broadcasted_iota(jnp.int32, (ROWS, 1), 0) + (start + first)
        return (places < total).astype(F32)

    def squares(row, value, valid):
        add_small(small_ref, row, jnp.sum(value * value * valid, axis=0, keepdims=True))

    small_ref[...] = jnp.zeros_like(small_ref)
    m_ref[...] = dot(mine_ref[...].T, wo_ref[at(side * part, part), :], 1, 0) + dot(
        came_ref[...].T, wo_ref[at((1 - side) * part, part), :], 1, 0
    )

    @pl.loop(0, rows // ROWS)
    def _(index):
        here = at(index * ROWS, ROWS)
        valid = valid_of(index * ROWS)
        x = x_ref[here, :].astype(F32)
        a = m_ref[here, :]
        r1 = x + a
        h = r1 * inverse_rms(r1) * g1_ref[...]
        r1_ref[here, :] = r1
        h_ref[here, :] = h
        hb_ref[here, :] = h.astype(BF16)
        squares(2, x, valid)
        squares(3, a, valid)

    turn_ref[...] = hb_ref[...].T
    relative_rows(hbt_ref, turn_ref, info_ref[1], blocks)
    m_ref[...] = jnp.zeros_like(m_ref)

    @pl.loop(0, act_ref.shape[1] // WIDE)
    def _(step):
        cols = at(step * WIDE, WIDE)
        gate = dot(hb_ref[...], wg_ref[:, cols], 1, 0)
        up = dot(hb_ref[...], wu_ref[:, cols], 1, 0)
        sig = 1.0 / (1.0 + jnp.exp(-gate))
        silu = gate * sig
        act = (silu * up).astype(BF16)
        act_ref[:, cols] = act
        s_ref[:, cols] = silu.astype(BF16)
        t_ref[:, cols] = (up * (sig + silu * (1.0 - sig))).astype(BF16)
        m_ref[...] += dot(act, wd_ref[cols, :], 1, 0)

    @pl.loop(0, rows // ROWS)
    def _(index):
        here = at(index * ROWS, ROWS)
        valid = valid_of(index * ROWS)
        m = m_ref[here, :]
        r2 = h_ref[here, :] + m
        gain = g2_ref[...]
        dr2, dgain = norm_back(r2, gain, cot_ref[here, :].astype(F32) * valid)
        out_ref[here, :] = (r2 * inverse_rms(r2) * gain).astype(BF16)
        dr2_ref[here, :] = dr2
        dm_ref[here, :] = dr2.astype(BF16)
        add_small(small_ref, 1, jnp.sum(dgain, axis=0, keepdims=True))
        squares(4, m, valid)

    add_small(small_ref, 5, jnp.full((1, width), jnp.clip(total - first, 0, rows).astype(F32)))
    turn_ref[...] = dm_ref[...].T
    relative_rows(dmt_ref, turn_ref, info_ref[1], blocks)


def ffn_forward(info, lengths, x, mine, came, w_out, g1, g2, wg, wu, wd, cot, blocks):
    rows, width = x.shape
    ff = wg.shape[1]
    return call(
        functools.partial(ffn_forward_kernel, blocks=blocks), "ffn_forward", (info, lengths),
        (x, mine, came, w_out, g1, g2, wg, wu, wd, cot),
        [shape(BF16, rows, ff)] * 3 + [shape(BF16, rows, width)] * 2 + [shape(BF16, width, rows)] * 2
        + [shape(F32, rows, width)] * 2 + [shape(F32, 16, WIDE)],
        6 * rows * width * ff,
        [
            pltpu.VMEM((rows, width), BF16), pltpu.VMEM((rows, width), F32),
            pltpu.VMEM((rows, width), F32), pltpu.VMEM((width, rows), BF16),
        ],
    )


def add_small(small_ref, row, value):
    for piece in range(-(-value.shape[1] // WIDE)):
        part = value[:, piece * WIDE : (piece + 1) * WIDE]
        small_ref[2 * row + piece : 2 * row + piece + 1, 0 : part.shape[1]] += part


def split_store(product, came, to_refs, order, blocks):
    size = product.shape[0] // blocks
    for block in range(blocks):
        place = position(block, order)
        rows = product[block * size : (block + 1) * size]
        if came is not None:
            rows = rows + came[place * size : (place + 1) * size].astype(F32)
        half = blocks // len(to_refs)
        start = (place % half) * size
        to_refs[place // half][start : start + size, :] = rows.astype(BF16)


def weight_kernel(info_ref, left_ref, right_ref, *rest, order, blocks):
    side = info_ref[0]
    mine = len(rest) == 3
    to_refs = rest[-2:] if mine else rest
    cols = to_refs[0].shape[1]
    start = (side if mine else 1 - side) * cols

    @pl.loop(0, cols // CHUNK)
    def _(step):
        here = at(step * CHUNK, CHUNK)
        right = right_ref[:, at(start + step * CHUNK, CHUNK)]
        came = rest[0][:, here] if mine else None
        split_store(dot(left_ref[...], right, 1, 0), came, [ref.at[:, here] for ref in to_refs], order, blocks)


def weight_grad(info, left, right, order, blocks, came=None):
    width, rows = left.shape
    cols = right.shape[1] // 2
    kernel = functools.partial(weight_kernel, order=order, blocks=blocks)
    flops = 2 * width * rows * cols
    if came is None:
        return call(kernel, "weight_away", (info,), (left, right), [shape(BF16, width, cols)], flops)[0]
    return call(
        kernel, "weight_mine", (info,), (left, right, came), [shape(BF16, width // 2, cols)] * 2, flops
    )


def swiglu_away_kernel(
    info_ref, dm_ref, wd_ref, s_ref, t_ref, hbt_ref, dgt_ref, dup_ref, gate_ref, up_ref, *, orders, blocks
):
    half = gate_ref.shape[1]

    @pl.loop(0, half // CHUNK)
    def _(step):
        here = at(step * CHUNK, CHUNK)
        dgt, dup = swiglu_grads(
            (1 - info_ref[0]) * half + step * CHUNK, dm_ref, wd_ref, s_ref, t_ref, dgt_ref, dup_ref
        )
        split_store(dot(hbt_ref[...], dgt, 1, 0), None, [gate_ref.at[:, here]], orders[0], blocks)
        split_store(dot(hbt_ref[...], dup, 1, 0), None, [up_ref.at[:, here]], orders[1], blocks)


def swiglu_grads(start, dm_ref, wd_ref, s_ref, t_ref, dgt_ref, dup_ref):
    cols = at(start, CHUNK)
    grad = dot(dm_ref[...], wd_ref[cols, :], 1, 1)
    dup = (grad * s_ref[:, cols].astype(F32)).astype(BF16)
    dgt = (grad * t_ref[:, cols].astype(F32)).astype(BF16)
    dup_ref[:, cols] = dup
    dgt_ref[:, cols] = dgt
    return dgt, dup


def swiglu_mine_kernel(info_ref, dm_ref, wd_ref, s_ref, t_ref, _, __, dgt_ref, dup_ref):
    half = s_ref.shape[1] // 2

    @pl.loop(0, half // CHUNK)
    def _(step):
        swiglu_grads(info_ref[0] * half + step * CHUNK, dm_ref, wd_ref, s_ref, t_ref, dgt_ref, dup_ref)


def swiglu_away(info, dm, wd, s, t, hbt, orders, blocks):
    rows, width = dm.shape
    ff = wd.shape[0]
    return call(
        functools.partial(swiglu_away_kernel, orders=orders, blocks=blocks), "swiglu_away", (info,),
        (dm, wd, s, t, hbt),
        [shape(BF16, rows, ff)] * 2 + [shape(BF16, width, ff // 2)] * 2,
        3 * rows * width * ff,
    )


def swiglu_mine(info, dm, wd, s, t, dgt, dup):
    return call(
        swiglu_mine_kernel, "swiglu_mine", (info,), (dm, wd, s, t, dgt, dup), [shape(BF16, *dgt.shape)] * 2,
        dm.shape[0] * dm.shape[1] * wd.shape[0], aliases={5: 0, 6: 1},
    )


def norm_one_kernel(
    info_ref, dgt_ref, dup_ref, wg_ref, wu_ref, r1_ref, dr2_ref, g1_ref, wo_ref, part_ref,
    dr1_ref, dat_ref, own_ref, away_ref, small_ref, acc_ref, da_ref, turn_ref, *, blocks,
):
    rows = r1_ref.shape[0]
    cols = own_ref.shape[0]
    side = info_ref[0]
    acc_ref[...] = dr2_ref[...]

    @pl.loop(0, wg_ref.shape[1] // WIDE)
    def _(step):
        here = at(step * WIDE, WIDE)
        acc_ref[...] += dot(dgt_ref[:, here], wg_ref[:, here], 1, 1) + dot(dup_ref[:, here], wu_ref[:, here], 1, 1)

    small_ref[...] = part_ref[...]

    @pl.loop(0, rows // ROWS)
    def _(index):
        here = at(index * ROWS, ROWS)
        dr1, dgain = norm_back(r1_ref[here, :], g1_ref[...], acc_ref[here, :])
        dr1_ref[here, :] = dr1
        da_ref[here, :] = dr1.astype(BF16)
        add_small(small_ref, 0, jnp.sum(dgain, axis=0, keepdims=True))

    away_ref[...] = dot(wo_ref[at((1 - side) * cols, cols), :], da_ref[...], 1, 1).astype(BF16)
    own_ref[...] = dot(wo_ref[at(side * cols, cols), :], da_ref[...], 1, 1).astype(BF16)
    turn_ref[...] = da_ref[...].T
    relative_rows(dat_ref, turn_ref, info_ref[1], blocks)


def norm_one(info, dgt, dup, wg, wu, r1, dr2, g1, w_out, part, blocks):
    rows, width = r1.shape
    ff = wg.shape[1]
    cols = w_out.shape[0] // 2
    return call(
        functools.partial(norm_one_kernel, blocks=blocks), "norm_one_back", (info,),
        (dgt, dup, wg, wu, r1, dr2, g1, w_out, part),
        [
            shape(F32, rows, width), shape(BF16, width, rows), shape(BF16, cols, rows),
            shape(BF16, cols, rows), shape(F32, 16, WIDE),
        ],
        4 * rows * width * ff,
        [pltpu.VMEM((rows, width), F32), pltpu.VMEM((rows, width), BF16), pltpu.VMEM((width, rows), BF16)],
    )


def out_grad_kernel(dat_ref, mine_ref, came_ref, keep_ref, away_ref):
    away_ref[...] = dot(dat_ref[...], came_ref[...], 1, 1).astype(BF16)
    keep_ref[...] = dot(dat_ref[...], mine_ref[...], 1, 1).astype(BF16)


def out_grad(dat, mine, came):
    width, rows = dat.shape
    cols = mine.shape[0]
    return call(
        out_grad_kernel, "out_grad", (), (dat, mine, came), [shape(BF16, width, cols)] * 2,
        4 * width * rows * cols,
    )


def project_grad_kernel(info_ref, x_ref, dq_ref, dk_ref, dv_ref, mine_ref, came_ref, *rest, orders, blocks):
    out_refs, (turn_ref, left_ref) = rest[:-2], rest[-2:]
    turn_ref[...] = x_ref[...].T
    relative_rows(left_ref, turn_ref, info_ref[1], blocks)
    left = left_ref[...]
    cols = dq_ref.shape[0]
    piece = cols // 3
    for index, grad_ref in enumerate((dq_ref, dk_ref, dv_ref)):
        lanes = slice(index * piece, (index + 1) * piece)
        pair = out_refs[2 * index : 2 * index + 2]
        main = [ref.at[:, 0:cols] for ref in pair]
        tail = [ref.at[:, cols : cols + piece] for ref in pair]
        split_store(dot(left, grad_ref[...], 1, 1), None, main, orders[index], blocks)
        both = mine_ref[:, lanes].astype(F32) + came_ref[:, lanes].astype(F32)
        split_store(both, None, tail, orders[index], blocks)


def project_grad(info, x, grads, mine, came, orders, blocks):
    rows, width = x.shape
    cols = grads[0].shape[0]
    wide = cols + cols // 3
    return call(
        functools.partial(project_grad_kernel, orders=orders, blocks=blocks), "project_grad", (info,),
        (x, *grads, mine, came), [shape(BF16, width // 2, wide)] * 6, 6 * rows * width * cols,
        [pltpu.VMEM((width, rows), BF16)] * 2,
    )


def stream_grad_kernel(info_ref, dq_ref, dk_ref, dv_ref, wq_ref, wk_ref, wv_ref, *rest):
    cols, pack = dq_ref.shape
    rows = pack // 2
    side = info_ref[0]
    mine = len(rest) == 3
    lanes = at((side if mine else 1 - side) * rows, rows)
    total = sum(
        dot(w_ref[...], g_ref[:, lanes], 1, 0)
        for w_ref, g_ref in ((wq_ref, dq_ref), (wk_ref, dk_ref), (wv_ref, dv_ref))
    )
    if mine:
        came_ref, dr1_ref, out_ref = rest
        total = total + came_ref[...].astype(F32)
        out_ref[...] = (dr1_ref[...] + total.T).astype(BF16)
    else:
        rest[0][...] = total.astype(BF16)


def stream_grad(info, grads, weights, *others):
    cols, pack = grads[0].shape
    width = weights[0].shape[0]
    rows = pack // 2
    out = (rows, width) if others else (width, rows)
    return call(
        stream_grad_kernel, "stream_grad", (info,), (*grads, *weights, *others), [shape(BF16, *out)],
        6 * rows * width * cols,
    )[0]


def stage_order(bits, turn):
    last = bits - 1
    return [(turn + step) % last for step in range(last)] + [last]


def swap_seq(value):
    return lax.ppermute(value, "seq", [(0, 1), (1, 0)])


def swap_dp(value, bit):
    size = lax.axis_size("dp")
    return lax.ppermute(value, "dp", [(i, i ^ (1 << bit)) for i in range(size)])


def halves_of(small):
    high = lax.reduce_precision(small, 8, 7)
    return high.astype(BF16), (small - high).astype(BF16)


def whole_of(high, low):
    return high.astype(F32) + low.astype(F32)


class Halving:
    def __init__(self, keep, away, order, shift, small=None):
        self.keep, self.order, self.shift, self.small = keep, order, shift, small
        self.sent, self.step = away, 0

    def send(self):
        if self.small is not None:
            self.pair = halves_of(self.small)
            self.sent = jnp.concatenate([self.sent, *self.pair], axis=0)
        self.came = swap_dp(self.sent, self.order[self.step] + self.shift)
        self.step += 1

    def receive(self):
        rows = self.keep.shape[0]
        if self.small is not None:
            count = self.small.shape[0]
            came = self.came[rows : rows + count], self.came[rows + count :]
            self.small = whole_of(*self.pair) + whole_of(*came)
        if self.step < len(self.order):
            self.sent = self.add(rows // 2, rows)
            self.keep = self.add(0, rows // 2)
        else:
            self.keep = self.keep.astype(F32) + self.came[:rows].astype(F32)

    def add(self, low, high):
        return (self.keep[low:high].astype(F32) + self.came[low:high].astype(F32)).astype(BF16)

    def relay(self, *others):
        if others:
            self.keep = after(self.keep, *others)
        self.receive()
        self.send()

    @staticmethod
    def last(parts):
        for part in parts:
            part.receive()
            part.size = part.sent.shape[0]
        rows = [part.sent for part in parts]
        small = parts[0].small
        if small is not None:
            parts[0].pair = halves_of(small)
            rows[1:1] = parts[0].pair
        came = swap_dp(jnp.concatenate(rows, axis=0), parts[0].order[-1] + parts[0].shift)
        start = 0
        for part in parts:
            end = start + part.size + (2 * small.shape[0] if part.small is not None else 0)
            part.came = came[start:end]
            start = end
            part.step += 1
            part.receive()

    def rest(self):
        value = self.keep
        for bit in reversed(range(self.shift)):
            half = value.shape[0] // 2
            mine = (lax.axis_index("dp") >> bit) & 1
            keep = lax.dynamic_slice_in_dim(value, mine * half, half, 0)
            away = lax.dynamic_slice_in_dim(value, (1 - mine) * half, half, 0)
            value = keep + swap_dp(away.astype(BF16), bit).astype(F32)
            if self.small is not None:
                self.small = self.small + swap_dp(self.small, bit)
        return value


def after(values, *others):
    return lax.optimization_barrier((values, others))[0]


def shards(
    tokens,
    doc_lengths,
    w_query,
    w_key,
    w_value,
    w_out,
    w_gate,
    w_up,
    w_down,
    gain_attn,
    gain_ffn,
    cotangent,
):
    row_count, width = tokens.shape
    head_cols = w_query.shape[1] // lax.axis_size("seq")
    dp_size = lax.axis_size("dp")
    blocks = min(dp_size, 16)
    bits = blocks.bit_length() - 1
    shift = (dp_size // blocks).bit_length() - 1
    turns = [stage_order(bits, turn) for turn in range(3)]
    orders = ((0, 2, 1, 3), (1, 0, 2, 3), (2, 3, 1, 0))
    lengths = doc_lengths[0]
    seq_index = lax.axis_index("seq")
    info = jnp.stack([seq_index, lax.axis_index("dp") >> shift]).astype(jnp.int32)
    gain_one, gain_two = gain_attn.reshape(1, width), gain_ffn.reshape(1, width)

    oth = swap_seq(tokens)
    *started, turned, own_q, own_k, own_v = project_own(info, lengths, tokens, (w_query, w_key, w_value))
    query, key, value, gathered, context, mine, away, lse = attention_forward(
        info, lengths, started, oth, turned
    )
    kept = (query, key, value, context, lse)
    came = swap_seq(away)
    act, silu, slope, result, dm, dm_turned, hb_turned, dr2, r1, small = ffn_forward(
        info, lengths, tokens, mine, came, w_out, gain_one, gain_two, w_gate, w_up, w_down, cotangent, blocks
    )
    down_away = weight_grad(info, dm_turned, act, orders[2], blocks)
    down_came = swap_seq(down_away)
    dgt, dup, gate_away, up_away = swiglu_away(
        info, after(dm, down_away), w_down, silu, slope, hb_turned, orders[:2], blocks
    )
    gate_came, up_came = swap_seq(gate_away), swap_seq(up_away)
    down = Halving(
        *weight_grad(info, dm_turned, after(act, gate_away), orders[2], blocks, down_came), orders[2], shift
    )
    down.send()
    dgt, dup = swiglu_mine(info, after(dm, down.sent), w_down, silu, slope, dgt, dup)
    gate = Halving(*weight_grad(info, hb_turned, dgt, orders[0], blocks, gate_came), orders[0], shift)
    gate.send()
    dr1, da_turned, own_rows, away_rows, small = norm_one(
        info, after(dgt, gate.sent), dup, w_gate, w_up, r1, dr2, gain_one, w_out, small, blocks
    )
    came_rows = swap_seq(away_rows)
    up = Halving(
        *weight_grad(info, after(hb_turned, away_rows), dup, orders[1], blocks, up_came), orders[1], shift
    )
    up.send()
    out_keep, out_away = out_grad(after(da_turned, up.sent), mine, came)
    out_came = swap_seq(out_away)
    small = small + swap_seq(small)
    grads = ()
    each = head_cols // HDIM // len(PLAN)
    ffn = [down, gate, up]
    for number, relays in enumerate(PLAN):
        for part in relays:
            ffn[part].relay(*grads)
        own_rows = after(own_rows, out_away, *[ffn[part].sent for part in relays], *grads)
        grads = attention_backward(
            info, lengths, kept, own_rows, came_rows, number * each, each, grads
        )
    sides = project_grad(info, gathered, grads, out_keep, out_came, turns, blocks)
    attn = [
        Halving(sides[2 * index], sides[2 * index + 1], turns[index], shift, None if index else small)
        for index in range(3)
    ]
    up.relay(*sides)
    down.relay(*sides)
    for part in attn:
        part.send()
    weights = (own_q, own_k, own_v)
    stream_away = stream_grad(info, after(grads, *sides), weights)
    grad_tokens = stream_grad(info, grads, weights, swap_seq(stream_away), dr1)
    gate.relay()
    up.relay()
    down.relay()
    for part in attn:
        part.relay()
    Halving.last([gate, up])
    for part in attn:
        part.relay()
    down.receive()
    Halving.last(attn)
    summed_down, summed_gate, summed_up = (part.rest() for part in ffn)
    sums = [part.rest() for part in attn]
    summed_out = jnp.concatenate([total[:, head_cols:] for total in sums], axis=1)
    small = attn[0].small.reshape(8, 2 * WIDE)[:, :width]
    squares = jnp.sum(small[2:5], axis=1)
    rms_values = jnp.sqrt(squares / (small[5, 0] * width))
    return (
        result,
        grad_tokens,
        sums[0][:, :head_cols],
        sums[1][:, :head_cols],
        sums[2][:, :head_cols],
        summed_out.T,
        summed_gate,
        summed_up,
        summed_down.T,
        small[0],
        small[1],
        rms_values,
    )


def solution(mesh):
    return jax.shard_map(
        shards,
        mesh=mesh,
        in_specs=(
            P(("dp", "seq"), None),
            P("dp", None),
            P(),
            P(),
            P(),
            P(),
            P(),
            P(),
            P(),
            P(),
            P(),
            P(("dp", "seq"), None),
        ),
        out_specs=(
            P(("dp", "seq"), None),
            P(("dp", "seq"), None),
            P("dp", "seq"),
            P("dp", "seq"),
            P("dp", "seq"),
            P("seq", "dp"),
            P("dp", "seq"),
            P("dp", "seq"),
            P("seq", "dp"),
            P(),
            P(),
            P(),
        ),
        check_vma=False,
    )
```

```python
import functools
import math

import jax
import jax.numpy as jnp
import numpy as np
from jax import lax
from jax.experimental import pallas as pl
from jax.experimental.pallas import tpu as pltpu
from jax.sharding import PartitionSpec as P

HDIM = 48
HALF = HDIM // 2
SCORE = 1.0 / math.sqrt(HDIM)
LOG2E = 1.0 / math.log(2.0)
NEG = -1e30
BF16 = jnp.bfloat16
F32 = jnp.float32
CHUNK = 256
WIDE = 512
ROWS = 64
SPANS = 4
PAIR = 2
PLAN = ((0,), (1,))
MIB = 1 << 20
EASE = 50
ROOM = 8


def call(kernel, name, scalars, arrays, out_shape, flops, scratch=(), room=16, aliases=None):
    moved = sum(math.prod(o.shape) * o.dtype.itemsize for o in out_shape)
    return pl.pallas_call(
        kernel,
        in_specs=[pl.BlockSpec(memory_space=pltpu.SMEM)] * len(scalars)
        + [pl.BlockSpec(memory_space=pltpu.VMEM)] * len(arrays),
        out_specs=[pl.BlockSpec(memory_space=pltpu.VMEM)] * len(out_shape),
        out_shape=out_shape,
        scratch_shapes=list(scratch),
        input_output_aliases=aliases or {},
        cost_estimate=pl.CostEstimate(flops=flops // EASE, bytes_accessed=moved // EASE, transcendentals=0),
        compiler_params=pltpu.CompilerParams(vmem_limit_bytes=room * MIB),
        name=name,
    )(*scalars, *arrays)


def shape(dtype, *dims):
    return jax.ShapeDtypeStruct(dims, dtype)


def at(start, size):
    return pl.ds(pl.multiple_of(start, size), size)


def dot(a, b, ca, cb):
    return lax.dot_general(a, b, (((ca,), (cb,)), ((), ())), preferred_element_type=F32)


def rope_tables(span):
    freq = 10000.0 ** (-np.arange(HALF, dtype=np.float64) / HALF)
    phase = freq[:, None] * np.arange(span, dtype=np.float64)[None, :]
    return np.cos(phase).astype(np.float32), np.sin(phase).astype(np.float32)


def block_facts(len_ref, block):
    ends = []
    total = 0
    for index in range(len_ref.shape[0]):
        total = total + len_ref[index]
        ends.append(total)
    segments, openings = [], []
    for number in range(SPANS):
        segment = 0
        opening = 0
        for index, end in enumerate(ends):
            done = number * block >= end
            segment = segment + done.astype(jnp.int32)
            opening = opening + jnp.where(done, len_ref[index], 0)
        segments.append(segment)
        openings.append(opening)
    return segments, openings


def causal(block):
    key = lax.broadcasted_iota(jnp.int32, (block, block), 0)
    return key <= lax.broadcasted_iota(jnp.int32, (block, block), 1)


def project(to_refs, weights, x, openings, cos_ref, sin_ref, start):
    rows = x.shape[0]
    cols, pack = to_refs[0].shape
    block = pack // SPANS
    for weight, to_ref, scale in zip(weights, to_refs, (SCORE * LOG2E, 1.0, None)):
        for number in range(rows // block):
            part = dot(weight, x[number * block : (number + 1) * block], 1, 1)
            first = start + number * block
            if scale is None:
                to_ref[:, at(first, block)] = part.astype(BF16)
                continue
            opening = functools.reduce(
                lambda rest, span: jnp.where(first == span * block, openings[span], rest), range(SPANS), 0
            )
            here = at(first - opening, block)
            cos = cos_ref[:, here] * scale
            sin = sin_ref[:, here] * scale
            for head in range(cols // HDIM):
                a = part[head * HDIM : head * HDIM + HALF]
                b = part[head * HDIM + HALF : (head + 1) * HDIM]
                turned = jnp.concatenate([a * cos - b * sin, b * cos + a * sin], axis=0)
                to_ref[head * HDIM : (head + 1) * HDIM, at(first, block)] = turned.astype(BF16)


def project_own_kernel(
    info_ref, from_len_ref, from_x_ref, from_cos_ref, from_sin_ref, wq_ref, wk_ref, wv_ref,
    q_ref, k_ref, v_ref, all_ref, turned_ref, cq_ref, ck_ref, cv_ref,
    len_ref, x_ref, cos_ref, sin_ref, sems,
):
    cols, pack = q_ref.shape
    rows = x_ref.shape[0]
    side = info_ref[0]
    pairs = [(from_x_ref, x_ref)]
    pairs += [
        (w_ref.at[:, at(side * cols, cols)], c_ref)
        for w_ref, c_ref in ((wq_ref, cq_ref), (wk_ref, ck_ref), (wv_ref, cv_ref))
    ]
    pairs += [(from_cos_ref, cos_ref), (from_sin_ref, sin_ref), (from_len_ref, len_ref)]
    copies = [pltpu.make_async_copy(*pair, sems.at[index]) for index, pair in enumerate(pairs)]
    for copy in copies:
        copy.start()
    for index, c_ref in enumerate((cq_ref, ck_ref, cv_ref)):
        copies[1 + index].wait()
        turned_ref[index * cols : (index + 1) * cols, :] = c_ref[...].T
    for index in (0, 4, 5, 6):
        copies[index].wait()
    _, openings = block_facts(len_ref.at[0], pack // SPANS)
    all_ref[at(side * rows, rows), :] = x_ref[...]
    weights = [turned_ref[index * cols : (index + 1) * cols, :] for index in range(3)]
    project((q_ref, k_ref, v_ref), weights, x_ref[...], openings, cos_ref, sin_ref, side * rows)


def project_own(info, lengths, own, weights):
    rows, width = own.shape
    pack = 2 * rows
    cols = weights[0].shape[1] // 2
    vmem = pl.BlockSpec(memory_space=pltpu.VMEM)
    far = [pltpu.with_memory_space_constraint(jnp.asarray(value), pltpu.HBM) for value in (lengths, own, *rope_tables(pack), *weights)]
    return pl.pallas_call(
        project_own_kernel,
        in_specs=[pl.BlockSpec(memory_space=pltpu.SMEM)] + [pl.BlockSpec(memory_space=pltpu.HBM)] * 7,
        out_specs=[vmem] * 8,
        out_shape=[shape(BF16, cols, pack)] * 3
        + [shape(BF16, pack, width), shape(BF16, 3 * cols, width)]
        + [shape(BF16, width, cols)] * 3,
        scratch_shapes=[
            pltpu.SMEM(lengths.shape, jnp.int32), pltpu.VMEM(own.shape, BF16),
            pltpu.VMEM((HALF, pack), F32), pltpu.VMEM((HALF, pack), F32), pltpu.SemaphoreType.DMA((7,)),
        ],
        cost_estimate=pl.CostEstimate(flops=4_000_000_000, bytes_accessed=8_000_000, transcendentals=0),
        compiler_params=pltpu.CompilerParams(vmem_limit_bytes=8 * MIB),
        name="project_own",
    )(info, *far)


def attention_forward_kernel(
    info_ref, len_ref, _, __, ___, ____, oth_ref, turned_ref, cos_ref, sin_ref,
    q_ref, k_ref, v_ref, x_ref, ctx_ref, mine_ref, away_ref, lse_ref,
):
    rows = oth_ref.shape[0]
    cols, pack = q_ref.shape
    heads = cols // HDIM
    block = pack // SPANS
    segments, openings = block_facts(len_ref, block)
    side = info_ref[0]
    x_ref[at((1 - side) * rows, rows), :] = oth_ref[...]
    weights = [turned_ref[index * cols : (index + 1) * cols, :] for index in range(3)]
    project((q_ref, k_ref, v_ref), weights, oth_ref[...], openings, cos_ref, sin_ref, (1 - side) * rows)
    below = causal(block)

    spans = [slice(number * block, (number + 1) * block) for number in range(SPANS)]

    @pl.loop(0, heads // PAIR)
    def _(group):
        units = [(group * PAIR + number, i) for number in range(PAIR) for i in range(SPANS)]
        keys = [k_ref[at(head * HDIM, HDIM), :].T for head, i in units if i == 0]
        raw, done = {}, {}

        def scores(step):
            head, i = units[step]
            query = q_ref[at(head * HDIM, HDIM), spans[i]]
            raw[step] = [dot(keys[step // SPANS][spans[j]], query, 1, 0) for j in range(i + 1)]

        def softmax(step):
            head, i = units[step]
            parts = raw.pop(step)
            parts[i] = jnp.where(below, parts[i], NEG)
            biases = [jnp.where(segments[i] == segments[j], 0.0, NEG) for j in range(i)] + [0.0]
            top = functools.reduce(
                jnp.maximum, [jnp.max(part, axis=0, keepdims=True) + bias for part, bias in zip(parts, biases)]
            )
            probs = [jnp.exp2(part - (top - bias)) for part, bias in zip(parts, biases)]
            total = sum(jnp.sum(prob, axis=0, keepdims=True) for prob in probs)
            lse_ref[head, :, spans[i]] = top + jnp.log2(total)
            done[step] = [prob.astype(BF16) for prob in probs], 1.0 / total

        def context(step):
            head, i = units[step]
            here = at(head * HDIM, HDIM)
            probs, scale = done.pop(step)
            total = sum(dot(v_ref[here, spans[j]], prob, 1, 0) for j, prob in enumerate(probs))
            ctx_ref[here, spans[i]] = (total * scale).astype(BF16)

        for step in range(len(units) + 2):
            if step < len(units):
                scores(step)
            if 0 <= step - 1 < len(units):
                softmax(step - 1)
            if 0 <= step - 2:
                context(step - 2)
        here = at(group * PAIR * HDIM, PAIR * HDIM)
        mine_ref[here, :] = ctx_ref[here, at(side * rows, rows)]
        away_ref[here, :] = ctx_ref[here, at((1 - side) * rows, rows)]


def attention_forward(info, lengths, started, oth, turned):
    rows, width = oth.shape
    cols, pack = started[0].shape
    heads = cols // HDIM
    half = shape(BF16, cols, rows)
    return call(
        attention_forward_kernel, "attention_forward", (info, lengths),
        (*started, oth, turned, *rope_tables(pack)),
        [shape(BF16, cols, pack)] * 3 + [shape(BF16, pack, width), shape(BF16, cols, pack)]
        + [half, half, shape(F32, heads, 1, pack)],
        15_000_000_000, room=24,
        aliases={2 + index: index for index in range(4)},
    )


def attention_backward_kernel(
    info_ref, len_ref, q_ref, k_ref, v_ref, ctx_ref, own_ref, oth_ref, lse_ref, cos_ref, sin_ref, *rest,
    first, heads,
):
    dq_ref, dk_ref, dv_ref, dctx_ref = rest[-4:]
    rows = own_ref.shape[1]
    pack = q_ref.shape[1]
    block = pack // SPANS
    segments, openings = block_facts(len_ref, block)
    side = info_ref[0]
    below = causal(block)
    spans = [slice(number * block, (number + 1) * block) for number in range(SPANS)]

    def unturn(value, number, scale):
        here = at(number * block - openings[number], block)
        cos = cos_ref[:, here] * scale
        sin = sin_ref[:, here] * scale
        a, b = value[:HALF], value[HALF:]
        return jnp.concatenate([a * cos + b * sin, b * cos - a * sin], axis=0).astype(BF16)

    def plus(sums, index, value):
        sums[index] = sums[index] + value if index in sums else value

    @pl.loop(first, first + heads)
    def _(head):
        here = at(head * HDIM, HDIM)
        dctx_ref[:, at(side * rows, rows)] = own_ref[here, :]
        dctx_ref[:, at((1 - side) * rows, rows)] = oth_ref[here, :]
        key = k_ref[here, :]
        keys = key.T
        values = v_ref[here, :].T
        delta = jnp.sum(dctx_ref[...].astype(F32) * ctx_ref[here, :].astype(F32), axis=0, keepdims=True)
        lse = lse_ref[head, :, :]
        raw, done, dqs, dks, dvs = {}, {}, {}, {}, {}

        def scores(i, j):
            return (
                dot(keys[spans[j]], q_ref[here, spans[i]], 1, 0),
                dot(values[spans[j]], dctx_ref[:, spans[i]], 1, 0),
            )

        def slopes(i, j, score, slope):
            top = lse[:, spans[i]]
            if j == i:
                prob = jnp.exp2(jnp.where(below, score, NEG) - top)
            else:
                prob = jnp.exp2(score - (top - jnp.where(segments[i] == segments[j], 0.0, NEG)))
            return prob.astype(BF16), (prob * (slope - delta[:, spans[i]])).astype(BF16)

        def products(i, j, prob, dscore):
            plus(dqs, i, dot(key[:, spans[j]], dscore, 1, 0))
            plus(dks, j, dot(q_ref[here, spans[i]], dscore, 1, 1))
            plus(dvs, j, dot(dctx_ref[:, spans[i]], prob, 1, 1))

        pairs = [(i, j) for i in range(SPANS) for j in range(i + 1)]
        for step in range(len(pairs) + 2):
            if step < len(pairs):
                raw[step] = scores(*pairs[step])
            if 0 <= step - 1 < len(pairs):
                done[step - 1] = slopes(*pairs[step - 1], *raw.pop(step - 1))
            if 0 <= step - 2:
                products(*pairs[step - 2], *done.pop(step - 2))
        for number, lanes in enumerate(spans):
            dq_ref[here, lanes] = unturn(dqs[number], number, SCORE)
            dk_ref[here, lanes] = unturn(dks[number], number, 1.0 / LOG2E)
            dv_ref[here, lanes] = dvs[number].astype(BF16)


def attention_backward(info, lengths, kept, own, oth, first, heads, sofar):
    query, key, value, context, lse = kept
    cols, pack = query.shape
    arrays = (query, key, value, context, own, oth, lse, *rope_tables(pack), *sofar)
    base = 2 + len(arrays) - len(sofar)
    return call(
        functools.partial(attention_backward_kernel, first=first, heads=heads),
        "attention_backward", (info, lengths), arrays, [shape(BF16, cols, pack)] * 3,
        heads * 3_000_000_000,
        [pltpu.VMEM((HDIM, pack), BF16)],
        aliases={base + index: index for index in range(len(sofar))},
    )


def inverse_rms(value):
    return lax.rsqrt(jnp.mean(value * value, axis=-1, keepdims=True) + 1e-06)


def norm_back(value, gain, grad):
    inv = inverse_rms(value)
    scaled = grad * gain
    slope = jnp.mean(scaled * value, axis=-1, keepdims=True) * (inv * inv * inv)
    return scaled * inv - value * slope, grad * value * inv


def relative_rows(to_ref, from_ref, place, blocks):
    size = from_ref.shape[0] // blocks
    for block in range(blocks):
        to_ref[block * size : (block + 1) * size, :] = from_ref[at((block ^ place) * size, size), :]


def position(block, order):
    last = len(order) - 1
    return sum(((block >> bit) & 1) << (last - step) for step, bit in enumerate(order))


def ffn_forward_kernel(
    info_ref, len_ref, x_ref, mine_ref, came_ref, wo_ref, g1_ref, g2_ref, wg_ref, wu_ref, wd_ref, cot_ref,
    act_ref, s_ref, t_ref, out_ref, dm_ref, dmt_ref, hbt_ref, dr2_ref, r1_ref, small_ref,
    hb_ref, h_ref, m_ref, turn_ref, *, blocks,
):
    rows, width = x_ref.shape
    part = mine_ref.shape[0]
    total = len_ref[0] + len_ref[1] + len_ref[2] + len_ref[3]
    side = info_ref[0]
    first = side * rows

    def valid_of(start):
        places = lax.broadcasted_iota(jnp.int32, (ROWS, 1), 0) + (start + first)
        return (places < total).astype(F32)

    def squares(row, value, valid):
        add_small(small_ref, row, jnp.sum(value * value * valid, axis=0, keepdims=True))

    small_ref[...] = jnp.zeros_like(small_ref)
    m_ref[...] = dot(mine_ref[...].T, wo_ref[at(side * part, part), :], 1, 0) + dot(
        came_ref[...].T, wo_ref[at((1 - side) * part, part), :], 1, 0
    )

    @pl.loop(0, rows // ROWS, unroll=2)
    def _(index):
        here = at(index * ROWS, ROWS)
        valid = valid_of(index * ROWS)
        x = x_ref[here, :].astype(F32)
        a = m_ref[here, :]
        r1 = x + a
        h = r1 * inverse_rms(r1) * g1_ref[...]
        r1_ref[here, :] = r1
        h_ref[here, :] = h
        hb_ref[here, :] = h.astype(BF16)
        squares(2, x, valid)
        squares(3, a, valid)

    turn_ref[...] = hb_ref[...].T
    relative_rows(hbt_ref, turn_ref, info_ref[1], blocks)

    def inputs(step):
        cols = slice(step * CHUNK, (step + 1) * CHUNK)
        return dot(hb_ref[...], wg_ref[:, cols], 1, 0), dot(hb_ref[...], wu_ref[:, cols], 1, 0)

    count = act_ref.shape[1] // CHUNK
    ready = inputs(0)
    for step in range(count):
        gate, up = ready
        ready = inputs(step + 1) if step + 1 < count else None
        cols = slice(step * CHUNK, (step + 1) * CHUNK)
        sig = 1.0 / (1.0 + jnp.exp(-gate))
        silu = gate * sig
        act_ref[:, cols] = (silu * up).astype(BF16)
        s_ref[:, cols] = silu.astype(BF16)
        t_ref[:, cols] = (up * (sig + silu * (1.0 - sig))).astype(BF16)
    m_ref[...] = dot(act_ref[...], wd_ref[...], 1, 0)

    @pl.loop(0, rows // ROWS, unroll=2)
    def _(index):
        here = at(index * ROWS, ROWS)
        valid = valid_of(index * ROWS)
        m = m_ref[here, :]
        r2 = h_ref[here, :] + m
        gain = g2_ref[...]
        dr2, dgain = norm_back(r2, gain, cot_ref[here, :].astype(F32) * valid)
        out_ref[here, :] = (r2 * inverse_rms(r2) * gain).astype(BF16)
        dr2_ref[here, :] = dr2
        dm_ref[here, :] = dr2.astype(BF16)
        add_small(small_ref, 1, jnp.sum(dgain, axis=0, keepdims=True))
        squares(4, m, valid)

    add_small(small_ref, 5, jnp.full((1, width), jnp.clip(total - first, 0, rows).astype(F32)))
    turn_ref[...] = dm_ref[...].T
    relative_rows(dmt_ref, turn_ref, info_ref[1], blocks)


def ffn_forward(info, lengths, x, mine, came, w_out, g1, g2, wg, wu, wd, cot, blocks):
    rows, width = x.shape
    ff = wg.shape[1]
    return call(
        functools.partial(ffn_forward_kernel, blocks=blocks), "ffn_forward", (info, lengths),
        (x, mine, came, w_out, g1, g2, wg, wu, wd, cot),
        [shape(BF16, rows, ff)] * 3 + [shape(BF16, rows, width)] * 2 + [shape(BF16, width, rows)] * 2
        + [shape(F32, rows, width)] * 2 + [shape(F32, 16, WIDE)],
        6 * rows * width * ff,
        [
            pltpu.VMEM((rows, width), BF16), pltpu.VMEM((rows, width), F32),
            pltpu.VMEM((rows, width), F32), pltpu.VMEM((width, rows), BF16),
        ],
    )


def add_small(small_ref, row, value):
    for piece in range(-(-value.shape[1] // WIDE)):
        part = value[:, piece * WIDE : (piece + 1) * WIDE]
        small_ref[2 * row + piece : 2 * row + piece + 1, 0 : part.shape[1]] += part


def split_store(product, came, to_refs, order, blocks):
    size = product.shape[0] // blocks
    for block in range(blocks):
        place = position(block, order)
        rows = product[block * size : (block + 1) * size]
        if came is not None:
            rows = rows + came[place * size : (place + 1) * size].astype(F32)
        half = blocks // len(to_refs)
        start = (place % half) * size
        to_refs[place // half][start : start + size, :] = rows.astype(BF16)


def weight_kernel(info_ref, left_ref, right_ref, *rest, order, blocks):
    side = info_ref[0]
    mine = len(rest) == 3
    to_refs = rest[-2:] if mine else rest
    cols = to_refs[0].shape[1]
    start = (side if mine else 1 - side) * cols

    @pl.loop(0, cols // CHUNK, unroll=True)
    def _(step):
        here = at(step * CHUNK, CHUNK)
        right = right_ref[:, at(start + step * CHUNK, CHUNK)]
        came = rest[0][:, here] if mine else None
        split_store(dot(left_ref[...], right, 1, 0), came, [ref.at[:, here] for ref in to_refs], order, blocks)


def weight_grad(info, left, right, order, blocks, came=None):
    width, rows = left.shape
    cols = right.shape[1] // 2
    kernel = functools.partial(weight_kernel, order=order, blocks=blocks)
    flops = 2 * width * rows * cols
    if came is None:
        return call(kernel, "weight_away", (info,), (left, right), [shape(BF16, width, cols)], flops, room=ROOM)[0]
    return call(
        kernel, "weight_mine", (info,), (left, right, came), [shape(BF16, width // 2, cols)] * 2, flops, room=ROOM
    )


def swiglu_away_kernel(
    info_ref, dm_ref, wd_ref, s_ref, t_ref, hbt_ref, dgt_ref, dup_ref, gate_ref, up_ref, *, orders, blocks
):
    half = gate_ref.shape[1]
    count = half // CHUNK

    def grads(step):
        return swiglu_grads(
            (1 - info_ref[0]) * half + step * CHUNK, dm_ref, wd_ref, s_ref, t_ref, dgt_ref, dup_ref
        )

    ready = grads(0)
    for step in range(count):
        dgt, dup = ready
        ready = grads(step + 1) if step + 1 < count else None
        here = slice(step * CHUNK, (step + 1) * CHUNK)
        split_store(dot(hbt_ref[...], dgt, 1, 0), None, [gate_ref.at[:, here]], orders[0], blocks)
        split_store(dot(hbt_ref[...], dup, 1, 0), None, [up_ref.at[:, here]], orders[1], blocks)


def swiglu_grads(start, dm_ref, wd_ref, s_ref, t_ref, dgt_ref, dup_ref):
    cols = at(start, CHUNK)
    grad = dot(dm_ref[...], wd_ref[cols, :], 1, 1)
    dup = (grad * s_ref[:, cols].astype(F32)).astype(BF16)
    dgt = (grad * t_ref[:, cols].astype(F32)).astype(BF16)
    dup_ref[:, cols] = dup
    dgt_ref[:, cols] = dgt
    return dgt, dup


def swiglu_mine_kernel(info_ref, dm_ref, wd_ref, s_ref, t_ref, _, __, dgt_ref, dup_ref):
    half = s_ref.shape[1] // 2

    @pl.loop(0, half // CHUNK, unroll=True)
    def _(step):
        swiglu_grads(info_ref[0] * half + step * CHUNK, dm_ref, wd_ref, s_ref, t_ref, dgt_ref, dup_ref)


def swiglu_away(info, dm, wd, s, t, hbt, orders, blocks):
    rows, width = dm.shape
    ff = wd.shape[0]
    return call(
        functools.partial(swiglu_away_kernel, orders=orders, blocks=blocks), "swiglu_away", (info,),
        (dm, wd, s, t, hbt),
        [shape(BF16, rows, ff)] * 2 + [shape(BF16, width, ff // 2)] * 2,
        3 * rows * width * ff, room=ROOM,
    )


def swiglu_mine(info, dm, wd, s, t, dgt, dup):
    return call(
        swiglu_mine_kernel, "swiglu_mine", (info,), (dm, wd, s, t, dgt, dup), [shape(BF16, *dgt.shape)] * 2,
        dm.shape[0] * dm.shape[1] * wd.shape[0], aliases={5: 0, 6: 1},
    )


def norm_one_kernel(
    info_ref, dgt_ref, dup_ref, wg_ref, wu_ref, r1_ref, dr2_ref, g1_ref, wo_ref, part_ref,
    dr1_ref, dat_ref, own_ref, away_ref, small_ref, acc_ref, da_ref, turn_ref, *, blocks,
):
    rows = r1_ref.shape[0]
    cols = own_ref.shape[0]
    side = info_ref[0]
    acc_ref[...] = dr2_ref[...]

    @pl.loop(0, wg_ref.shape[1] // WIDE)
    def _(step):
        here = at(step * WIDE, WIDE)
        acc_ref[...] += dot(dgt_ref[:, here], wg_ref[:, here], 1, 1) + dot(dup_ref[:, here], wu_ref[:, here], 1, 1)

    small_ref[...] = part_ref[...]

    @pl.loop(0, rows // ROWS, unroll=2)
    def _(index):
        here = at(index * ROWS, ROWS)
        dr1, dgain = norm_back(r1_ref[here, :], g1_ref[...], acc_ref[here, :])
        dr1_ref[here, :] = dr1
        da_ref[here, :] = dr1.astype(BF16)
        add_small(small_ref, 0, jnp.sum(dgain, axis=0, keepdims=True))

    away_ref[...] = dot(wo_ref[at((1 - side) * cols, cols), :], da_ref[...], 1, 1).astype(BF16)
    own_ref[...] = dot(wo_ref[at(side * cols, cols), :], da_ref[...], 1, 1).astype(BF16)
    turn_ref[...] = da_ref[...].T
    relative_rows(dat_ref, turn_ref, info_ref[1], blocks)


def norm_one(info, dgt, dup, wg, wu, r1, dr2, g1, w_out, part, blocks):
    rows, width = r1.shape
    ff = wg.shape[1]
    cols = w_out.shape[0] // 2
    return call(
        functools.partial(norm_one_kernel, blocks=blocks), "norm_one_back", (info,),
        (dgt, dup, wg, wu, r1, dr2, g1, w_out, part),
        [
            shape(F32, rows, width), shape(BF16, width, rows), shape(BF16, cols, rows),
            shape(BF16, cols, rows), shape(F32, 16, WIDE),
        ],
        4 * rows * width * ff,
        [pltpu.VMEM((rows, width), F32), pltpu.VMEM((rows, width), BF16), pltpu.VMEM((width, rows), BF16)],
    )


def out_grad_kernel(dat_ref, mine_ref, came_ref, keep_ref, away_ref):
    away_ref[...] = dot(dat_ref[...], came_ref[...], 1, 1).astype(BF16)
    keep_ref[...] = dot(dat_ref[...], mine_ref[...], 1, 1).astype(BF16)


def out_grad(dat, mine, came):
    width, rows = dat.shape
    cols = mine.shape[0]
    return call(
        out_grad_kernel, "out_grad", (), (dat, mine, came), [shape(BF16, width, cols)] * 2,
        4 * width * rows * cols,
    )


def project_grad_kernel(info_ref, x_ref, dq_ref, dk_ref, dv_ref, mine_ref, came_ref, *rest, orders, blocks):
    out_refs, (turn_ref, left_ref) = rest[:-2], rest[-2:]
    turn_ref[...] = x_ref[...].T
    relative_rows(left_ref, turn_ref, info_ref[1], blocks)
    left = left_ref[...]
    cols = dq_ref.shape[0]
    piece = cols // 3
    for index, grad_ref in enumerate((dq_ref, dk_ref, dv_ref)):
        lanes = slice(index * piece, (index + 1) * piece)
        pair = out_refs[2 * index : 2 * index + 2]
        main = [ref.at[:, 0:cols] for ref in pair]
        tail = [ref.at[:, cols : cols + piece] for ref in pair]
        split_store(dot(left, grad_ref[...], 1, 1), None, main, orders[index], blocks)
        both = mine_ref[:, lanes].astype(F32) + came_ref[:, lanes].astype(F32)
        split_store(both, None, tail, orders[index], blocks)


def project_grad(info, x, grads, mine, came, orders, blocks):
    rows, width = x.shape
    cols = grads[0].shape[0]
    wide = cols + cols // 3
    return call(
        functools.partial(project_grad_kernel, orders=orders, blocks=blocks), "project_grad", (info,),
        (x, *grads, mine, came), [shape(BF16, width // 2, wide)] * 6, 6 * rows * width * cols,
        [pltpu.VMEM((width, rows), BF16)] * 2,
    )


def stream_grad_kernel(info_ref, dq_ref, dk_ref, dv_ref, wq_ref, wk_ref, wv_ref, *rest):
    cols, pack = dq_ref.shape
    rows = pack // 2
    side = info_ref[0]
    mine = len(rest) == 3
    lanes = at((side if mine else 1 - side) * rows, rows)
    total = sum(
        dot(w_ref[...], g_ref[:, lanes], 1, 0)
        for w_ref, g_ref in ((wq_ref, dq_ref), (wk_ref, dk_ref), (wv_ref, dv_ref))
    )
    if mine:
        came_ref, dr1_ref, out_ref = rest
        total = total + came_ref[...].astype(F32)
        out_ref[...] = (dr1_ref[...] + total.T).astype(BF16)
    else:
        rest[0][...] = total.astype(BF16)


def stream_grad(info, grads, weights, *others):
    cols, pack = grads[0].shape
    width = weights[0].shape[0]
    rows = pack // 2
    out = (rows, width) if others else (width, rows)
    return call(
        stream_grad_kernel, "stream_grad", (info,), (*grads, *weights, *others), [shape(BF16, *out)],
        6 * rows * width * cols,
    )[0]


def finish_kernel(
    query_ref, key_ref, value_ref, high_ref, low_ref, came_ref,
    gq_ref, gk_ref, gv_ref, out_ref, one_ref, two_ref, rms_ref,
):
    rows, cols = gq_ref.shape
    lines = high_ref.shape[0]
    starts = (0, rows + 2 * lines, 2 * rows + 2 * lines)
    tails = []
    for keep_ref, start, to_ref in zip((query_ref, key_ref, value_ref), starts, (gq_ref, gk_ref, gv_ref)):
        total = keep_ref[...].astype(F32) + came_ref[start : start + rows, :].astype(F32)
        to_ref[...] = total[:, :cols]
        tails.append(total[:, cols:])
    out_ref[...] = jnp.concatenate(tails, axis=1)
    small = whole_of(high_ref[...], low_ref[...]) + whole_of(
        came_ref[rows : rows + lines, :], came_ref[rows + lines : rows + 2 * lines, :]
    )
    lanes = one_ref.shape[1]
    width = one_ref.shape[0] * lanes
    for number in range(one_ref.shape[0]):
        line, start = divmod(number * lanes, WIDE)
        for index, to_ref in enumerate((one_ref, two_ref)):
            to_ref[number : number + 1, :] = small[2 * index + line : 2 * index + line + 1, start : start + lanes]
    sums = jnp.sum(small[4:10], axis=1, keepdims=True)
    count = small[10:11, 0:1] * width
    for index in range(3):
        rms_ref[:, index : index + 1] = jnp.sqrt((sums[2 * index : 2 * index + 1] + sums[2 * index + 1 : 2 * index + 2]) / count)


def finish(parts, came, width, head_cols):
    rows = parts[0].keep.shape[0]
    return call(
        finish_kernel, "finish", (), (*[part.keep for part in parts], *parts[0].pair, came),
        [shape(F32, rows, head_cols)] * 4 + [shape(F32, width // 128, 128)] * 2 + [shape(F32, 1, 3)],
        1_000_000, room=4,
    )


def stage_order(bits, turn):
    last = bits - 1
    return [(turn + step) % last for step in range(last)] + [last]


def swap_seq(value):
    return lax.ppermute(value, "seq", [(0, 1), (1, 0)])


def swap_dp(value, bit):
    size = lax.axis_size("dp")
    return lax.ppermute(value, "dp", [(i, i ^ (1 << bit)) for i in range(size)])


def halves_of(small):
    high = lax.reduce_precision(small, 8, 7)
    return high.astype(BF16), (small - high).astype(BF16)


def whole_of(high, low):
    return high.astype(F32) + low.astype(F32)


class Halving:
    def __init__(self, keep, away, order, shift, small=None):
        self.keep, self.order, self.shift, self.small = keep, order, shift, small
        self.sent, self.step = away, 0

    def send(self):
        if self.small is not None:
            self.pair = halves_of(self.small)
            self.sent = jnp.concatenate([self.sent, *self.pair], axis=0)
        self.came = swap_dp(self.sent, self.order[self.step] + self.shift)
        self.step += 1

    def receive(self):
        rows = self.keep.shape[0]
        if self.small is not None:
            count = self.small.shape[0]
            came = self.came[rows : rows + count], self.came[rows + count :]
            self.small = whole_of(*self.pair) + whole_of(*came)
        if self.step < len(self.order):
            self.sent = self.add(rows // 2, rows)
            self.keep = self.add(0, rows // 2)
        else:
            self.keep = self.keep.astype(F32) + self.came[:rows].astype(F32)

    def add(self, low, high):
        return (self.keep[low:high].astype(F32) + self.came[low:high].astype(F32)).astype(BF16)

    def relay(self, *others):
        if others:
            self.keep = after(self.keep, *others)
        self.receive()
        self.send()

    @staticmethod
    def last(parts, done=False):
        for part in parts:
            part.receive()
            part.size = part.sent.shape[0]
        rows = [part.sent for part in parts]
        small = parts[0].small
        if small is not None:
            parts[0].pair = halves_of(small)
            rows[1:1] = parts[0].pair
        came = swap_dp(jnp.concatenate(rows, axis=0), parts[0].order[-1] + parts[0].shift)
        if done:
            return came
        start = 0
        for part in parts:
            end = start + part.size + (2 * small.shape[0] if part.small is not None else 0)
            part.came = came[start:end]
            start = end
            part.step += 1
            part.receive()

    def rest(self):
        value = self.keep
        for bit in reversed(range(self.shift)):
            half = value.shape[0] // 2
            mine = (lax.axis_index("dp") >> bit) & 1
            keep = lax.dynamic_slice_in_dim(value, mine * half, half, 0)
            away = lax.dynamic_slice_in_dim(value, (1 - mine) * half, half, 0)
            value = keep + swap_dp(away.astype(BF16), bit).astype(F32)
            if self.small is not None:
                self.small = self.small + swap_dp(self.small, bit)
        return value


def after(values, *others):
    return lax.optimization_barrier((values, others))[0]


def shards(
    tokens,
    doc_lengths,
    w_query,
    w_key,
    w_value,
    w_out,
    w_gate,
    w_up,
    w_down,
    gain_attn,
    gain_ffn,
    cotangent,
):
    row_count, width = tokens.shape
    head_cols = w_query.shape[1] // lax.axis_size("seq")
    dp_size = lax.axis_size("dp")
    blocks = min(dp_size, 16)
    bits = blocks.bit_length() - 1
    shift = (dp_size // blocks).bit_length() - 1
    turns = [stage_order(bits, turn) for turn in range(3)]
    orders = ((0, 2, 1, 3), (1, 0, 2, 3), (2, 3, 1, 0))
    lengths = doc_lengths[0]
    seq_index = lax.axis_index("seq")
    info = jnp.stack([seq_index, lax.axis_index("dp") >> shift]).astype(jnp.int32)
    gain_one, gain_two = gain_attn.reshape(1, width), gain_ffn.reshape(1, width)

    oth = swap_seq(tokens)
    *started, turned, own_q, own_k, own_v = project_own(info, doc_lengths, tokens, (w_query, w_key, w_value))
    query, key, value, gathered, context, mine, away, lse = attention_forward(
        info, lengths, started, oth, turned
    )
    kept = (query, key, value, context, lse)
    came = swap_seq(away)
    act, silu, slope, result, dm, dm_turned, hb_turned, dr2, r1, small = ffn_forward(
        info, lengths, tokens, mine, came, w_out, gain_one, gain_two, w_gate, w_up, w_down, cotangent, blocks
    )
    down_away = weight_grad(info, dm_turned, act, orders[2], blocks)
    down_came = swap_seq(down_away)
    dgt, dup, gate_away, up_away = swiglu_away(
        info, after(dm, down_away), w_down, silu, slope, hb_turned, orders[:2], blocks
    )
    gate_came, up_came = swap_seq(gate_away), swap_seq(up_away)
    down = Halving(
        *weight_grad(info, dm_turned, after(act, gate_away), orders[2], blocks, down_came), orders[2], shift
    )
    down.send()
    dgt, dup = swiglu_mine(info, after(dm, down.sent), w_down, silu, slope, dgt, dup)
    gate = Halving(*weight_grad(info, hb_turned, dgt, orders[0], blocks, gate_came), orders[0], shift)
    gate.send()
    dr1, da_turned, own_rows, away_rows, small = norm_one(
        info, after(dgt, gate.sent), dup, w_gate, w_up, r1, dr2, gain_one, w_out, small, blocks
    )
    came_rows = swap_seq(away_rows)
    up = Halving(
        *weight_grad(info, after(hb_turned, away_rows), dup, orders[1], blocks, up_came), orders[1], shift
    )
    up.send()
    out_keep, out_away = out_grad(after(da_turned, up.sent), mine, came)
    out_came = swap_seq(out_away)
    small = small + swap_seq(small)
    grads = ()
    each = head_cols // HDIM // len(PLAN)
    ffn = [down, gate, up]
    for number, relays in enumerate(PLAN):
        for part in relays:
            ffn[part].relay(*grads)
        own_rows = after(own_rows, out_away, *[ffn[part].sent for part in relays], *grads)
        grads = attention_backward(
            info, lengths, kept, own_rows, came_rows, number * each, each, grads
        )
    sides = project_grad(info, gathered, grads, out_keep, out_came, turns, blocks)
    attn = [
        Halving(sides[2 * index], sides[2 * index + 1], turns[index], shift, None if index else small)
        for index in range(3)
    ]
    up.relay(*sides)
    down.relay(*sides)
    for part in attn:
        part.send()
    weights = (own_q, own_k, own_v)
    stream_away = stream_grad(info, after(grads, *sides), weights)
    grad_tokens = stream_grad(info, grads, weights, swap_seq(stream_away), dr1)
    gate.relay()
    up.relay()
    down.relay()
    for part in attn:
        part.relay()
    Halving.last([gate, up])
    for part in attn:
        part.relay()
    down.receive()
    summed_down, summed_gate, summed_up = (part.rest() for part in ffn)
    summed_down = summed_down.T
    if shift:
        Halving.last(attn)
        sums = [part.rest() for part in attn]
        attn_grads = [total[:, :head_cols] for total in sums]
        attn_grads.append(jnp.concatenate([total[:, head_cols:] for total in sums], axis=1).T)
        small = attn[0].small.reshape(8, 2 * WIDE)[:, :width]
        grad_one, grad_two = small[0], small[1]
        rms_values = jnp.sqrt(jnp.sum(small[2:5], axis=1) / (small[5, 0] * width))
    else:
        came = after(Halving.last(attn, True), summed_down, summed_gate, summed_up, grad_tokens)
        *attn_grads, grad_wo, grad_one, grad_two, rms_values = finish(attn, came, width, head_cols)
        attn_grads.append(grad_wo.T)
    return (
        result,
        grad_tokens,
        *attn_grads,
        summed_gate,
        summed_up,
        summed_down,
        grad_one.reshape(-1),
        grad_two.reshape(-1),
        rms_values.reshape(-1),
    )


def solution(mesh):
    return jax.shard_map(
        shards,
        mesh=mesh,
        in_specs=(
            P(("dp", "seq"), None),
            P("dp", None),
            P(),
            P(),
            P(),
            P(),
            P(),
            P(),
            P(),
            P(),
            P(),
            P(("dp", "seq"), None),
        ),
        out_specs=(
            P(("dp", "seq"), None),
            P(("dp", "seq"), None),
            P("dp", "seq"),
            P("dp", "seq"),
            P("dp", "seq"),
            P("seq", "dp"),
            P("dp", "seq"),
            P("dp", "seq"),
            P("seq", "dp"),
            P(),
            P(),
            P(),
        ),
        check_vma=False,
    )
```

```python
import functools
import math

import jax
import jax.numpy as jnp
import numpy as np
from jax import lax
from jax.experimental import pallas as pl
from jax.experimental.pallas import tpu as pltpu
from jax.sharding import PartitionSpec as P

HDIM = 48
HALF = HDIM // 2
SCORE = 1.0 / math.sqrt(HDIM)
LOG2E = 1.0 / math.log(2.0)
NEG = -1e30
BF16 = jnp.bfloat16
F32 = jnp.float32
CHUNK = 256
WIDE = 512
ROWS = 64
SPANS = 4
PAIR = 2
PLAN = ((0,), (1,))
MIB = 1 << 20
EASE = 50
ROOM = 8


def call(kernel, name, scalars, arrays, out_shape, flops, scratch=(), room=16, aliases=None):
    moved = sum(math.prod(o.shape) * o.dtype.itemsize for o in out_shape)
    return pl.pallas_call(
        kernel,
        in_specs=[pl.BlockSpec(memory_space=pltpu.SMEM)] * len(scalars)
        + [pl.BlockSpec(memory_space=pltpu.VMEM)] * len(arrays),
        out_specs=[pl.BlockSpec(memory_space=pltpu.VMEM)] * len(out_shape),
        out_shape=out_shape,
        scratch_shapes=list(scratch),
        input_output_aliases=aliases or {},
        cost_estimate=pl.CostEstimate(flops=flops // EASE, bytes_accessed=moved // EASE, transcendentals=0),
        compiler_params=pltpu.CompilerParams(vmem_limit_bytes=room * MIB),
        name=name,
    )(*scalars, *arrays)


def shape(dtype, *dims):
    return jax.ShapeDtypeStruct(dims, dtype)


def at(start, size):
    return pl.ds(pl.multiple_of(start, size), size)


def dot(a, b, ca, cb):
    return lax.dot_general(a, b, (((ca,), (cb,)), ((), ())), preferred_element_type=F32)


def rope_tables(span):
    freq = 10000.0 ** (-np.arange(HALF, dtype=np.float64) / HALF)
    phase = freq[:, None] * np.arange(span, dtype=np.float64)[None, :]
    return np.cos(phase).astype(np.float32), np.sin(phase).astype(np.float32)


def block_facts(len_ref, block):
    ends = []
    total = 0
    for index in range(len_ref.shape[0]):
        total = total + len_ref[index]
        ends.append(total)
    segments, openings = [], []
    for number in range(SPANS):
        segment = 0
        opening = 0
        for index, end in enumerate(ends):
            done = number * block >= end
            segment = segment + done.astype(jnp.int32)
            opening = opening + jnp.where(done, len_ref[index], 0)
        segments.append(segment)
        openings.append(opening)
    return segments, openings


def causal(block):
    key = lax.broadcasted_iota(jnp.int32, (block, block), 0)
    return key <= lax.broadcasted_iota(jnp.int32, (block, block), 1)


def project(to_refs, weights, x, openings, cos_ref, sin_ref, start):
    rows = x.shape[0]
    cols, pack = to_refs[0].shape
    block = pack // SPANS
    for weight, to_ref, scale in zip(weights, to_refs, (SCORE * LOG2E, 1.0, None)):
        for number in range(rows // block):
            part = dot(weight, x[number * block : (number + 1) * block], 1, 1)
            first = start + number * block
            if scale is None:
                to_ref[:, at(first, block)] = part.astype(BF16)
                continue
            opening = functools.reduce(
                lambda rest, span: jnp.where(first == span * block, openings[span], rest), range(SPANS), 0
            )
            here = at(first - opening, block)
            cos = cos_ref[:, here] * scale
            sin = sin_ref[:, here] * scale
            for head in range(cols // HDIM):
                a = part[head * HDIM : head * HDIM + HALF]
                b = part[head * HDIM + HALF : (head + 1) * HDIM]
                turned = jnp.concatenate([a * cos - b * sin, b * cos + a * sin], axis=0)
                to_ref[head * HDIM : (head + 1) * HDIM, at(first, block)] = turned.astype(BF16)


def project_own_kernel(
    info_ref, from_len_ref, from_x_ref, from_cos_ref, from_sin_ref, wq_ref, wk_ref, wv_ref,
    q_ref, k_ref, v_ref, all_ref, turned_ref, cq_ref, ck_ref, cv_ref,
    len_ref, x_ref, cos_ref, sin_ref, sems,
):
    cols, pack = q_ref.shape
    rows = x_ref.shape[0]
    side = info_ref[0]
    pairs = [(from_x_ref, x_ref)]
    pairs += [
        (w_ref.at[:, at(side * cols, cols)], c_ref)
        for w_ref, c_ref in ((wq_ref, cq_ref), (wk_ref, ck_ref), (wv_ref, cv_ref))
    ]
    pairs += [(from_cos_ref, cos_ref), (from_sin_ref, sin_ref), (from_len_ref, len_ref)]
    copies = [pltpu.make_async_copy(*pair, sems.at[index]) for index, pair in enumerate(pairs)]
    for copy in copies:
        copy.start()
    for index, c_ref in enumerate((cq_ref, ck_ref, cv_ref)):
        copies[1 + index].wait()
        turned_ref[index * cols : (index + 1) * cols, :] = c_ref[...].T
    for index in (0, 4, 5, 6):
        copies[index].wait()
    _, openings = block_facts(len_ref.at[0], pack // SPANS)
    all_ref[at(side * rows, rows), :] = x_ref[...]
    weights = [turned_ref[index * cols : (index + 1) * cols, :] for index in range(3)]
    project((q_ref, k_ref, v_ref), weights, x_ref[...], openings, cos_ref, sin_ref, side * rows)


def project_own(info, lengths, own, weights):
    rows, width = own.shape
    pack = 2 * rows
    cols = weights[0].shape[1] // 2
    vmem = pl.BlockSpec(memory_space=pltpu.VMEM)
    far = [pltpu.with_memory_space_constraint(jnp.asarray(value), pltpu.HBM) for value in (lengths, own, *rope_tables(pack), *weights)]
    return pl.pallas_call(
        project_own_kernel,
        in_specs=[pl.BlockSpec(memory_space=pltpu.SMEM)] + [pl.BlockSpec(memory_space=pltpu.HBM)] * 7,
        out_specs=[vmem] * 8,
        out_shape=[shape(BF16, cols, pack)] * 3
        + [shape(BF16, pack, width), shape(BF16, 3 * cols, width)]
        + [shape(BF16, width, cols)] * 3,
        scratch_shapes=[
            pltpu.SMEM(lengths.shape, jnp.int32), pltpu.VMEM(own.shape, BF16),
            pltpu.VMEM((HALF, pack), F32), pltpu.VMEM((HALF, pack), F32), pltpu.SemaphoreType.DMA((7,)),
        ],
        cost_estimate=pl.CostEstimate(flops=4_000_000_000, bytes_accessed=8_000_000, transcendentals=0),
        compiler_params=pltpu.CompilerParams(vmem_limit_bytes=8 * MIB),
        name="project_own",
    )(info, *far)


def attention_forward_kernel(
    info_ref, len_ref, _, __, ___, ____, oth_ref, turned_ref, cos_ref, sin_ref,
    q_ref, k_ref, v_ref, x_ref, ctx_ref, mine_ref, away_ref, lse_ref,
):
    rows = oth_ref.shape[0]
    cols, pack = q_ref.shape
    heads = cols // HDIM
    block = pack // SPANS
    segments, openings = block_facts(len_ref, block)
    side = info_ref[0]
    x_ref[at((1 - side) * rows, rows), :] = oth_ref[...]
    weights = [turned_ref[index * cols : (index + 1) * cols, :] for index in range(3)]
    project((q_ref, k_ref, v_ref), weights, oth_ref[...], openings, cos_ref, sin_ref, (1 - side) * rows)
    below = causal(block)

    spans = [slice(number * block, (number + 1) * block) for number in range(SPANS)]

    @pl.loop(0, heads // PAIR)
    def _(group):
        units = [(group * PAIR + number, i) for number in range(PAIR) for i in range(SPANS)]
        keys = [k_ref[at(head * HDIM, HDIM), :].T for head, i in units if i == 0]
        raw, done = {}, {}

        def scores(step):
            head, i = units[step]
            query = q_ref[at(head * HDIM, HDIM), spans[i]]
            raw[step] = [dot(keys[step // SPANS][spans[j]], query, 1, 0) for j in range(i + 1)]

        def softmax(step):
            head, i = units[step]
            parts = raw.pop(step)
            parts[i] = jnp.where(below, parts[i], NEG)
            biases = [jnp.where(segments[i] == segments[j], 0.0, NEG) for j in range(i)] + [0.0]
            top = functools.reduce(
                jnp.maximum, [jnp.max(part, axis=0, keepdims=True) + bias for part, bias in zip(parts, biases)]
            )
            probs = [jnp.exp2(part - (top - bias)) for part, bias in zip(parts, biases)]
            total = sum(jnp.sum(prob, axis=0, keepdims=True) for prob in probs)
            lse_ref[head, :, spans[i]] = top + jnp.log2(total)
            done[step] = [prob.astype(BF16) for prob in probs], 1.0 / total

        def context(step):
            head, i = units[step]
            here = at(head * HDIM, HDIM)
            probs, scale = done.pop(step)
            total = sum(dot(v_ref[here, spans[j]], prob, 1, 0) for j, prob in enumerate(probs))
            ctx_ref[here, spans[i]] = (total * scale).astype(BF16)

        for step in range(len(units) + 2):
            if step < len(units):
                scores(step)
            if 0 <= step - 1 < len(units):
                softmax(step - 1)
            if 0 <= step - 2:
                context(step - 2)
        here = at(group * PAIR * HDIM, PAIR * HDIM)
        mine_ref[here, :] = ctx_ref[here, at(side * rows, rows)]
        away_ref[here, :] = ctx_ref[here, at((1 - side) * rows, rows)]


def attention_forward(info, lengths, started, oth, turned):
    rows, width = oth.shape
    cols, pack = started[0].shape
    heads = cols // HDIM
    half = shape(BF16, cols, rows)
    return call(
        attention_forward_kernel, "attention_forward", (info, lengths),
        (*started, oth, turned, *rope_tables(pack)),
        [shape(BF16, cols, pack)] * 3 + [shape(BF16, pack, width), shape(BF16, cols, pack)]
        + [half, half, shape(F32, heads, 1, pack)],
        15_000_000_000, room=24,
        aliases={2 + index: index for index in range(4)},
    )


def attention_backward_kernel(
    info_ref, len_ref, q_ref, k_ref, v_ref, ctx_ref, own_ref, oth_ref, lse_ref, cos_ref, sin_ref, *rest,
    first, heads,
):
    dq_ref, dk_ref, dv_ref, dctx_ref = rest[-4:]
    rows = own_ref.shape[1]
    pack = q_ref.shape[1]
    block = pack // SPANS
    segments, openings = block_facts(len_ref, block)
    side = info_ref[0]
    below = causal(block)
    spans = [slice(number * block, (number + 1) * block) for number in range(SPANS)]

    def unturn(value, number, scale):
        here = at(number * block - openings[number], block)
        cos = cos_ref[:, here] * scale
        sin = sin_ref[:, here] * scale
        a, b = value[:HALF], value[HALF:]
        return jnp.concatenate([a * cos + b * sin, b * cos - a * sin], axis=0).astype(BF16)

    def plus(sums, index, value):
        sums[index] = sums[index] + value if index in sums else value

    @pl.loop(first, first + heads)
    def _(head):
        here = at(head * HDIM, HDIM)
        dctx_ref[:, at(side * rows, rows)] = own_ref[here, :]
        dctx_ref[:, at((1 - side) * rows, rows)] = oth_ref[here, :]
        key = k_ref[here, :]
        keys = key.T
        values = v_ref[here, :].T
        delta = jnp.sum(dctx_ref[...].astype(F32) * ctx_ref[here, :].astype(F32), axis=0, keepdims=True)
        lse = lse_ref[head, :, :]
        raw, done, dqs, dks, dvs = {}, {}, {}, {}, {}

        def scores(i, j):
            return (
                dot(keys[spans[j]], q_ref[here, spans[i]], 1, 0),
                dot(values[spans[j]], dctx_ref[:, spans[i]], 1, 0),
            )

        def slopes(i, j, score, slope):
            top = lse[:, spans[i]]
            if j == i:
                prob = jnp.exp2(jnp.where(below, score, NEG) - top)
            else:
                prob = jnp.exp2(score - (top - jnp.where(segments[i] == segments[j], 0.0, NEG)))
            return prob.astype(BF16), (prob * (slope - delta[:, spans[i]])).astype(BF16)

        def products(i, j, prob, dscore):
            plus(dqs, i, dot(key[:, spans[j]], dscore, 1, 0))
            plus(dks, j, dot(q_ref[here, spans[i]], dscore, 1, 1))
            plus(dvs, j, dot(dctx_ref[:, spans[i]], prob, 1, 1))

        pairs = [(i, j) for i in range(SPANS) for j in range(i + 1)]
        for step in range(len(pairs) + 2):
            if step < len(pairs):
                raw[step] = scores(*pairs[step])
            if 0 <= step - 1 < len(pairs):
                done[step - 1] = slopes(*pairs[step - 1], *raw.pop(step - 1))
            if 0 <= step - 2:
                products(*pairs[step - 2], *done.pop(step - 2))
        for number, lanes in enumerate(spans):
            dq_ref[here, lanes] = unturn(dqs[number], number, SCORE)
            dk_ref[here, lanes] = unturn(dks[number], number, 1.0 / LOG2E)
            dv_ref[here, lanes] = dvs[number].astype(BF16)


def attention_backward(info, lengths, kept, own, oth, first, heads, sofar):
    query, key, value, context, lse = kept
    cols, pack = query.shape
    arrays = (query, key, value, context, own, oth, lse, *rope_tables(pack), *sofar)
    base = 2 + len(arrays) - len(sofar)
    return call(
        functools.partial(attention_backward_kernel, first=first, heads=heads),
        "attention_backward", (info, lengths), arrays, [shape(BF16, cols, pack)] * 3,
        heads * 3_000_000_000,
        [pltpu.VMEM((HDIM, pack), BF16)],
        aliases={base + index: index for index in range(len(sofar))},
    )


def inverse_rms(value):
    return lax.rsqrt(jnp.mean(value * value, axis=-1, keepdims=True) + 1e-06)


def norm_back(value, gain, grad):
    inv = inverse_rms(value)
    scaled = grad * gain
    slope = jnp.mean(scaled * value, axis=-1, keepdims=True) * (inv * inv * inv)
    return scaled * inv - value * slope, grad * value * inv


def relative_rows(to_ref, from_ref, place, blocks):
    size = from_ref.shape[0] // blocks
    for block in range(blocks):
        to_ref[block * size : (block + 1) * size, :] = from_ref[at((block ^ place) * size, size), :]


def position(block, order):
    last = len(order) - 1
    return sum(((block >> bit) & 1) << (last - step) for step, bit in enumerate(order))


def ffn_forward_kernel(
    info_ref, len_ref, x_ref, mine_ref, came_ref, wo_ref, g1_ref, g2_ref, wg_ref, wu_ref, wd_ref, cot_ref,
    act_ref, s_ref, t_ref, out_ref, dm_ref, dmt_ref, hbt_ref, dr2_ref, r1_ref, small_ref,
    hb_ref, h_ref, m_ref, turn_ref, *, blocks,
):
    rows, width = x_ref.shape
    part = mine_ref.shape[0]
    total = len_ref[0] + len_ref[1] + len_ref[2] + len_ref[3]
    side = info_ref[0]
    first = side * rows

    def valid_of(start):
        places = lax.broadcasted_iota(jnp.int32, (ROWS, 1), 0) + (start + first)
        return (places < total).astype(F32)

    def squares(row, value, valid):
        add_small(small_ref, row, jnp.sum(value * value * valid, axis=0, keepdims=True))

    small_ref[...] = jnp.zeros_like(small_ref)
    m_ref[...] = dot(mine_ref[...].T, wo_ref[at(side * part, part), :], 1, 0) + dot(
        came_ref[...].T, wo_ref[at((1 - side) * part, part), :], 1, 0
    )

    @pl.loop(0, rows // ROWS, unroll=2)
    def _(index):
        here = at(index * ROWS, ROWS)
        valid = valid_of(index * ROWS)
        x = x_ref[here, :].astype(F32)
        a = m_ref[here, :]
        r1 = x + a
        h = r1 * inverse_rms(r1) * g1_ref[...]
        r1_ref[here, :] = r1
        h_ref[here, :] = h
        hb_ref[here, :] = h.astype(BF16)
        squares(2, x, valid)
        squares(3, a, valid)

    turn_ref[...] = hb_ref[...].T
    relative_rows(hbt_ref, turn_ref, info_ref[1], blocks)

    def inputs(step):
        cols = slice(step * CHUNK, (step + 1) * CHUNK)
        return dot(hb_ref[...], wg_ref[:, cols], 1, 0), dot(hb_ref[...], wu_ref[:, cols], 1, 0)

    count = act_ref.shape[1] // CHUNK
    ready = inputs(0)
    for step in range(count):
        gate, up = ready
        ready = inputs(step + 1) if step + 1 < count else None
        cols = slice(step * CHUNK, (step + 1) * CHUNK)
        sig = 1.0 / (1.0 + jnp.exp(-gate))
        silu = gate * sig
        act_ref[:, cols] = (silu * up).astype(BF16)
        s_ref[:, cols] = silu.astype(BF16)
        t_ref[:, cols] = (up * (sig + silu * (1.0 - sig))).astype(BF16)
    m_ref[...] = dot(act_ref[...], wd_ref[...], 1, 0)

    @pl.loop(0, rows // ROWS, unroll=2)
    def _(index):
        here = at(index * ROWS, ROWS)
        valid = valid_of(index * ROWS)
        m = m_ref[here, :]
        r2 = h_ref[here, :] + m
        gain = g2_ref[...]
        dr2, dgain = norm_back(r2, gain, cot_ref[here, :].astype(F32) * valid)
        out_ref[here, :] = (r2 * inverse_rms(r2) * gain).astype(BF16)
        dr2_ref[here, :] = dr2
        dm_ref[here, :] = dr2.astype(BF16)
        add_small(small_ref, 1, jnp.sum(dgain, axis=0, keepdims=True))
        squares(4, m, valid)

    add_small(small_ref, 5, jnp.full((1, width), jnp.clip(total - first, 0, rows).astype(F32)))
    turn_ref[...] = dm_ref[...].T
    relative_rows(dmt_ref, turn_ref, info_ref[1], blocks)


def ffn_forward(info, lengths, x, mine, came, w_out, g1, g2, wg, wu, wd, cot, blocks):
    rows, width = x.shape
    ff = wg.shape[1]
    return call(
        functools.partial(ffn_forward_kernel, blocks=blocks), "ffn_forward", (info, lengths),
        (x, mine, came, w_out, g1, g2, wg, wu, wd, cot),
        [shape(BF16, rows, ff)] * 3 + [shape(BF16, rows, width)] * 2 + [shape(BF16, width, rows)] * 2
        + [shape(F32, rows, width)] * 2 + [shape(F32, 16, WIDE)],
        6 * rows * width * ff,
        [
            pltpu.VMEM((rows, width), BF16), pltpu.VMEM((rows, width), F32),
            pltpu.VMEM((rows, width), F32), pltpu.VMEM((width, rows), BF16),
        ],
    )


def add_small(small_ref, row, value):
    for piece in range(-(-value.shape[1] // WIDE)):
        part = value[:, piece * WIDE : (piece + 1) * WIDE]
        small_ref[2 * row + piece : 2 * row + piece + 1, 0 : part.shape[1]] += part


def split_store(product, came, to_refs, order, blocks):
    size = product.shape[0] // blocks
    for block in range(blocks):
        place = position(block, order)
        rows = product[block * size : (block + 1) * size]
        if came is not None:
            rows = rows + came[place * size : (place + 1) * size].astype(F32)
        half = blocks // len(to_refs)
        start = (place % half) * size
        to_refs[place // half][start : start + size, :] = rows.astype(BF16)


def weight_kernel(info_ref, left_ref, right_ref, *rest, order, blocks):
    side = info_ref[0]
    mine = len(rest) == 3
    to_refs = rest[-2:] if mine else rest
    cols = to_refs[0].shape[1]
    start = (side if mine else 1 - side) * cols

    @pl.loop(0, cols // CHUNK, unroll=True)
    def _(step):
        here = at(step * CHUNK, CHUNK)
        right = right_ref[:, at(start + step * CHUNK, CHUNK)]
        came = rest[0][:, here] if mine else None
        split_store(dot(left_ref[...], right, 1, 0), came, [ref.at[:, here] for ref in to_refs], order, blocks)


def weight_grad(info, left, right, order, blocks, came=None):
    width, rows = left.shape
    cols = right.shape[1] // 2
    kernel = functools.partial(weight_kernel, order=order, blocks=blocks)
    flops = 2 * width * rows * cols
    if came is None:
        return call(kernel, "weight_away", (info,), (left, right), [shape(BF16, width, cols)], flops, room=ROOM)[0]
    return call(
        kernel, "weight_mine", (info,), (left, right, came), [shape(BF16, width // 2, cols)] * 2, flops, room=ROOM
    )


def swiglu_away_kernel(
    info_ref, dm_ref, wd_ref, s_ref, t_ref, hbt_ref, dgt_ref, dup_ref, gate_ref, up_ref, *, orders, blocks
):
    half = gate_ref.shape[1]
    count = half // CHUNK

    def grads(step):
        return swiglu_grads(
            (1 - info_ref[0]) * half + step * CHUNK, dm_ref, wd_ref, s_ref, t_ref, dgt_ref, dup_ref
        )

    ready = grads(0)
    for step in range(count):
        dgt, dup = ready
        ready = grads(step + 1) if step + 1 < count else None
        here = slice(step * CHUNK, (step + 1) * CHUNK)
        split_store(dot(hbt_ref[...], dgt, 1, 0), None, [gate_ref.at[:, here]], orders[0], blocks)
        split_store(dot(hbt_ref[...], dup, 1, 0), None, [up_ref.at[:, here]], orders[1], blocks)


def swiglu_grads(start, dm_ref, wd_ref, s_ref, t_ref, dgt_ref, dup_ref):
    cols = at(start, CHUNK)
    grad = dot(dm_ref[...], wd_ref[cols, :], 1, 1)
    dup = (grad * s_ref[:, cols].astype(F32)).astype(BF16)
    dgt = (grad * t_ref[:, cols].astype(F32)).astype(BF16)
    dup_ref[:, cols] = dup
    dgt_ref[:, cols] = dgt
    return dgt, dup


def swiglu_mine_kernel(info_ref, dm_ref, wd_ref, s_ref, t_ref, _, __, dgt_ref, dup_ref):
    half = s_ref.shape[1] // 2

    @pl.loop(0, half // CHUNK, unroll=True)
    def _(step):
        swiglu_grads(info_ref[0] * half + step * CHUNK, dm_ref, wd_ref, s_ref, t_ref, dgt_ref, dup_ref)


def swiglu_away(info, dm, wd, s, t, hbt, orders, blocks):
    rows, width = dm.shape
    ff = wd.shape[0]
    return call(
        functools.partial(swiglu_away_kernel, orders=orders, blocks=blocks), "swiglu_away", (info,),
        (dm, wd, s, t, hbt),
        [shape(BF16, rows, ff)] * 2 + [shape(BF16, width, ff // 2)] * 2,
        3 * rows * width * ff, room=ROOM,
    )


def swiglu_mine(info, dm, wd, s, t, dgt, dup):
    return call(
        swiglu_mine_kernel, "swiglu_mine", (info,), (dm, wd, s, t, dgt, dup), [shape(BF16, *dgt.shape)] * 2,
        dm.shape[0] * dm.shape[1] * wd.shape[0], aliases={5: 0, 6: 1},
    )


def norm_one_kernel(
    info_ref, dgt_ref, dup_ref, wg_ref, wu_ref, r1_ref, dr2_ref, g1_ref, wo_ref, part_ref,
    dr1_ref, dat_ref, own_ref, away_ref, small_ref, acc_ref, da_ref, turn_ref, *, blocks,
):
    rows = r1_ref.shape[0]
    cols = own_ref.shape[0]
    side = info_ref[0]
    acc_ref[...] = dr2_ref[...]

    @pl.loop(0, wg_ref.shape[1] // WIDE)
    def _(step):
        here = at(step * WIDE, WIDE)
        acc_ref[...] += dot(dgt_ref[:, here], wg_ref[:, here], 1, 1) + dot(dup_ref[:, here], wu_ref[:, here], 1, 1)

    small_ref[...] = part_ref[...]

    @pl.loop(0, rows // ROWS, unroll=2)
    def _(index):
        here = at(index * ROWS, ROWS)
        dr1, dgain = norm_back(r1_ref[here, :], g1_ref[...], acc_ref[here, :])
        dr1_ref[here, :] = dr1
        da_ref[here, :] = dr1.astype(BF16)
        add_small(small_ref, 0, jnp.sum(dgain, axis=0, keepdims=True))

    away_ref[...] = dot(wo_ref[at((1 - side) * cols, cols), :], da_ref[...], 1, 1).astype(BF16)
    own_ref[...] = dot(wo_ref[at(side * cols, cols), :], da_ref[...], 1, 1).astype(BF16)
    turn_ref[...] = da_ref[...].T
    relative_rows(dat_ref, turn_ref, info_ref[1], blocks)


def norm_one(info, dgt, dup, wg, wu, r1, dr2, g1, w_out, part, blocks):
    rows, width = r1.shape
    ff = wg.shape[1]
    cols = w_out.shape[0] // 2
    return call(
        functools.partial(norm_one_kernel, blocks=blocks), "norm_one_back", (info,),
        (dgt, dup, wg, wu, r1, dr2, g1, w_out, part),
        [
            shape(F32, rows, width), shape(BF16, width, rows), shape(BF16, cols, rows),
            shape(BF16, cols, rows), shape(F32, 16, WIDE),
        ],
        4 * rows * width * ff,
        [pltpu.VMEM((rows, width), F32), pltpu.VMEM((rows, width), BF16), pltpu.VMEM((width, rows), BF16)],
    )


def out_grad_kernel(dat_ref, mine_ref, came_ref, keep_ref, away_ref):
    away_ref[...] = dot(dat_ref[...], came_ref[...], 1, 1).astype(BF16)
    keep_ref[...] = dot(dat_ref[...], mine_ref[...], 1, 1).astype(BF16)


def out_grad(dat, mine, came):
    width, rows = dat.shape
    cols = mine.shape[0]
    return call(
        out_grad_kernel, "out_grad", (), (dat, mine, came), [shape(BF16, width, cols)] * 2,
        4 * width * rows * cols,
    )


def project_grad_kernel(info_ref, x_ref, dq_ref, dk_ref, dv_ref, mine_ref, came_ref, *rest, orders, blocks):
    out_refs, (turn_ref, left_ref) = rest[:-2], rest[-2:]
    turn_ref[...] = x_ref[...].T
    relative_rows(left_ref, turn_ref, info_ref[1], blocks)
    left = left_ref[...]
    cols = dq_ref.shape[0]
    piece = cols // 3
    for index, grad_ref in enumerate((dq_ref, dk_ref, dv_ref)):
        lanes = slice(index * piece, (index + 1) * piece)
        pair = out_refs[2 * index : 2 * index + 2]
        main = [ref.at[:, 0:cols] for ref in pair]
        tail = [ref.at[:, cols : cols + piece] for ref in pair]
        split_store(dot(left, grad_ref[...], 1, 1), None, main, orders[index], blocks)
        both = mine_ref[:, lanes].astype(F32) + came_ref[:, lanes].astype(F32)
        split_store(both, None, tail, orders[index], blocks)


def project_grad(info, x, grads, mine, came, orders, blocks):
    rows, width = x.shape
    cols = grads[0].shape[0]
    wide = cols + cols // 3
    return call(
        functools.partial(project_grad_kernel, orders=orders, blocks=blocks), "project_grad", (info,),
        (x, *grads, mine, came), [shape(BF16, width // 2, wide)] * 6, 6 * rows * width * cols,
        [pltpu.VMEM((width, rows), BF16)] * 2,
    )


def stream_grad_kernel(info_ref, dq_ref, dk_ref, dv_ref, wq_ref, wk_ref, wv_ref, *rest):
    cols, pack = dq_ref.shape
    rows = pack // 2
    side = info_ref[0]
    mine = len(rest) == 3
    lanes = at((side if mine else 1 - side) * rows, rows)
    total = sum(
        dot(w_ref[...], g_ref[:, lanes], 1, 0)
        for w_ref, g_ref in ((wq_ref, dq_ref), (wk_ref, dk_ref), (wv_ref, dv_ref))
    )
    if mine:
        came_ref, dr1_ref, out_ref = rest
        total = total + came_ref[...].astype(F32)
        out_ref[...] = (dr1_ref[...] + total.T).astype(BF16)
    else:
        rest[0][...] = total.astype(BF16)


def stream_grad(info, grads, weights, *others):
    cols, pack = grads[0].shape
    width = weights[0].shape[0]
    rows = pack // 2
    out = (rows, width) if others else (width, rows)
    return call(
        stream_grad_kernel, "stream_grad", (info,), (*grads, *weights, *others), [shape(BF16, *out)],
        6 * rows * width * cols,
    )[0]


def finish_kernel(
    query_ref, key_ref, value_ref, high_ref, low_ref, came_ref,
    gq_ref, gk_ref, gv_ref, out_ref, one_ref, two_ref, rms_ref,
):
    rows, cols = gq_ref.shape
    lines = high_ref.shape[0]
    starts = (0, rows + 2 * lines, 2 * rows + 2 * lines)
    tails = []
    for keep_ref, start, to_ref in zip((query_ref, key_ref, value_ref), starts, (gq_ref, gk_ref, gv_ref)):
        total = keep_ref[...].astype(F32) + came_ref[start : start + rows, :].astype(F32)
        to_ref[...] = total[:, :cols]
        tails.append(total[:, cols:])
    out_ref[...] = jnp.concatenate(tails, axis=1)
    small = whole_of(high_ref[...], low_ref[...]) + whole_of(
        came_ref[rows : rows + lines, :], came_ref[rows + lines : rows + 2 * lines, :]
    )
    lanes = one_ref.shape[1]
    width = one_ref.shape[0] * lanes
    for number in range(one_ref.shape[0]):
        line, start = divmod(number * lanes, WIDE)
        for index, to_ref in enumerate((one_ref, two_ref)):
            to_ref[number : number + 1, :] = small[2 * index + line : 2 * index + line + 1, start : start + lanes]
    sums = jnp.sum(small[4:10], axis=1, keepdims=True)
    count = small[10:11, 0:1] * width
    for index in range(3):
        rms_ref[:, index : index + 1] = jnp.sqrt((sums[2 * index : 2 * index + 1] + sums[2 * index + 1 : 2 * index + 2]) / count)


def finish(parts, came, width, head_cols):
    rows = parts[0].keep.shape[0]
    return call(
        finish_kernel, "finish", (), (*[part.keep for part in parts], *parts[0].pair, came),
        [shape(F32, rows, head_cols)] * 4 + [shape(F32, width // 128, 128)] * 2 + [shape(F32, 1, 3)],
        1_000_000, room=4,
    )


def swap_seq(value):
    return lax.ppermute(value, "seq", [(0, 1), (1, 0)])


def swap_dp(value, bit):
    size = lax.axis_size("dp")
    return lax.ppermute(value, "dp", [(i, i ^ (1 << bit)) for i in range(size)])


def halves_of(small):
    high = lax.reduce_precision(small, 8, 7)
    return high.astype(BF16), (small - high).astype(BF16)


def whole_of(high, low):
    return high.astype(F32) + low.astype(F32)


class Halving:
    def __init__(self, keep, away, order, shift, small=None):
        self.keep, self.order, self.shift, self.small = keep, order, shift, small
        self.sent, self.step = away, 0

    def send(self):
        if self.small is not None:
            self.pair = halves_of(self.small)
            self.sent = jnp.concatenate([self.sent, *self.pair], axis=0)
        self.came = swap_dp(self.sent, self.order[self.step] + self.shift)
        self.step += 1

    def receive(self):
        rows = self.keep.shape[0]
        if self.small is not None:
            count = self.small.shape[0]
            came = self.came[rows : rows + count], self.came[rows + count :]
            self.small = whole_of(*self.pair) + whole_of(*came)
        if self.step < len(self.order):
            self.sent = self.add(rows // 2, rows)
            self.keep = self.add(0, rows // 2)
        else:
            self.keep = self.keep.astype(F32) + self.came[:rows].astype(F32)

    def add(self, low, high):
        return (self.keep[low:high].astype(F32) + self.came[low:high].astype(F32)).astype(BF16)

    def relay(self, *others):
        if others:
            self.keep = after(self.keep, *others)
        self.receive()
        self.send()

    @staticmethod
    def last(parts, done=False):
        for part in parts:
            part.receive()
            part.size = part.sent.shape[0]
        rows = [part.sent for part in parts]
        small = parts[0].small
        if small is not None:
            parts[0].pair = halves_of(small)
            rows[1:1] = parts[0].pair
        joint = jnp.concatenate(rows, axis=0)
        came = swap_dp(joint, parts[0].order[-1] + parts[0].shift)
        if done:
            return came
        start = 0
        for part in parts:
            end = start + part.size + (2 * small.shape[0] if part.small is not None else 0)
            part.came = came[start:end]
            start = end
            part.step += 1
            part.receive()
        return joint

    def rest(self):
        value = self.keep
        for bit in reversed(range(self.shift)):
            half = value.shape[0] // 2
            mine = (lax.axis_index("dp") >> bit) & 1
            keep = lax.dynamic_slice_in_dim(value, mine * half, half, 0)
            away = lax.dynamic_slice_in_dim(value, (1 - mine) * half, half, 0)
            value = keep + swap_dp(away.astype(BF16), bit).astype(F32)
            if self.small is not None:
                self.small = self.small + swap_dp(self.small, bit)
        return value


def after(values, *others):
    return lax.optimization_barrier((values, others))[0]


def shards(
    tokens,
    doc_lengths,
    w_query,
    w_key,
    w_value,
    w_out,
    w_gate,
    w_up,
    w_down,
    gain_attn,
    gain_ffn,
    cotangent,
):
    row_count, width = tokens.shape
    head_cols = w_query.shape[1] // lax.axis_size("seq")
    dp_size = lax.axis_size("dp")
    blocks = min(dp_size, 16)
    shift = (dp_size // blocks).bit_length() - 1
    orders = ((0, 2, 1, 3), (1, 0, 2, 3), (2, 3, 0, 1))
    turns = ((1, 2, 0, 3), (1, 0, 2, 3), (2, 1, 0, 3))
    lengths = doc_lengths[0]
    seq_index = lax.axis_index("seq")
    info = jnp.stack([seq_index, lax.axis_index("dp") >> shift]).astype(jnp.int32)
    gain_one, gain_two = gain_attn.reshape(1, width), gain_ffn.reshape(1, width)

    oth = swap_seq(tokens)
    *started, turned, own_q, own_k, own_v = project_own(info, doc_lengths, tokens, (w_query, w_key, w_value))
    query, key, value, gathered, context, mine, away, lse = attention_forward(
        info, lengths, started, oth, turned
    )
    kept = (query, key, value, context, lse)
    came = swap_seq(away)
    act, silu, slope, result, dm, dm_turned, hb_turned, dr2, r1, small = ffn_forward(
        info, lengths, tokens, mine, came, w_out, gain_one, gain_two, w_gate, w_up, w_down, cotangent, blocks
    )
    down_away = weight_grad(info, dm_turned, act, orders[2], blocks)
    down_came = swap_seq(down_away)
    dgt, dup, gate_away, up_away = swiglu_away(
        info, after(dm, down_away), w_down, silu, slope, hb_turned, orders[:2], blocks
    )
    gate_came, up_came = swap_seq(gate_away), swap_seq(up_away)
    down = Halving(
        *weight_grad(info, dm_turned, after(act, gate_away), orders[2], blocks, down_came), orders[2], shift
    )
    down.send()
    dgt, dup = swiglu_mine(info, after(dm, down.sent), w_down, silu, slope, dgt, dup)
    gate = Halving(*weight_grad(info, hb_turned, dgt, orders[0], blocks, gate_came), orders[0], shift)
    gate.send()
    dr1, da_turned, own_rows, away_rows, small = norm_one(
        info, after(dgt, gate.sent), dup, w_gate, w_up, r1, dr2, gain_one, w_out, small, blocks
    )
    came_rows = swap_seq(away_rows)
    up = Halving(
        *weight_grad(info, after(hb_turned, away_rows), dup, orders[1], blocks, up_came), orders[1], shift
    )
    up.send()
    out_keep, out_away = out_grad(after(da_turned, up.sent), mine, came)
    out_came = swap_seq(out_away)
    small = small + swap_seq(small)
    grads = ()
    each = head_cols // HDIM // len(PLAN)
    ffn = [down, gate, up]
    for number, relays in enumerate(PLAN):
        for part in relays:
            ffn[part].relay(*grads)
        own_rows = after(own_rows, out_away, *[ffn[part].sent for part in relays], *grads)
        grads = attention_backward(
            info, lengths, kept, own_rows, came_rows, number * each, each, grads
        )
    sides = project_grad(info, gathered, grads, out_keep, out_came, turns, blocks)
    attn = [
        Halving(sides[2 * index], sides[2 * index + 1], turns[index], shift, None if index else small)
        for index in range(3)
    ]
    up.relay(*sides)
    query_part, key_part, value_part = attn
    key_part.send()
    value_part.send()
    weights = (own_q, own_k, own_v)
    stream_away = stream_grad(info, after(grads, *sides, up.sent), weights)
    stream_came = swap_seq(stream_away)
    gate.relay(stream_away)
    down.relay(stream_away)
    query_part.sent = after(query_part.sent, gate.sent, down.sent, key_part.came)
    query_part.send()
    grad_tokens = stream_grad(info, after(grads, key_part.came), weights, stream_came, dr1)
    up.relay(grad_tokens)
    key_part.relay(up.sent)
    value_part.relay(up.sent)
    joint = Halving.last([gate, up])
    down.relay(joint)
    query_part.relay(joint)
    for part in (key_part, value_part, query_part):
        part.relay(joint)
    down.receive()
    summed_down, summed_gate, summed_up = (part.rest() for part in ffn)
    summed_down = summed_down.T
    if shift:
        Halving.last(attn)
        sums = [part.rest() for part in attn]
        attn_grads = [total[:, :head_cols] for total in sums]
        attn_grads.append(jnp.concatenate([total[:, head_cols:] for total in sums], axis=1).T)
        small = attn[0].small.reshape(8, 2 * WIDE)[:, :width]
        grad_one, grad_two = small[0], small[1]
        rms_values = jnp.sqrt(jnp.sum(small[2:5], axis=1) / (small[5, 0] * width))
    else:
        came = after(Halving.last(attn, True), summed_down, summed_gate, summed_up, grad_tokens)
        *attn_grads, grad_wo, grad_one, grad_two, rms_values = finish(attn, came, width, head_cols)
        attn_grads.append(grad_wo.T)
    return (
        result,
        grad_tokens,
        *attn_grads,
        summed_gate,
        summed_up,
        summed_down,
        grad_one.reshape(-1),
        grad_two.reshape(-1),
        rms_values.reshape(-1),
    )


def solution(mesh):
    return jax.shard_map(
        shards,
        mesh=mesh,
        in_specs=(
            P(("dp", "seq"), None),
            P("dp", None),
            P(),
            P(),
            P(),
            P(),
            P(),
            P(),
            P(),
            P(),
            P(),
            P(("dp", "seq"), None),
        ),
        out_specs=(
            P(("dp", "seq"), None),
            P(("dp", "seq"), None),
            P("dp", "seq"),
            P("dp", "seq"),
            P("dp", "seq"),
            P("seq", "dp"),
            P("dp", "seq"),
            P("dp", "seq"),
            P("seq", "dp"),
            P(),
            P(),
            P(),
        ),
        check_vma=False,
    )
```

```python
import functools
import math

import jax
import jax.numpy as jnp
import numpy as np
from jax import lax
from jax.experimental import pallas as pl
from jax.experimental.pallas import tpu as pltpu
from jax.sharding import PartitionSpec as P

HDIM = 48
HALF = HDIM // 2
SCORE = 1.0 / math.sqrt(HDIM)
LOG2E = 1.0 / math.log(2.0)
NEG = -1e30
BF16 = jnp.bfloat16
F32 = jnp.float32
CHUNK = 256
WIDE = 512
ROWS = 64
SPANS = 4
PAIR = 2
PLAN = ((), (0, 1))
MIB = 1 << 20
EASE = 50
ROOM = 8


def call(kernel, name, scalars, arrays, out_shape, flops, scratch=(), room=16, aliases=None):
    moved = sum(math.prod(o.shape) * o.dtype.itemsize for o in out_shape)
    return pl.pallas_call(
        kernel,
        in_specs=[pl.BlockSpec(memory_space=pltpu.SMEM)] * len(scalars)
        + [pl.BlockSpec(memory_space=pltpu.VMEM)] * len(arrays),
        out_specs=[pl.BlockSpec(memory_space=pltpu.VMEM)] * len(out_shape),
        out_shape=out_shape,
        scratch_shapes=list(scratch),
        input_output_aliases=aliases or {},
        cost_estimate=pl.CostEstimate(flops=flops // EASE, bytes_accessed=moved // EASE, transcendentals=0),
        compiler_params=pltpu.CompilerParams(vmem_limit_bytes=room * MIB),
        name=name,
    )(*scalars, *arrays)


def shape(dtype, *dims):
    return jax.ShapeDtypeStruct(dims, dtype)


def at(start, size):
    return pl.ds(pl.multiple_of(start, size), size)


def dot(a, b, ca, cb):
    return lax.dot_general(a, b, (((ca,), (cb,)), ((), ())), preferred_element_type=F32)


def rope_tables(span):
    freq = 10000.0 ** (-np.arange(HALF, dtype=np.float64) / HALF)
    phase = freq[:, None] * np.arange(span, dtype=np.float64)[None, :]
    return np.cos(phase).astype(np.float32), np.sin(phase).astype(np.float32)


def block_facts(len_ref, block):
    ends = []
    total = 0
    for index in range(len_ref.shape[0]):
        total = total + len_ref[index]
        ends.append(total)
    segments, openings = [], []
    for number in range(SPANS):
        segment = 0
        opening = 0
        for index, end in enumerate(ends):
            done = number * block >= end
            segment = segment + done.astype(jnp.int32)
            opening = opening + jnp.where(done, len_ref[index], 0)
        segments.append(segment)
        openings.append(opening)
    return segments, openings


def causal(block):
    key = lax.broadcasted_iota(jnp.int32, (block, block), 0)
    return key <= lax.broadcasted_iota(jnp.int32, (block, block), 1)


def project(to_refs, weights, x, openings, cos_ref, sin_ref, start):
    rows = x.shape[0]
    cols, pack = to_refs[0].shape
    block = pack // SPANS
    for weight, to_ref, scale in zip(weights, to_refs, (SCORE * LOG2E, 1.0, None)):
        for number in range(rows // block):
            part = dot(weight, x[number * block : (number + 1) * block], 1, 1)
            first = start + number * block
            if scale is None:
                to_ref[:, at(first, block)] = part.astype(BF16)
                continue
            opening = functools.reduce(
                lambda rest, span: jnp.where(first == span * block, openings[span], rest), range(SPANS), 0
            )
            here = at(first - opening, block)
            cos = cos_ref[:, here] * scale
            sin = sin_ref[:, here] * scale
            for head in range(cols // HDIM):
                a = part[head * HDIM : head * HDIM + HALF]
                b = part[head * HDIM + HALF : (head + 1) * HDIM]
                turned = jnp.concatenate([a * cos - b * sin, b * cos + a * sin], axis=0)
                to_ref[head * HDIM : (head + 1) * HDIM, at(first, block)] = turned.astype(BF16)


def project_own_kernel(
    info_ref, from_len_ref, from_x_ref, from_cos_ref, from_sin_ref, wq_ref, wk_ref, wv_ref,
    q_ref, k_ref, v_ref, all_ref, turned_ref, cq_ref, ck_ref, cv_ref,
    len_ref, x_ref, cos_ref, sin_ref, sems,
):
    cols, pack = q_ref.shape
    rows = x_ref.shape[0]
    side = info_ref[0]
    pairs = [(from_x_ref, x_ref)]
    pairs += [
        (w_ref.at[:, at(side * cols, cols)], c_ref)
        for w_ref, c_ref in ((wq_ref, cq_ref), (wk_ref, ck_ref), (wv_ref, cv_ref))
    ]
    pairs += [(from_cos_ref, cos_ref), (from_sin_ref, sin_ref), (from_len_ref, len_ref)]
    copies = [pltpu.make_async_copy(*pair, sems.at[index]) for index, pair in enumerate(pairs)]
    for copy in copies:
        copy.start()
    for index, c_ref in enumerate((cq_ref, ck_ref, cv_ref)):
        copies[1 + index].wait()
        turned_ref[index * cols : (index + 1) * cols, :] = c_ref[...].T
    for index in (0, 4, 5, 6):
        copies[index].wait()
    _, openings = block_facts(len_ref.at[0], pack // SPANS)
    all_ref[at(side * rows, rows), :] = x_ref[...]
    weights = [turned_ref[index * cols : (index + 1) * cols, :] for index in range(3)]
    project((q_ref, k_ref, v_ref), weights, x_ref[...], openings, cos_ref, sin_ref, side * rows)


def project_own(info, lengths, own, weights):
    rows, width = own.shape
    pack = 2 * rows
    cols = weights[0].shape[1] // 2
    vmem = pl.BlockSpec(memory_space=pltpu.VMEM)
    far = [pltpu.with_memory_space_constraint(jnp.asarray(value), pltpu.HBM) for value in (lengths, own, *rope_tables(pack), *weights)]
    return pl.pallas_call(
        project_own_kernel,
        in_specs=[pl.BlockSpec(memory_space=pltpu.SMEM)] + [pl.BlockSpec(memory_space=pltpu.HBM)] * 7,
        out_specs=[vmem] * 8,
        out_shape=[shape(BF16, cols, pack)] * 3
        + [shape(BF16, pack, width), shape(BF16, 3 * cols, width)]
        + [shape(BF16, width, cols)] * 3,
        scratch_shapes=[
            pltpu.SMEM(lengths.shape, jnp.int32), pltpu.VMEM(own.shape, BF16),
            pltpu.VMEM((HALF, pack), F32), pltpu.VMEM((HALF, pack), F32), pltpu.SemaphoreType.DMA((7,)),
        ],
        cost_estimate=pl.CostEstimate(flops=4_000_000_000, bytes_accessed=8_000_000, transcendentals=0),
        compiler_params=pltpu.CompilerParams(vmem_limit_bytes=8 * MIB),
        name="project_own",
    )(info, *far)


def attention_forward_kernel(
    info_ref, len_ref, _, __, ___, ____, oth_ref, turned_ref, cos_ref, sin_ref,
    q_ref, k_ref, v_ref, x_ref, ctx_ref, mine_ref, away_ref, lse_ref,
):
    rows = oth_ref.shape[0]
    cols, pack = q_ref.shape
    heads = cols // HDIM
    block = pack // SPANS
    segments, openings = block_facts(len_ref, block)
    side = info_ref[0]
    x_ref[at((1 - side) * rows, rows), :] = oth_ref[...]
    weights = [turned_ref[index * cols : (index + 1) * cols, :] for index in range(3)]
    project((q_ref, k_ref, v_ref), weights, oth_ref[...], openings, cos_ref, sin_ref, (1 - side) * rows)
    below = causal(block)

    spans = [slice(number * block, (number + 1) * block) for number in range(SPANS)]

    @pl.loop(0, heads // PAIR)
    def _(group):
        units = [(group * PAIR + number, i) for number in range(PAIR) for i in range(SPANS)]
        keys = [k_ref[at(head * HDIM, HDIM), :].T for head, i in units if i == 0]
        raw, done = {}, {}

        def scores(step):
            head, i = units[step]
            query = q_ref[at(head * HDIM, HDIM), spans[i]]
            raw[step] = [dot(keys[step // SPANS][spans[j]], query, 1, 0) for j in range(i + 1)]

        def softmax(step):
            head, i = units[step]
            parts = raw.pop(step)
            parts[i] = jnp.where(below, parts[i], NEG)
            biases = [jnp.where(segments[i] == segments[j], 0.0, NEG) for j in range(i)] + [0.0]
            top = functools.reduce(
                jnp.maximum, [jnp.max(part, axis=0, keepdims=True) + bias for part, bias in zip(parts, biases)]
            )
            probs = [jnp.exp2(part - (top - bias)) for part, bias in zip(parts, biases)]
            total = sum(jnp.sum(prob, axis=0, keepdims=True) for prob in probs)
            lse_ref[head, :, spans[i]] = top + jnp.log2(total)
            done[step] = [prob.astype(BF16) for prob in probs], 1.0 / total

        def context(step):
            head, i = units[step]
            here = at(head * HDIM, HDIM)
            probs, scale = done.pop(step)
            total = sum(dot(v_ref[here, spans[j]], prob, 1, 0) for j, prob in enumerate(probs))
            ctx_ref[here, spans[i]] = (total * scale).astype(BF16)

        for step in range(len(units) + 2):
            if step < len(units):
                scores(step)
            if 0 <= step - 1 < len(units):
                softmax(step - 1)
            if 0 <= step - 2:
                context(step - 2)
        here = at(group * PAIR * HDIM, PAIR * HDIM)
        mine_ref[here, :] = ctx_ref[here, at(side * rows, rows)]
        away_ref[here, :] = ctx_ref[here, at((1 - side) * rows, rows)]


def attention_forward(info, lengths, started, oth, turned):
    rows, width = oth.shape
    cols, pack = started[0].shape
    heads = cols // HDIM
    half = shape(BF16, cols, rows)
    return call(
        attention_forward_kernel, "attention_forward", (info, lengths),
        (*started, oth, turned, *rope_tables(pack)),
        [shape(BF16, cols, pack)] * 3 + [shape(BF16, pack, width), shape(BF16, cols, pack)]
        + [half, half, shape(F32, heads, 1, pack)],
        15_000_000_000, room=24,
        aliases={2 + index: index for index in range(4)},
    )


def attention_backward_kernel(
    info_ref, len_ref, q_ref, k_ref, v_ref, ctx_ref, own_ref, oth_ref, lse_ref, cos_ref, sin_ref, *rest,
    first, heads,
):
    dq_ref, dk_ref, dv_ref, dctx_ref = rest[-4:]
    rows = own_ref.shape[1]
    pack = q_ref.shape[1]
    block = pack // SPANS
    segments, openings = block_facts(len_ref, block)
    side = info_ref[0]
    below = causal(block)
    spans = [slice(number * block, (number + 1) * block) for number in range(SPANS)]

    def unturn(value, number, scale):
        here = at(number * block - openings[number], block)
        cos = cos_ref[:, here] * scale
        sin = sin_ref[:, here] * scale
        a, b = value[:HALF], value[HALF:]
        return jnp.concatenate([a * cos + b * sin, b * cos - a * sin], axis=0).astype(BF16)

    def plus(sums, index, value):
        sums[index] = sums[index] + value if index in sums else value

    @pl.loop(first, first + heads)
    def _(head):
        here = at(head * HDIM, HDIM)
        dctx_ref[:, at(side * rows, rows)] = own_ref[here, :]
        dctx_ref[:, at((1 - side) * rows, rows)] = oth_ref[here, :]
        key = k_ref[here, :]
        keys = key.T
        values = v_ref[here, :].T
        delta = jnp.sum(dctx_ref[...].astype(F32) * ctx_ref[here, :].astype(F32), axis=0, keepdims=True)
        lse = lse_ref[head, :, :]
        raw, done, dqs, dks, dvs = {}, {}, {}, {}, {}

        def scores(i, j):
            return (
                dot(keys[spans[j]], q_ref[here, spans[i]], 1, 0),
                dot(values[spans[j]], dctx_ref[:, spans[i]], 1, 0),
            )

        def slopes(i, j, score, slope):
            top = lse[:, spans[i]]
            if j == i:
                prob = jnp.exp2(jnp.where(below, score, NEG) - top)
            else:
                prob = jnp.exp2(score - (top - jnp.where(segments[i] == segments[j], 0.0, NEG)))
            return prob.astype(BF16), (prob * (slope - delta[:, spans[i]])).astype(BF16)

        def products(i, j, prob, dscore):
            plus(dqs, i, dot(key[:, spans[j]], dscore, 1, 0))
            plus(dks, j, dot(q_ref[here, spans[i]], dscore, 1, 1))
            plus(dvs, j, dot(dctx_ref[:, spans[i]], prob, 1, 1))

        pairs = [(i, j) for i in range(SPANS) for j in range(i + 1)]
        for step in range(len(pairs) + 2):
            if step < len(pairs):
                raw[step] = scores(*pairs[step])
            if 0 <= step - 1 < len(pairs):
                done[step - 1] = slopes(*pairs[step - 1], *raw.pop(step - 1))
            if 0 <= step - 2:
                products(*pairs[step - 2], *done.pop(step - 2))
        for number, lanes in enumerate(spans):
            dq_ref[here, lanes] = unturn(dqs[number], number, SCORE)
            dk_ref[here, lanes] = unturn(dks[number], number, 1.0 / LOG2E)
            dv_ref[here, lanes] = dvs[number].astype(BF16)


def attention_backward(info, lengths, kept, own, oth, first, heads, sofar):
    query, key, value, context, lse = kept
    cols, pack = query.shape
    arrays = (query, key, value, context, own, oth, lse, *rope_tables(pack), *sofar)
    base = 2 + len(arrays) - len(sofar)
    return call(
        functools.partial(attention_backward_kernel, first=first, heads=heads),
        "attention_backward", (info, lengths), arrays, [shape(BF16, cols, pack)] * 3,
        heads * 3_000_000_000,
        [pltpu.VMEM((HDIM, pack), BF16)],
        aliases={base + index: index for index in range(len(sofar))},
    )


def inverse_rms(value):
    return lax.rsqrt(jnp.mean(value * value, axis=-1, keepdims=True) + 1e-06)


def norm_back(value, gain, grad):
    inv = inverse_rms(value)
    scaled = grad * gain
    slope = jnp.mean(scaled * value, axis=-1, keepdims=True) * (inv * inv * inv)
    return scaled * inv - value * slope, grad * value * inv


def relative_rows(to_ref, from_ref, place, blocks):
    size = from_ref.shape[0] // blocks
    for block in range(blocks):
        to_ref[block * size : (block + 1) * size, :] = from_ref[at((block ^ place) * size, size), :]


def position(block, order):
    last = len(order) - 1
    return sum(((block >> bit) & 1) << (last - step) for step, bit in enumerate(order))


def ffn_forward_kernel(
    info_ref, len_ref, x_ref, mine_ref, came_ref, wo_ref, g1_ref, g2_ref, wg_ref, wu_ref, wd_ref, cot_ref,
    act_ref, s_ref, t_ref, out_ref, dm_ref, dmt_ref, hbt_ref, dr2_ref, r1_ref, small_ref,
    hb_ref, h_ref, m_ref, turn_ref, *, blocks,
):
    rows, width = x_ref.shape
    part = mine_ref.shape[0]
    total = len_ref[0] + len_ref[1] + len_ref[2] + len_ref[3]
    side = info_ref[0]
    first = side * rows

    def valid_of(start):
        places = lax.broadcasted_iota(jnp.int32, (ROWS, 1), 0) + (start + first)
        return (places < total).astype(F32)

    def squares(row, value, valid):
        add_small(small_ref, row, jnp.sum(value * value * valid, axis=0, keepdims=True))

    small_ref[...] = jnp.zeros_like(small_ref)
    m_ref[...] = dot(mine_ref[...].T, wo_ref[at(side * part, part), :], 1, 0) + dot(
        came_ref[...].T, wo_ref[at((1 - side) * part, part), :], 1, 0
    )

    @pl.loop(0, rows // ROWS, unroll=2)
    def _(index):
        here = at(index * ROWS, ROWS)
        valid = valid_of(index * ROWS)
        x = x_ref[here, :].astype(F32)
        a = m_ref[here, :]
        r1 = x + a
        h = r1 * inverse_rms(r1) * g1_ref[...]
        r1_ref[here, :] = r1
        h_ref[here, :] = h
        hb_ref[here, :] = h.astype(BF16)
        squares(2, x, valid)
        squares(3, a, valid)

    turn_ref[...] = hb_ref[...].T
    relative_rows(hbt_ref, turn_ref, info_ref[1], blocks)

    def inputs(step):
        cols = slice(step * CHUNK, (step + 1) * CHUNK)
        return dot(hb_ref[...], wg_ref[:, cols], 1, 0), dot(hb_ref[...], wu_ref[:, cols], 1, 0)

    count = act_ref.shape[1] // CHUNK
    ready = inputs(0)
    for step in range(count):
        gate, up = ready
        ready = inputs(step + 1) if step + 1 < count else None
        cols = slice(step * CHUNK, (step + 1) * CHUNK)
        sig = 1.0 / (1.0 + jnp.exp(-gate))
        silu = gate * sig
        act_ref[:, cols] = (silu * up).astype(BF16)
        s_ref[:, cols] = silu.astype(BF16)
        t_ref[:, cols] = (up * (sig + silu * (1.0 - sig))).astype(BF16)
    m_ref[...] = dot(act_ref[...], wd_ref[...], 1, 0)

    @pl.loop(0, rows // ROWS, unroll=2)
    def _(index):
        here = at(index * ROWS, ROWS)
        valid = valid_of(index * ROWS)
        m = m_ref[here, :]
        r2 = h_ref[here, :] + m
        gain = g2_ref[...]
        dr2, dgain = norm_back(r2, gain, cot_ref[here, :].astype(F32) * valid)
        out_ref[here, :] = (r2 * inverse_rms(r2) * gain).astype(BF16)
        dr2_ref[here, :] = dr2
        dm_ref[here, :] = dr2.astype(BF16)
        add_small(small_ref, 1, jnp.sum(dgain, axis=0, keepdims=True))
        squares(4, m, valid)

    add_small(small_ref, 5, jnp.full((1, width), jnp.clip(total - first, 0, rows).astype(F32)))
    turn_ref[...] = dm_ref[...].T
    relative_rows(dmt_ref, turn_ref, info_ref[1], blocks)


def ffn_forward(info, lengths, x, mine, came, w_out, g1, g2, wg, wu, wd, cot, blocks):
    rows, width = x.shape
    ff = wg.shape[1]
    return call(
        functools.partial(ffn_forward_kernel, blocks=blocks), "ffn_forward", (info, lengths),
        (x, mine, came, w_out, g1, g2, wg, wu, wd, cot),
        [shape(BF16, rows, ff)] * 3 + [shape(BF16, rows, width)] * 2 + [shape(BF16, width, rows)] * 2
        + [shape(F32, rows, width)] * 2 + [shape(F32, 16, WIDE)],
        6 * rows * width * ff,
        [
            pltpu.VMEM((rows, width), BF16), pltpu.VMEM((rows, width), F32),
            pltpu.VMEM((rows, width), F32), pltpu.VMEM((width, rows), BF16),
        ],
    )


def add_small(small_ref, row, value):
    for piece in range(-(-value.shape[1] // WIDE)):
        part = value[:, piece * WIDE : (piece + 1) * WIDE]
        small_ref[2 * row + piece : 2 * row + piece + 1, 0 : part.shape[1]] += part


def split_store(product, came, to_refs, order, blocks):
    size = product.shape[0] // blocks
    for block in range(blocks):
        place = position(block, order)
        rows = product[block * size : (block + 1) * size]
        if came is not None:
            rows = rows + came[place * size : (place + 1) * size].astype(F32)
        half = blocks // len(to_refs)
        start = (place % half) * size
        to_refs[place // half][start : start + size, :] = rows.astype(BF16)


def weight_kernel(info_ref, left_ref, right_ref, *rest, order, blocks):
    side = info_ref[0]
    mine = len(rest) == 3
    to_refs = rest[-2:] if mine else rest
    cols = to_refs[0].shape[1]
    start = (side if mine else 1 - side) * cols

    @pl.loop(0, cols // CHUNK, unroll=True)
    def _(step):
        here = at(step * CHUNK, CHUNK)
        right = right_ref[:, at(start + step * CHUNK, CHUNK)]
        came = rest[0][:, here] if mine else None
        split_store(dot(left_ref[...], right, 1, 0), came, [ref.at[:, here] for ref in to_refs], order, blocks)


def weight_grad(info, left, right, order, blocks, came=None):
    width, rows = left.shape
    cols = right.shape[1] // 2
    kernel = functools.partial(weight_kernel, order=order, blocks=blocks)
    flops = 2 * width * rows * cols
    if came is None:
        return call(kernel, "weight_away", (info,), (left, right), [shape(BF16, width, cols)], flops, room=ROOM)[0]
    return call(
        kernel, "weight_mine", (info,), (left, right, came), [shape(BF16, width // 2, cols)] * 2, flops, room=ROOM
    )


def swiglu_away_kernel(
    info_ref, dm_ref, wd_ref, s_ref, t_ref, hbt_ref, dgt_ref, dup_ref, gate_ref, up_ref, *, orders, blocks
):
    half = gate_ref.shape[1]
    count = half // CHUNK

    def grads(step):
        return swiglu_grads(
            (1 - info_ref[0]) * half + step * CHUNK, dm_ref, wd_ref, s_ref, t_ref, dgt_ref, dup_ref
        )

    ready = grads(0)
    for step in range(count):
        dgt, dup = ready
        ready = grads(step + 1) if step + 1 < count else None
        here = slice(step * CHUNK, (step + 1) * CHUNK)
        split_store(dot(hbt_ref[...], dgt, 1, 0), None, [gate_ref.at[:, here]], orders[0], blocks)
        split_store(dot(hbt_ref[...], dup, 1, 0), None, [up_ref.at[:, here]], orders[1], blocks)


def swiglu_grads(start, dm_ref, wd_ref, s_ref, t_ref, dgt_ref, dup_ref):
    cols = at(start, CHUNK)
    grad = dot(dm_ref[...], wd_ref[cols, :], 1, 1)
    dup = (grad * s_ref[:, cols].astype(F32)).astype(BF16)
    dgt = (grad * t_ref[:, cols].astype(F32)).astype(BF16)
    dup_ref[:, cols] = dup
    dgt_ref[:, cols] = dgt
    return dgt, dup


def swiglu_mine_kernel(info_ref, dm_ref, wd_ref, s_ref, t_ref, _, __, dgt_ref, dup_ref):
    half = s_ref.shape[1] // 2

    @pl.loop(0, half // CHUNK, unroll=True)
    def _(step):
        swiglu_grads(info_ref[0] * half + step * CHUNK, dm_ref, wd_ref, s_ref, t_ref, dgt_ref, dup_ref)


def swiglu_away(info, dm, wd, s, t, hbt, orders, blocks):
    rows, width = dm.shape
    ff = wd.shape[0]
    return call(
        functools.partial(swiglu_away_kernel, orders=orders, blocks=blocks), "swiglu_away", (info,),
        (dm, wd, s, t, hbt),
        [shape(BF16, rows, ff)] * 2 + [shape(BF16, width, ff // 2)] * 2,
        3 * rows * width * ff, room=ROOM,
    )


def swiglu_mine(info, dm, wd, s, t, dgt, dup):
    return call(
        swiglu_mine_kernel, "swiglu_mine", (info,), (dm, wd, s, t, dgt, dup), [shape(BF16, *dgt.shape)] * 2,
        dm.shape[0] * dm.shape[1] * wd.shape[0], aliases={5: 0, 6: 1},
    )


def norm_one_kernel(
    info_ref, dgt_ref, dup_ref, wg_ref, wu_ref, r1_ref, dr2_ref, g1_ref, wo_ref, part_ref,
    dr1_ref, dat_ref, own_ref, away_ref, small_ref, acc_ref, da_ref, turn_ref, *, blocks,
):
    rows = r1_ref.shape[0]
    cols = own_ref.shape[0]
    side = info_ref[0]
    acc_ref[...] = dr2_ref[...]

    @pl.loop(0, wg_ref.shape[1] // WIDE)
    def _(step):
        here = at(step * WIDE, WIDE)
        acc_ref[...] += dot(dgt_ref[:, here], wg_ref[:, here], 1, 1) + dot(dup_ref[:, here], wu_ref[:, here], 1, 1)

    small_ref[...] = part_ref[...]

    @pl.loop(0, rows // ROWS, unroll=2)
    def _(index):
        here = at(index * ROWS, ROWS)
        dr1, dgain = norm_back(r1_ref[here, :], g1_ref[...], acc_ref[here, :])
        dr1_ref[here, :] = dr1
        da_ref[here, :] = dr1.astype(BF16)
        add_small(small_ref, 0, jnp.sum(dgain, axis=0, keepdims=True))

    away_ref[...] = dot(wo_ref[at((1 - side) * cols, cols), :], da_ref[...], 1, 1).astype(BF16)
    own_ref[...] = dot(wo_ref[at(side * cols, cols), :], da_ref[...], 1, 1).astype(BF16)
    turn_ref[...] = da_ref[...].T
    relative_rows(dat_ref, turn_ref, info_ref[1], blocks)


def norm_one(info, dgt, dup, wg, wu, r1, dr2, g1, w_out, part, blocks):
    rows, width = r1.shape
    ff = wg.shape[1]
    cols = w_out.shape[0] // 2
    return call(
        functools.partial(norm_one_kernel, blocks=blocks), "norm_one_back", (info,),
        (dgt, dup, wg, wu, r1, dr2, g1, w_out, part),
        [
            shape(F32, rows, width), shape(BF16, width, rows), shape(BF16, cols, rows),
            shape(BF16, cols, rows), shape(F32, 16, WIDE),
        ],
        4 * rows * width * ff,
        [pltpu.VMEM((rows, width), F32), pltpu.VMEM((rows, width), BF16), pltpu.VMEM((width, rows), BF16)],
    )


def out_grad_kernel(dat_ref, mine_ref, came_ref, keep_ref, away_ref):
    away_ref[...] = dot(dat_ref[...], came_ref[...], 1, 1).astype(BF16)
    keep_ref[...] = dot(dat_ref[...], mine_ref[...], 1, 1).astype(BF16)


def out_grad(dat, mine, came):
    width, rows = dat.shape
    cols = mine.shape[0]
    return call(
        out_grad_kernel, "out_grad", (), (dat, mine, came), [shape(BF16, width, cols)] * 2,
        4 * width * rows * cols,
    )


def project_grad_kernel(info_ref, x_ref, dq_ref, dk_ref, dv_ref, mine_ref, came_ref, *rest, orders, blocks):
    out_refs, (turn_ref, left_ref) = rest[:-2], rest[-2:]
    turn_ref[...] = x_ref[...].T
    relative_rows(left_ref, turn_ref, info_ref[1], blocks)
    left = left_ref[...]
    cols = dq_ref.shape[0]
    piece = cols // 3
    for index, grad_ref in enumerate((dq_ref, dk_ref, dv_ref)):
        lanes = slice(index * piece, (index + 1) * piece)
        pair = out_refs[2 * index : 2 * index + 2]
        main = [ref.at[:, 0:cols] for ref in pair]
        tail = [ref.at[:, cols : cols + piece] for ref in pair]
        split_store(dot(left, grad_ref[...], 1, 1), None, main, orders[index], blocks)
        both = mine_ref[:, lanes].astype(F32) + came_ref[:, lanes].astype(F32)
        split_store(both, None, tail, orders[index], blocks)


def project_grad(info, x, grads, mine, came, orders, blocks):
    rows, width = x.shape
    cols = grads[0].shape[0]
    wide = cols + cols // 3
    return call(
        functools.partial(project_grad_kernel, orders=orders, blocks=blocks), "project_grad", (info,),
        (x, *grads, mine, came), [shape(BF16, width // 2, wide)] * 6, 6 * rows * width * cols,
        [pltpu.VMEM((width, rows), BF16)] * 2,
    )


def stream_grad_kernel(info_ref, dq_ref, dk_ref, dv_ref, wq_ref, wk_ref, wv_ref, *rest):
    cols, pack = dq_ref.shape
    rows = pack // 2
    side = info_ref[0]
    mine = len(rest) == 3
    lanes = at((side if mine else 1 - side) * rows, rows)
    total = sum(
        dot(w_ref[...], g_ref[:, lanes], 1, 0)
        for w_ref, g_ref in ((wq_ref, dq_ref), (wk_ref, dk_ref), (wv_ref, dv_ref))
    )
    if mine:
        came_ref, dr1_ref, out_ref = rest
        total = total + came_ref[...].astype(F32)
        out_ref[...] = (dr1_ref[...] + total.T).astype(BF16)
    else:
        rest[0][...] = total.astype(BF16)


def stream_grad(info, grads, weights, *others):
    cols, pack = grads[0].shape
    width = weights[0].shape[0]
    rows = pack // 2
    out = (rows, width) if others else (width, rows)
    return call(
        stream_grad_kernel, "stream_grad", (info,), (*grads, *weights, *others), [shape(BF16, *out)],
        6 * rows * width * cols,
    )[0]


def finish_kernel(
    query_ref, key_ref, value_ref, high_ref, low_ref, came_ref,
    gq_ref, gk_ref, gv_ref, out_ref, one_ref, two_ref, rms_ref,
):
    rows, cols = gq_ref.shape
    lines = high_ref.shape[0]
    starts = (0, rows + 2 * lines, 2 * rows + 2 * lines)
    tails = []
    for keep_ref, start, to_ref in zip((query_ref, key_ref, value_ref), starts, (gq_ref, gk_ref, gv_ref)):
        total = keep_ref[...].astype(F32) + came_ref[start : start + rows, :].astype(F32)
        to_ref[...] = total[:, :cols]
        tails.append(total[:, cols:])
    out_ref[...] = jnp.concatenate(tails, axis=1)
    small = whole_of(high_ref[...], low_ref[...]) + whole_of(
        came_ref[rows : rows + lines, :], came_ref[rows + lines : rows + 2 * lines, :]
    )
    lanes = one_ref.shape[1]
    width = one_ref.shape[0] * lanes
    for number in range(one_ref.shape[0]):
        line, start = divmod(number * lanes, WIDE)
        for index, to_ref in enumerate((one_ref, two_ref)):
            to_ref[number : number + 1, :] = small[2 * index + line : 2 * index + line + 1, start : start + lanes]
    sums = jnp.sum(small[4:10], axis=1, keepdims=True)
    count = small[10:11, 0:1] * width
    for index in range(3):
        rms_ref[:, index : index + 1] = jnp.sqrt((sums[2 * index : 2 * index + 1] + sums[2 * index + 1 : 2 * index + 2]) / count)


def finish(parts, came, width, head_cols):
    rows = parts[0].keep.shape[0]
    return call(
        finish_kernel, "finish", (), (*[part.keep for part in parts], *parts[0].pair, came),
        [shape(F32, rows, head_cols)] * 4 + [shape(F32, width // 128, 128)] * 2 + [shape(F32, 1, 3)],
        1_000_000, room=4,
    )


def swap_seq(value):
    return lax.ppermute(value, "seq", [(0, 1), (1, 0)])


def swap_dp(value, bit):
    size = lax.axis_size("dp")
    return lax.ppermute(value, "dp", [(i, i ^ (1 << bit)) for i in range(size)])


def halves_of(small):
    high = lax.reduce_precision(small, 8, 7)
    return high.astype(BF16), (small - high).astype(BF16)


def whole_of(high, low):
    return high.astype(F32) + low.astype(F32)


class Halving:
    def __init__(self, keep, away, order, shift, small=None):
        self.keep, self.order, self.shift, self.small = keep, order, shift, small
        self.sent, self.step = away, 0

    def send(self):
        if self.small is not None:
            self.pair = halves_of(self.small)
            self.sent = jnp.concatenate([self.sent, *self.pair], axis=0)
        self.came = swap_dp(self.sent, self.order[self.step] + self.shift)
        self.step += 1

    def receive(self):
        rows = self.keep.shape[0]
        if self.small is not None:
            count = self.small.shape[0]
            came = self.came[rows : rows + count], self.came[rows + count :]
            self.small = whole_of(*self.pair) + whole_of(*came)
        if self.step < len(self.order):
            self.sent = self.add(rows // 2, rows)
            self.keep = self.add(0, rows // 2)
        else:
            self.keep = self.keep.astype(F32) + self.came[:rows].astype(F32)

    def add(self, low, high):
        return (self.keep[low:high].astype(F32) + self.came[low:high].astype(F32)).astype(BF16)

    def relay(self, *others):
        if others:
            self.keep = after(self.keep, *others)
        self.receive()
        self.send()

    @staticmethod
    def last(parts, done=False):
        for part in parts:
            part.receive()
            part.size = part.sent.shape[0]
        rows = [part.sent for part in parts]
        small = parts[0].small
        if small is not None:
            parts[0].pair = halves_of(small)
            rows[1:1] = parts[0].pair
        joint = jnp.concatenate(rows, axis=0)
        came = swap_dp(joint, parts[0].order[-1] + parts[0].shift)
        if done:
            return came
        start = 0
        for part in parts:
            end = start + part.size + (2 * small.shape[0] if part.small is not None else 0)
            part.came = came[start:end]
            start = end
            part.step += 1
            part.receive()
        return joint

    def rest(self):
        value = self.keep
        for bit in reversed(range(self.shift)):
            half = value.shape[0] // 2
            mine = (lax.axis_index("dp") >> bit) & 1
            keep = lax.dynamic_slice_in_dim(value, mine * half, half, 0)
            away = lax.dynamic_slice_in_dim(value, (1 - mine) * half, half, 0)
            value = keep + swap_dp(away.astype(BF16), bit).astype(F32)
            if self.small is not None:
                self.small = self.small + swap_dp(self.small, bit)
        return value


def after(values, *others):
    return lax.optimization_barrier((values, others))[0]


def shards(
    tokens,
    doc_lengths,
    w_query,
    w_key,
    w_value,
    w_out,
    w_gate,
    w_up,
    w_down,
    gain_attn,
    gain_ffn,
    cotangent,
):
    row_count, width = tokens.shape
    head_cols = w_query.shape[1] // lax.axis_size("seq")
    dp_size = lax.axis_size("dp")
    blocks = min(dp_size, 16)
    shift = (dp_size // blocks).bit_length() - 1
    orders = ((0, 2, 1, 3), (1, 0, 2, 3), (2, 3, 0, 1))
    turns = ((1, 2, 0, 3), (1, 0, 2, 3), (2, 1, 0, 3))
    lengths = doc_lengths[0]
    seq_index = lax.axis_index("seq")
    info = jnp.stack([seq_index, lax.axis_index("dp") >> shift]).astype(jnp.int32)
    gain_one, gain_two = gain_attn.reshape(1, width), gain_ffn.reshape(1, width)

    oth = swap_seq(tokens)
    *started, turned, own_q, own_k, own_v = project_own(info, doc_lengths, tokens, (w_query, w_key, w_value))
    query, key, value, gathered, context, mine, away, lse = attention_forward(
        info, lengths, started, oth, turned
    )
    kept = (query, key, value, context, lse)
    came = swap_seq(away)
    act, silu, slope, result, dm, dm_turned, hb_turned, dr2, r1, small = ffn_forward(
        info, lengths, tokens, mine, came, w_out, gain_one, gain_two, w_gate, w_up, w_down, cotangent, blocks
    )
    down_away = weight_grad(info, dm_turned, act, orders[2], blocks)
    down_came = swap_seq(down_away)
    dgt, dup, gate_away, up_away = swiglu_away(
        info, after(dm, down_away), w_down, silu, slope, hb_turned, orders[:2], blocks
    )
    gate_came, up_came = swap_seq(gate_away), swap_seq(up_away)
    down = Halving(
        *weight_grad(info, dm_turned, after(act, gate_away), orders[2], blocks, down_came), orders[2], shift
    )
    down.send()
    dgt, dup = swiglu_mine(info, after(dm, down.sent), w_down, silu, slope, dgt, dup)
    gate = Halving(*weight_grad(info, hb_turned, dgt, orders[0], blocks, gate_came), orders[0], shift)
    gate.send()
    dr1, da_turned, own_rows, away_rows, small = norm_one(
        info, after(dgt, gate.sent), dup, w_gate, w_up, r1, dr2, gain_one, w_out, small, blocks
    )
    came_rows = swap_seq(away_rows)
    up = Halving(
        *weight_grad(info, after(hb_turned, away_rows), dup, orders[1], blocks, up_came), orders[1], shift
    )
    up.send()
    out_keep, out_away = out_grad(after(da_turned, up.sent), mine, came)
    out_came = swap_seq(out_away)
    small = small + swap_seq(small)
    grads = ()
    each = head_cols // HDIM // len(PLAN)
    ffn = [down, gate, up]
    for number, relays in enumerate(PLAN):
        for part in relays:
            ffn[part].relay(*grads)
        own_rows = after(own_rows, out_away, *[ffn[part].sent for part in relays], *grads)
        grads = attention_backward(
            info, lengths, kept, own_rows, came_rows, number * each, each, grads
        )
    sides = project_grad(info, gathered, grads, out_keep, out_came, turns, blocks)
    attn = [
        Halving(sides[2 * index], sides[2 * index + 1], turns[index], shift, None if index else small)
        for index in range(3)
    ]
    up.relay(*sides)
    query_part, key_part, value_part = attn
    key_part.send()
    value_part.send()
    weights = (own_q, own_k, own_v)
    stream_away = stream_grad(info, after(grads, *sides, up.sent), weights)
    stream_came = swap_seq(stream_away)
    gate.relay(stream_away)
    down.relay(stream_away)
    query_part.sent = after(query_part.sent, gate.sent, down.sent, key_part.came)
    query_part.send()
    grad_tokens = stream_grad(info, after(grads, key_part.came), weights, stream_came, dr1)
    up.relay(grad_tokens)
    key_part.relay(up.sent)
    value_part.relay(up.sent)
    joint = Halving.last([gate, up])
    down.relay(joint)
    query_part.relay(joint)
    for part in (key_part, value_part, query_part):
        part.relay(joint)
    down.receive()
    summed_down, summed_gate, summed_up = (part.rest() for part in ffn)
    summed_down = summed_down.T
    if shift:
        Halving.last(attn)
        sums = [part.rest() for part in attn]
        attn_grads = [total[:, :head_cols] for total in sums]
        attn_grads.append(jnp.concatenate([total[:, head_cols:] for total in sums], axis=1).T)
        small = attn[0].small.reshape(8, 2 * WIDE)[:, :width]
        grad_one, grad_two = small[0], small[1]
        rms_values = jnp.sqrt(jnp.sum(small[2:5], axis=1) / (small[5, 0] * width))
    else:
        came = after(Halving.last(attn, True), summed_down, summed_gate, summed_up, grad_tokens)
        *attn_grads, grad_wo, grad_one, grad_two, rms_values = finish(attn, came, width, head_cols)
        attn_grads.append(grad_wo.T)
    return (
        result,
        grad_tokens,
        *attn_grads,
        summed_gate,
        summed_up,
        summed_down,
        grad_one.reshape(-1),
        grad_two.reshape(-1),
        rms_values.reshape(-1),
    )


def solution(mesh):
    return jax.shard_map(
        shards,
        mesh=mesh,
        in_specs=(
            P(("dp", "seq"), None),
            P("dp", None),
            P(),
            P(),
            P(),
            P(),
            P(),
            P(),
            P(),
            P(),
            P(),
            P(("dp", "seq"), None),
        ),
        out_specs=(
            P(("dp", "seq"), None),
            P(("dp", "seq"), None),
            P("dp", "seq"),
            P("dp", "seq"),
            P("dp", "seq"),
            P("seq", "dp"),
            P("dp", "seq"),
            P("dp", "seq"),
            P("seq", "dp"),
            P(),
            P(),
            P(),
        ),
        check_vma=False,
    )
```

```python
import functools
import math

import jax
import jax.numpy as jnp
import numpy as np
from jax import lax
from jax.experimental import pallas as pl
from jax.experimental.pallas import tpu as pltpu
from jax.sharding import PartitionSpec as P

HDIM = 48
HALF = HDIM // 2
SCORE = 1.0 / math.sqrt(HDIM)
LOG2E = 1.0 / math.log(2.0)
NEG = -1e30
BF16 = jnp.bfloat16
F32 = jnp.float32
CHUNK = 256
WIDE = 512
ROWS = 64
SPANS = 4
PAIR = 2
PLAN = ((), (0, 1))
MIB = 1 << 20
EASE = 50
ROOM = 8


def call(kernel, name, scalars, arrays, out_shape, flops, scratch=(), room=16, aliases=None):
    moved = sum(math.prod(o.shape) * o.dtype.itemsize for o in out_shape)
    return pl.pallas_call(
        kernel,
        in_specs=[pl.BlockSpec(memory_space=pltpu.SMEM)] * len(scalars)
        + [pl.BlockSpec(memory_space=pltpu.VMEM)] * len(arrays),
        out_specs=[pl.BlockSpec(memory_space=pltpu.VMEM)] * len(out_shape),
        out_shape=out_shape,
        scratch_shapes=list(scratch),
        input_output_aliases=aliases or {},
        cost_estimate=pl.CostEstimate(flops=flops // EASE, bytes_accessed=moved // EASE, transcendentals=0),
        compiler_params=pltpu.CompilerParams(vmem_limit_bytes=room * MIB),
        name=name,
    )(*scalars, *arrays)


def shape(dtype, *dims):
    return jax.ShapeDtypeStruct(dims, dtype)


def at(start, size):
    return pl.ds(pl.multiple_of(start, size), size)


def dot(a, b, ca, cb):
    return lax.dot_general(a, b, (((ca,), (cb,)), ((), ())), preferred_element_type=F32)


def rope_tables(span):
    freq = 10000.0 ** (-np.arange(HALF, dtype=np.float64) / HALF)
    phase = freq[:, None] * np.arange(span, dtype=np.float64)[None, :]
    return np.cos(phase).astype(np.float32), np.sin(phase).astype(np.float32)


def block_facts(len_ref, block):
    ends = []
    total = 0
    for index in range(len_ref.shape[0]):
        total = total + len_ref[index]
        ends.append(total)
    segments, openings = [], []
    for number in range(SPANS):
        segment = 0
        opening = 0
        for index, end in enumerate(ends):
            done = number * block >= end
            segment = segment + done.astype(jnp.int32)
            opening = opening + jnp.where(done, len_ref[index], 0)
        segments.append(segment)
        openings.append(opening)
    return segments, openings


def causal(block):
    key = lax.broadcasted_iota(jnp.int32, (block, block), 0)
    return key <= lax.broadcasted_iota(jnp.int32, (block, block), 1)


def project(to_refs, weights, x, openings, cos_ref, sin_ref, start):
    rows = x.shape[0]
    cols, pack = to_refs[0].shape
    block = pack // SPANS
    for weight, to_ref, scale in zip(weights, to_refs, (SCORE * LOG2E, 1.0, None)):
        for number in range(rows // block):
            part = dot(weight, x[number * block : (number + 1) * block], 1, 1)
            first = start + number * block
            if scale is None:
                to_ref[:, at(first, block)] = part.astype(BF16)
                continue
            opening = functools.reduce(
                lambda rest, span: jnp.where(first == span * block, openings[span], rest), range(SPANS), 0
            )
            here = at(first - opening, block)
            cos = cos_ref[:, here] * scale
            sin = sin_ref[:, here] * scale
            for head in range(cols // HDIM):
                a = part[head * HDIM : head * HDIM + HALF]
                b = part[head * HDIM + HALF : (head + 1) * HDIM]
                turned = jnp.concatenate([a * cos - b * sin, b * cos + a * sin], axis=0)
                to_ref[head * HDIM : (head + 1) * HDIM, at(first, block)] = turned.astype(BF16)


def project_own_kernel(
    info_ref, from_len_ref, from_x_ref, from_cos_ref, from_sin_ref, wq_ref, wk_ref, wv_ref,
    q_ref, k_ref, v_ref, all_ref, turned_ref, cq_ref, ck_ref, cv_ref,
    len_ref, x_ref, cos_ref, sin_ref, sems,
):
    cols, pack = q_ref.shape
    rows = x_ref.shape[0]
    side = info_ref[0]
    pairs = [(from_x_ref, x_ref)]
    pairs += [
        (w_ref.at[:, at(side * cols, cols)], c_ref)
        for w_ref, c_ref in ((wq_ref, cq_ref), (wk_ref, ck_ref), (wv_ref, cv_ref))
    ]
    pairs += [(from_cos_ref, cos_ref), (from_sin_ref, sin_ref), (from_len_ref, len_ref)]
    copies = [pltpu.make_async_copy(*pair, sems.at[index]) for index, pair in enumerate(pairs)]
    for copy in copies:
        copy.start()
    for index, c_ref in enumerate((cq_ref, ck_ref, cv_ref)):
        copies[1 + index].wait()
        turned_ref[index * cols : (index + 1) * cols, :] = c_ref[...].T
    for index in (0, 4, 5, 6):
        copies[index].wait()
    _, openings = block_facts(len_ref.at[0], pack // SPANS)
    all_ref[at(side * rows, rows), :] = x_ref[...]
    weights = [turned_ref[index * cols : (index + 1) * cols, :] for index in range(3)]
    project((q_ref, k_ref, v_ref), weights, x_ref[...], openings, cos_ref, sin_ref, side * rows)


def project_own(info, lengths, own, weights):
    rows, width = own.shape
    pack = 2 * rows
    cols = weights[0].shape[1] // 2
    vmem = pl.BlockSpec(memory_space=pltpu.VMEM)
    far = [pltpu.with_memory_space_constraint(jnp.asarray(value), pltpu.HBM) for value in (lengths, own, *rope_tables(pack), *weights)]
    return pl.pallas_call(
        project_own_kernel,
        in_specs=[pl.BlockSpec(memory_space=pltpu.SMEM)] + [pl.BlockSpec(memory_space=pltpu.HBM)] * 7,
        out_specs=[vmem] * 8,
        out_shape=[shape(BF16, cols, pack)] * 3
        + [shape(BF16, pack, width), shape(BF16, 3 * cols, width)]
        + [shape(BF16, width, cols)] * 3,
        scratch_shapes=[
            pltpu.SMEM(lengths.shape, jnp.int32), pltpu.VMEM(own.shape, BF16),
            pltpu.VMEM((HALF, pack), F32), pltpu.VMEM((HALF, pack), F32), pltpu.SemaphoreType.DMA((7,)),
        ],
        cost_estimate=pl.CostEstimate(flops=4_000_000_000, bytes_accessed=8_000_000, transcendentals=0),
        compiler_params=pltpu.CompilerParams(vmem_limit_bytes=8 * MIB),
        name="project_own",
    )(info, *far)


def attention_forward_kernel(
    info_ref, len_ref, _, __, ___, ____, oth_ref, turned_ref, cos_ref, sin_ref,
    q_ref, k_ref, v_ref, x_ref, ctx_ref, mine_ref, away_ref, lse_ref,
):
    rows = oth_ref.shape[0]
    cols, pack = q_ref.shape
    heads = cols // HDIM
    block = pack // SPANS
    segments, openings = block_facts(len_ref, block)
    side = info_ref[0]
    x_ref[at((1 - side) * rows, rows), :] = oth_ref[...]
    weights = [turned_ref[index * cols : (index + 1) * cols, :] for index in range(3)]
    project((q_ref, k_ref, v_ref), weights, oth_ref[...], openings, cos_ref, sin_ref, (1 - side) * rows)
    below = causal(block)

    spans = [slice(number * block, (number + 1) * block) for number in range(SPANS)]

    @pl.loop(0, heads // PAIR)
    def _(group):
        units = [(group * PAIR + number, i) for number in range(PAIR) for i in range(SPANS)]
        keys = [k_ref[at(head * HDIM, HDIM), :].T for head, i in units if i == 0]
        raw, done = {}, {}

        def scores(step):
            head, i = units[step]
            query = q_ref[at(head * HDIM, HDIM), spans[i]]
            raw[step] = [dot(keys[step // SPANS][spans[j]], query, 1, 0) for j in range(i + 1)]

        def softmax(step):
            head, i = units[step]
            parts = raw.pop(step)
            parts[i] = jnp.where(below, parts[i], NEG)
            biases = [jnp.where(segments[i] == segments[j], 0.0, NEG) for j in range(i)] + [0.0]
            top = functools.reduce(
                jnp.maximum, [jnp.max(part, axis=0, keepdims=True) + bias for part, bias in zip(parts, biases)]
            )
            probs = [jnp.exp2(part - (top - bias)) for part, bias in zip(parts, biases)]
            total = sum(jnp.sum(prob, axis=0, keepdims=True) for prob in probs)
            lse_ref[head, :, spans[i]] = top + jnp.log2(total)
            done[step] = [prob.astype(BF16) for prob in probs], 1.0 / total

        def context(step):
            head, i = units[step]
            here = at(head * HDIM, HDIM)
            probs, scale = done.pop(step)
            total = sum(dot(v_ref[here, spans[j]], prob, 1, 0) for j, prob in enumerate(probs))
            ctx_ref[here, spans[i]] = (total * scale).astype(BF16)

        for step in range(len(units) + 2):
            if step < len(units):
                scores(step)
            if 0 <= step - 1 < len(units):
                softmax(step - 1)
            if 0 <= step - 2:
                context(step - 2)
        here = at(group * PAIR * HDIM, PAIR * HDIM)
        mine_ref[here, :] = ctx_ref[here, at(side * rows, rows)]
        away_ref[here, :] = ctx_ref[here, at((1 - side) * rows, rows)]


def attention_forward(info, lengths, started, oth, turned):
    rows, width = oth.shape
    cols, pack = started[0].shape
    heads = cols // HDIM
    half = shape(BF16, cols, rows)
    return call(
        attention_forward_kernel, "attention_forward", (info, lengths),
        (*started, oth, turned, *rope_tables(pack)),
        [shape(BF16, cols, pack)] * 3 + [shape(BF16, pack, width), shape(BF16, cols, pack)]
        + [half, half, shape(F32, heads, 1, pack)],
        15_000_000_000, room=24,
        aliases={2 + index: index for index in range(4)},
    )


def attention_backward_kernel(
    info_ref, len_ref, q_ref, k_ref, v_ref, ctx_ref, own_ref, oth_ref, lse_ref, cos_ref, sin_ref, *rest,
    first, heads,
):
    dq_ref, dk_ref, dv_ref, dctx_ref = rest[-4:]
    rows = own_ref.shape[1]
    pack = q_ref.shape[1]
    block = pack // SPANS
    segments, openings = block_facts(len_ref, block)
    side = info_ref[0]
    below = causal(block)
    spans = [slice(number * block, (number + 1) * block) for number in range(SPANS)]

    def unturn(value, number, scale):
        here = at(number * block - openings[number], block)
        cos = cos_ref[:, here] * scale
        sin = sin_ref[:, here] * scale
        a, b = value[:HALF], value[HALF:]
        return jnp.concatenate([a * cos + b * sin, b * cos - a * sin], axis=0).astype(BF16)

    def plus(sums, index, value):
        sums[index] = sums[index] + value if index in sums else value

    @pl.loop(first, first + heads)
    def _(head):
        here = at(head * HDIM, HDIM)
        dctx_ref[:, at(side * rows, rows)] = own_ref[here, :]
        dctx_ref[:, at((1 - side) * rows, rows)] = oth_ref[here, :]
        key = k_ref[here, :]
        keys = key.T
        values = v_ref[here, :].T
        delta = jnp.sum(dctx_ref[...].astype(F32) * ctx_ref[here, :].astype(F32), axis=0, keepdims=True)
        lse = lse_ref[head, :, :]
        raw, done, dqs, dks, dvs = {}, {}, {}, {}, {}

        def scores(i, j):
            return (
                dot(keys[spans[j]], q_ref[here, spans[i]], 1, 0),
                dot(values[spans[j]], dctx_ref[:, spans[i]], 1, 0),
            )

        def slopes(i, j, score, slope):
            top = lse[:, spans[i]]
            if j == i:
                prob = jnp.exp2(jnp.where(below, score, NEG) - top)
            else:
                prob = jnp.exp2(score - (top - jnp.where(segments[i] == segments[j], 0.0, NEG)))
            return prob.astype(BF16), (prob * (slope - delta[:, spans[i]])).astype(BF16)

        def products(i, j, prob, dscore):
            plus(dqs, i, dot(key[:, spans[j]], dscore, 1, 0))
            plus(dks, j, dot(q_ref[here, spans[i]], dscore, 1, 1))
            plus(dvs, j, dot(dctx_ref[:, spans[i]], prob, 1, 1))

        pairs = [(i, j) for i in range(SPANS) for j in range(i + 1)]
        for step in range(len(pairs) + 2):
            if step < len(pairs):
                raw[step] = scores(*pairs[step])
            if 0 <= step - 1 < len(pairs):
                done[step - 1] = slopes(*pairs[step - 1], *raw.pop(step - 1))
            if 0 <= step - 2:
                products(*pairs[step - 2], *done.pop(step - 2))
        for number, lanes in enumerate(spans):
            dq_ref[here, lanes] = unturn(dqs[number], number, SCORE)
            dk_ref[here, lanes] = unturn(dks[number], number, 1.0 / LOG2E)
            dv_ref[here, lanes] = dvs[number].astype(BF16)


def attention_backward(info, lengths, kept, own, oth, first, heads, sofar):
    query, key, value, context, lse = kept
    cols, pack = query.shape
    arrays = (query, key, value, context, own, oth, lse, *rope_tables(pack), *sofar)
    base = 2 + len(arrays) - len(sofar)
    return call(
        functools.partial(attention_backward_kernel, first=first, heads=heads),
        "attention_backward", (info, lengths), arrays, [shape(BF16, cols, pack)] * 3,
        heads * 3_000_000_000,
        [pltpu.VMEM((HDIM, pack), BF16)],
        aliases={base + index: index for index in range(len(sofar))},
    )


def inverse_rms(value):
    return lax.rsqrt(jnp.mean(value * value, axis=-1, keepdims=True) + 1e-06)


def norm_back(value, gain, grad):
    inv = inverse_rms(value)
    scaled = grad * gain
    slope = jnp.mean(scaled * value, axis=-1, keepdims=True) * (inv * inv * inv)
    return scaled * inv - value * slope, grad * value * inv


def relative_rows(to_ref, from_ref, place, blocks):
    size = from_ref.shape[0] // blocks
    for block in range(blocks):
        to_ref[block * size : (block + 1) * size, :] = from_ref[at((block ^ place) * size, size), :]


def position(block, order):
    last = len(order) - 1
    return sum(((block >> bit) & 1) << (last - step) for step, bit in enumerate(order))


def ffn_forward_kernel(
    info_ref, len_ref, x_ref, mine_ref, came_ref, wo_ref, g1_ref, g2_ref, wg_ref, wu_ref, wd_ref, cot_ref,
    act_ref, s_ref, t_ref, out_ref, dm_ref, dmt_ref, hbt_ref, dr2_ref, r1_ref, small_ref,
    hb_ref, h_ref, m_ref, turn_ref, *, blocks,
):
    rows, width = x_ref.shape
    part = mine_ref.shape[0]
    total = len_ref[0] + len_ref[1] + len_ref[2] + len_ref[3]
    side = info_ref[0]
    first = side * rows

    def valid_of(start):
        places = lax.broadcasted_iota(jnp.int32, (ROWS, 1), 0) + (start + first)
        return (places < total).astype(F32)

    def squares(row, value, valid):
        add_small(small_ref, row, jnp.sum(value * value * valid, axis=0, keepdims=True))

    small_ref[...] = jnp.zeros_like(small_ref)
    m_ref[...] = dot(mine_ref[...].T, wo_ref[at(side * part, part), :], 1, 0) + dot(
        came_ref[...].T, wo_ref[at((1 - side) * part, part), :], 1, 0
    )

    @pl.loop(0, rows // ROWS, unroll=2)
    def _(index):
        here = at(index * ROWS, ROWS)
        valid = valid_of(index * ROWS)
        x = x_ref[here, :].astype(F32)
        a = m_ref[here, :]
        r1 = x + a
        h = r1 * inverse_rms(r1) * g1_ref[...]
        r1_ref[here, :] = r1
        h_ref[here, :] = h
        hb_ref[here, :] = h.astype(BF16)
        squares(2, x, valid)
        squares(3, a, valid)

    turn_ref[...] = hb_ref[...].T
    relative_rows(hbt_ref, turn_ref, info_ref[1], blocks)

    def inputs(step):
        cols = slice(step * CHUNK, (step + 1) * CHUNK)
        return dot(hb_ref[...], wg_ref[:, cols], 1, 0), dot(hb_ref[...], wu_ref[:, cols], 1, 0)

    count = act_ref.shape[1] // CHUNK
    ready = inputs(0)
    for step in range(count):
        gate, up = ready
        ready = inputs(step + 1) if step + 1 < count else None
        cols = slice(step * CHUNK, (step + 1) * CHUNK)
        sig = 1.0 / (1.0 + jnp.exp(-gate))
        silu = gate * sig
        act_ref[:, cols] = (silu * up).astype(BF16)
        s_ref[:, cols] = silu.astype(BF16)
        t_ref[:, cols] = (up * (sig + silu * (1.0 - sig))).astype(BF16)
    m_ref[...] = dot(act_ref[...], wd_ref[...], 1, 0)

    @pl.loop(0, rows // ROWS, unroll=2)
    def _(index):
        here = at(index * ROWS, ROWS)
        valid = valid_of(index * ROWS)
        m = m_ref[here, :]
        r2 = h_ref[here, :] + m
        gain = g2_ref[...]
        dr2, dgain = norm_back(r2, gain, cot_ref[here, :].astype(F32) * valid)
        out_ref[here, :] = (r2 * inverse_rms(r2) * gain).astype(BF16)
        dr2_ref[here, :] = dr2
        dm_ref[here, :] = dr2.astype(BF16)
        add_small(small_ref, 1, jnp.sum(dgain, axis=0, keepdims=True))
        squares(4, m, valid)

    add_small(small_ref, 5, jnp.full((1, width), jnp.clip(total - first, 0, rows).astype(F32)))
    turn_ref[...] = dm_ref[...].T
    relative_rows(dmt_ref, turn_ref, info_ref[1], blocks)


def ffn_forward(info, lengths, x, mine, came, w_out, g1, g2, wg, wu, wd, cot, blocks):
    rows, width = x.shape
    ff = wg.shape[1]
    return call(
        functools.partial(ffn_forward_kernel, blocks=blocks), "ffn_forward", (info, lengths),
        (x, mine, came, w_out, g1, g2, wg, wu, wd, cot),
        [shape(BF16, rows, ff)] * 3 + [shape(BF16, rows, width)] * 2 + [shape(BF16, width, rows)] * 2
        + [shape(F32, rows, width)] * 2 + [shape(F32, 16, WIDE)],
        6 * rows * width * ff,
        [
            pltpu.VMEM((rows, width), BF16), pltpu.VMEM((rows, width), F32),
            pltpu.VMEM((rows, width), F32), pltpu.VMEM((width, rows), BF16),
        ],
    )


def add_small(small_ref, row, value):
    for piece in range(-(-value.shape[1] // WIDE)):
        part = value[:, piece * WIDE : (piece + 1) * WIDE]
        small_ref[2 * row + piece : 2 * row + piece + 1, 0 : part.shape[1]] += part


def split_store(product, came, to_refs, order, blocks):
    size = product.shape[0] // blocks
    for block in range(blocks):
        place = position(block, order)
        rows = product[block * size : (block + 1) * size]
        if came is not None:
            rows = rows + came[place * size : (place + 1) * size].astype(F32)
        half = blocks // len(to_refs)
        start = (place % half) * size
        to_refs[place // half][start : start + size, :] = rows.astype(BF16)


def weight_kernel(info_ref, left_ref, right_ref, *rest, order, blocks):
    side = info_ref[0]
    mine = len(rest) == 3
    to_refs = rest[-2:] if mine else rest
    cols = to_refs[0].shape[1]
    start = (side if mine else 1 - side) * cols

    @pl.loop(0, cols // CHUNK, unroll=True)
    def _(step):
        here = at(step * CHUNK, CHUNK)
        right = right_ref[:, at(start + step * CHUNK, CHUNK)]
        came = rest[0][:, here] if mine else None
        split_store(dot(left_ref[...], right, 1, 0), came, [ref.at[:, here] for ref in to_refs], order, blocks)


def weight_grad(info, left, right, order, blocks, came=None):
    width, rows = left.shape
    cols = right.shape[1] // 2
    kernel = functools.partial(weight_kernel, order=order, blocks=blocks)
    flops = 2 * width * rows * cols
    if came is None:
        return call(kernel, "weight_away", (info,), (left, right), [shape(BF16, width, cols)], flops, room=ROOM)[0]
    return call(
        kernel, "weight_mine", (info,), (left, right, came), [shape(BF16, width // 2, cols)] * 2, flops, room=ROOM
    )


def swiglu_away_kernel(
    info_ref, dm_ref, wd_ref, s_ref, t_ref, hbt_ref, dgt_ref, dup_ref, gate_ref, up_ref, *, orders, blocks
):
    half = gate_ref.shape[1]
    count = half // CHUNK

    def grads(step):
        return swiglu_grads(
            (1 - info_ref[0]) * half + step * CHUNK, dm_ref, wd_ref, s_ref, t_ref, dgt_ref, dup_ref
        )

    ready = grads(0)
    for step in range(count):
        dgt, dup = ready
        ready = grads(step + 1) if step + 1 < count else None
        here = slice(step * CHUNK, (step + 1) * CHUNK)
        split_store(dot(hbt_ref[...], dgt, 1, 0), None, [gate_ref.at[:, here]], orders[0], blocks)
        split_store(dot(hbt_ref[...], dup, 1, 0), None, [up_ref.at[:, here]], orders[1], blocks)


def swiglu_grads(start, dm_ref, wd_ref, s_ref, t_ref, dgt_ref, dup_ref):
    cols = at(start, CHUNK)
    grad = dot(dm_ref[...], wd_ref[cols, :], 1, 1)
    dup = (grad * s_ref[:, cols].astype(F32)).astype(BF16)
    dgt = (grad * t_ref[:, cols].astype(F32)).astype(BF16)
    dup_ref[:, cols] = dup
    dgt_ref[:, cols] = dgt
    return dgt, dup


def swiglu_mine_kernel(info_ref, dm_ref, wd_ref, s_ref, t_ref, _, __, dgt_ref, dup_ref):
    half = s_ref.shape[1] // 2

    @pl.loop(0, half // CHUNK, unroll=True)
    def _(step):
        swiglu_grads(info_ref[0] * half + step * CHUNK, dm_ref, wd_ref, s_ref, t_ref, dgt_ref, dup_ref)


def swiglu_away(info, dm, wd, s, t, hbt, orders, blocks):
    rows, width = dm.shape
    ff = wd.shape[0]
    return call(
        functools.partial(swiglu_away_kernel, orders=orders, blocks=blocks), "swiglu_away", (info,),
        (dm, wd, s, t, hbt),
        [shape(BF16, rows, ff)] * 2 + [shape(BF16, width, ff // 2)] * 2,
        3 * rows * width * ff, room=ROOM,
    )


def swiglu_mine(info, dm, wd, s, t, dgt, dup):
    return call(
        swiglu_mine_kernel, "swiglu_mine", (info,), (dm, wd, s, t, dgt, dup), [shape(BF16, *dgt.shape)] * 2,
        dm.shape[0] * dm.shape[1] * wd.shape[0], aliases={5: 0, 6: 1},
    )


def norm_one_kernel(
    info_ref, dgt_ref, dup_ref, wg_ref, wu_ref, r1_ref, dr2_ref, g1_ref, wo_ref, part_ref,
    dr1_ref, dat_ref, own_ref, away_ref, small_ref, acc_ref, da_ref, turn_ref, *, blocks,
):
    rows = r1_ref.shape[0]
    cols = own_ref.shape[0]
    side = info_ref[0]
    acc_ref[...] = dr2_ref[...]

    @pl.loop(0, wg_ref.shape[1] // WIDE)
    def _(step):
        here = at(step * WIDE, WIDE)
        acc_ref[...] += dot(dgt_ref[:, here], wg_ref[:, here], 1, 1) + dot(dup_ref[:, here], wu_ref[:, here], 1, 1)

    small_ref[...] = part_ref[...]

    @pl.loop(0, rows // ROWS, unroll=2)
    def _(index):
        here = at(index * ROWS, ROWS)
        dr1, dgain = norm_back(r1_ref[here, :], g1_ref[...], acc_ref[here, :])
        dr1_ref[here, :] = dr1
        da_ref[here, :] = dr1.astype(BF16)
        add_small(small_ref, 0, jnp.sum(dgain, axis=0, keepdims=True))

    away_ref[...] = dot(wo_ref[at((1 - side) * cols, cols), :], da_ref[...], 1, 1).astype(BF16)
    own_ref[...] = dot(wo_ref[at(side * cols, cols), :], da_ref[...], 1, 1).astype(BF16)
    turn_ref[...] = da_ref[...].T
    relative_rows(dat_ref, turn_ref, info_ref[1], blocks)


def norm_one(info, dgt, dup, wg, wu, r1, dr2, g1, w_out, part, blocks):
    rows, width = r1.shape
    ff = wg.shape[1]
    cols = w_out.shape[0] // 2
    return call(
        functools.partial(norm_one_kernel, blocks=blocks), "norm_one_back", (info,),
        (dgt, dup, wg, wu, r1, dr2, g1, w_out, part),
        [
            shape(F32, rows, width), shape(BF16, width, rows), shape(BF16, cols, rows),
            shape(BF16, cols, rows), shape(F32, 16, WIDE),
        ],
        4 * rows * width * ff,
        [pltpu.VMEM((rows, width), F32), pltpu.VMEM((rows, width), BF16), pltpu.VMEM((width, rows), BF16)],
    )


def out_grad_kernel(dat_ref, mine_ref, came_ref, keep_ref, away_ref):
    away_ref[...] = dot(dat_ref[...], came_ref[...], 1, 1).astype(BF16)
    keep_ref[...] = dot(dat_ref[...], mine_ref[...], 1, 1).astype(BF16)


def out_grad(dat, mine, came):
    width, rows = dat.shape
    cols = mine.shape[0]
    return call(
        out_grad_kernel, "out_grad", (), (dat, mine, came), [shape(BF16, width, cols)] * 2,
        4 * width * rows * cols,
    )


def project_grad_kernel(info_ref, x_ref, dq_ref, dk_ref, dv_ref, mine_ref, came_ref, *rest, orders, blocks):
    out_refs, (turn_ref, left_ref) = rest[:-2], rest[-2:]
    turn_ref[...] = x_ref[...].T
    relative_rows(left_ref, turn_ref, info_ref[1], blocks)
    left = left_ref[...]
    cols = dq_ref.shape[0]
    piece = cols // 3
    for index, grad_ref in enumerate((dq_ref, dk_ref, dv_ref)):
        lanes = slice(index * piece, (index + 1) * piece)
        pair = out_refs[2 * index : 2 * index + 2]
        main = [ref.at[:, 0:cols] for ref in pair]
        tail = [ref.at[:, cols : cols + piece] for ref in pair]
        split_store(dot(left, grad_ref[...], 1, 1), None, main, orders[index], blocks)
        both = mine_ref[:, lanes].astype(F32) + came_ref[:, lanes].astype(F32)
        split_store(both, None, tail, orders[index], blocks)


def project_grad(info, x, grads, mine, came, orders, blocks):
    rows, width = x.shape
    cols = grads[0].shape[0]
    wide = cols + cols // 3
    return call(
        functools.partial(project_grad_kernel, orders=orders, blocks=blocks), "project_grad", (info,),
        (x, *grads, mine, came), [shape(BF16, width // 2, wide)] * 6, 6 * rows * width * cols,
        [pltpu.VMEM((width, rows), BF16)] * 2,
    )


def stream_grad_kernel(info_ref, dq_ref, dk_ref, dv_ref, wq_ref, wk_ref, wv_ref, *rest):
    cols, pack = dq_ref.shape
    rows = pack // 2
    side = info_ref[0]
    mine = len(rest) == 3
    lanes = at((side if mine else 1 - side) * rows, rows)
    total = sum(
        dot(w_ref[...], g_ref[:, lanes], 1, 0)
        for w_ref, g_ref in ((wq_ref, dq_ref), (wk_ref, dk_ref), (wv_ref, dv_ref))
    )
    if mine:
        came_ref, dr1_ref, out_ref = rest
        total = total + came_ref[...].astype(F32)
        out_ref[...] = (dr1_ref[...] + total.T).astype(BF16)
    else:
        rest[0][...] = total.astype(BF16)


def stream_grad(info, grads, weights, *others):
    cols, pack = grads[0].shape
    width = weights[0].shape[0]
    rows = pack // 2
    out = (rows, width) if others else (width, rows)
    return call(
        stream_grad_kernel, "stream_grad", (info,), (*grads, *weights, *others), [shape(BF16, *out)],
        6 * rows * width * cols,
    )[0]


def finish_kernel(
    query_ref, key_ref, value_ref, high_ref, low_ref, came_ref,
    gq_ref, gk_ref, gv_ref, out_ref, one_ref, two_ref, rms_ref,
):
    rows, cols = gq_ref.shape
    lines = high_ref.shape[0]
    starts = (0, rows + 2 * lines, 2 * rows + 2 * lines)
    tails = []
    for keep_ref, start, to_ref in zip((query_ref, key_ref, value_ref), starts, (gq_ref, gk_ref, gv_ref)):
        total = keep_ref[...].astype(F32) + came_ref[start : start + rows, :].astype(F32)
        to_ref[...] = total[:, :cols]
        tails.append(total[:, cols:])
    out_ref[...] = jnp.concatenate(tails, axis=1)
    small = whole_of(high_ref[...], low_ref[...]) + whole_of(
        came_ref[rows : rows + lines, :], came_ref[rows + lines : rows + 2 * lines, :]
    )
    lanes = one_ref.shape[1]
    width = one_ref.shape[0] * lanes
    for number in range(one_ref.shape[0]):
        line, start = divmod(number * lanes, WIDE)
        for index, to_ref in enumerate((one_ref, two_ref)):
            to_ref[number : number + 1, :] = small[2 * index + line : 2 * index + line + 1, start : start + lanes]
    sums = jnp.sum(small[4:10], axis=1, keepdims=True)
    count = small[10:11, 0:1] * width
    for index in range(3):
        rms_ref[:, index : index + 1] = jnp.sqrt((sums[2 * index : 2 * index + 1] + sums[2 * index + 1 : 2 * index + 2]) / count)


def finish(parts, came, width, head_cols):
    rows = parts[0].keep.shape[0]
    return call(
        finish_kernel, "finish", (), (*[part.keep for part in parts], *parts[0].pair, came),
        [shape(F32, rows, head_cols)] * 4 + [shape(F32, width // 128, 128)] * 2 + [shape(F32, 1, 3)],
        1_000_000, room=4,
    )


def swap_seq(value):
    return lax.ppermute(value, "seq", [(0, 1), (1, 0)])


def swap_dp(value, bit):
    size = lax.axis_size("dp")
    return lax.ppermute(value, "dp", [(i, i ^ (1 << bit)) for i in range(size)])


def halves_of(small):
    high = lax.reduce_precision(small, 8, 7)
    return high.astype(BF16), (small - high).astype(BF16)


def whole_of(high, low):
    return high.astype(F32) + low.astype(F32)


class Halving:
    def __init__(self, keep, away, order, shift, small=None):
        self.keep, self.order, self.shift, self.small = keep, order, shift, small
        self.sent, self.step = away, 0

    def send(self):
        if self.small is not None:
            self.pair = halves_of(self.small)
            self.sent = jnp.concatenate([self.sent, *self.pair], axis=0)
        self.came = swap_dp(self.sent, self.order[self.step] + self.shift)
        self.step += 1

    def receive(self):
        rows = self.keep.shape[0]
        if self.small is not None:
            count = self.small.shape[0]
            came = self.came[rows : rows + count], self.came[rows + count :]
            self.small = whole_of(*self.pair) + whole_of(*came)
        if self.step < len(self.order):
            self.sent = self.add(rows // 2, rows)
            self.keep = self.add(0, rows // 2)
        else:
            self.keep = self.keep.astype(F32) + self.came[:rows].astype(F32)

    def add(self, low, high):
        return (self.keep[low:high].astype(F32) + self.came[low:high].astype(F32)).astype(BF16)

    def relay(self, *others):
        if others:
            self.keep = after(self.keep, *others)
        self.receive()
        self.send()

    @staticmethod
    def last(parts, done=False):
        for part in parts:
            part.receive()
            part.size = part.sent.shape[0]
        rows = [part.sent for part in parts]
        small = parts[0].small
        if small is not None:
            parts[0].pair = halves_of(small)
            rows[1:1] = parts[0].pair
        joint = jnp.concatenate(rows, axis=0)
        came = swap_dp(joint, parts[0].order[-1] + parts[0].shift)
        if done:
            return came
        start = 0
        for part in parts:
            end = start + part.size + (2 * small.shape[0] if part.small is not None else 0)
            part.came = came[start:end]
            start = end
            part.step += 1
            part.receive()
        return joint

    def rest(self):
        value = self.keep
        for bit in reversed(range(self.shift)):
            half = value.shape[0] // 2
            mine = (lax.axis_index("dp") >> bit) & 1
            keep = lax.dynamic_slice_in_dim(value, mine * half, half, 0)
            away = lax.dynamic_slice_in_dim(value, (1 - mine) * half, half, 0)
            value = keep + swap_dp(away.astype(BF16), bit).astype(F32)
            if self.small is not None:
                self.small = self.small + swap_dp(self.small, bit)
        return value


def after(values, *others):
    return lax.optimization_barrier((values, others))[0]


def shards(
    tokens,
    doc_lengths,
    w_query,
    w_key,
    w_value,
    w_out,
    w_gate,
    w_up,
    w_down,
    gain_attn,
    gain_ffn,
    cotangent,
):
    row_count, width = tokens.shape
    head_cols = w_query.shape[1] // lax.axis_size("seq")
    dp_size = lax.axis_size("dp")
    blocks = min(dp_size, 16)
    shift = (dp_size // blocks).bit_length() - 1
    orders = ((0, 2, 1, 3), (1, 0, 2, 3), (2, 3, 0, 1))
    turns = ((1, 2, 0, 3), (1, 0, 2, 3), (2, 0, 1, 3))
    lengths = doc_lengths[0]
    seq_index = lax.axis_index("seq")
    info = jnp.stack([seq_index, lax.axis_index("dp") >> shift]).astype(jnp.int32)
    gain_one, gain_two = gain_attn.reshape(1, width), gain_ffn.reshape(1, width)

    oth = swap_seq(tokens)
    *started, turned, own_q, own_k, own_v = project_own(info, doc_lengths, tokens, (w_query, w_key, w_value))
    query, key, value, gathered, context, mine, away, lse = attention_forward(
        info, lengths, started, oth, turned
    )
    kept = (query, key, value, context, lse)
    came = swap_seq(away)
    act, silu, slope, result, dm, dm_turned, hb_turned, dr2, r1, small = ffn_forward(
        info, lengths, tokens, mine, came, w_out, gain_one, gain_two, w_gate, w_up, w_down, cotangent, blocks
    )
    down_away = weight_grad(info, dm_turned, act, orders[2], blocks)
    down_came = swap_seq(down_away)
    dgt, dup, gate_away, up_away = swiglu_away(
        info, after(dm, down_away), w_down, silu, slope, hb_turned, orders[:2], blocks
    )
    gate_came, up_came = swap_seq(gate_away), swap_seq(up_away)
    down = Halving(
        *weight_grad(info, dm_turned, after(act, gate_away), orders[2], blocks, down_came), orders[2], shift
    )
    down.send()
    dgt, dup = swiglu_mine(info, after(dm, down.sent), w_down, silu, slope, dgt, dup)
    gate = Halving(*weight_grad(info, hb_turned, dgt, orders[0], blocks, gate_came), orders[0], shift)
    gate.send()
    dr1, da_turned, own_rows, away_rows, small = norm_one(
        info, after(dgt, gate.sent), dup, w_gate, w_up, r1, dr2, gain_one, w_out, small, blocks
    )
    came_rows = swap_seq(away_rows)
    up = Halving(
        *weight_grad(info, after(hb_turned, away_rows), dup, orders[1], blocks, up_came), orders[1], shift
    )
    up.send()
    out_keep, out_away = out_grad(after(da_turned, up.sent), mine, came)
    out_came = swap_seq(out_away)
    small = small + swap_seq(small)
    grads = ()
    each = head_cols // HDIM // len(PLAN)
    ffn = [down, gate, up]
    for number, relays in enumerate(PLAN):
        for part in relays:
            ffn[part].relay(*grads)
        own_rows = after(own_rows, out_away, *[ffn[part].sent for part in relays], *grads)
        grads = attention_backward(
            info, lengths, kept, own_rows, came_rows, number * each, each, grads
        )
    sides = project_grad(info, gathered, grads, out_keep, out_came, turns, blocks)
    attn = [
        Halving(sides[2 * index], sides[2 * index + 1], turns[index], shift, None if index else small)
        for index in range(3)
    ]
    up.relay(*sides)
    query_part, key_part, value_part = attn
    key_part.send()
    value_part.send()
    weights = (own_q, own_k, own_v)
    stream_away = stream_grad(info, after(grads, *sides, up.sent), weights)
    stream_came = swap_seq(stream_away)
    gate.relay(stream_away)
    down.relay(stream_away)
    query_part.sent = after(query_part.sent, gate.sent, down.sent, key_part.came)
    query_part.send()
    grad_tokens = stream_grad(info, after(grads, key_part.came), weights, stream_came, dr1)
    up.relay(grad_tokens)
    key_part.relay(up.sent)
    value_part.relay(up.sent)
    joint = Halving.last([gate, up])
    down.relay(joint)
    query_part.relay(joint)
    for part in (key_part, value_part, query_part):
        part.relay(joint)
    down.receive()
    summed_down, summed_gate, summed_up = (part.rest() for part in ffn)
    summed_down = summed_down.T
    if shift:
        Halving.last(attn)
        sums = [part.rest() for part in attn]
        attn_grads = [total[:, :head_cols] for total in sums]
        attn_grads.append(jnp.concatenate([total[:, head_cols:] for total in sums], axis=1).T)
        small = attn[0].small.reshape(8, 2 * WIDE)[:, :width]
        grad_one, grad_two = small[0], small[1]
        rms_values = jnp.sqrt(jnp.sum(small[2:5], axis=1) / (small[5, 0] * width))
    else:
        came = after(Halving.last(attn, True), summed_down, summed_gate, summed_up, grad_tokens)
        *attn_grads, grad_wo, grad_one, grad_two, rms_values = finish(attn, came, width, head_cols)
        attn_grads.append(grad_wo.T)
    return (
        result,
        grad_tokens,
        *attn_grads,
        summed_gate,
        summed_up,
        summed_down,
        grad_one.reshape(-1),
        grad_two.reshape(-1),
        rms_values.reshape(-1),
    )


def solution(mesh):
    return jax.shard_map(
        shards,
        mesh=mesh,
        in_specs=(
            P(("dp", "seq"), None),
            P("dp", None),
            P(),
            P(),
            P(),
            P(),
            P(),
            P(),
            P(),
            P(),
            P(),
            P(("dp", "seq"), None),
        ),
        out_specs=(
            P(("dp", "seq"), None),
            P(("dp", "seq"), None),
            P("dp", "seq"),
            P("dp", "seq"),
            P("dp", "seq"),
            P("seq", "dp"),
            P("dp", "seq"),
            P("dp", "seq"),
            P("seq", "dp"),
            P(),
            P(),
            P(),
        ),
        check_vma=False,
    )
```
